128 devices in a mesh: rows: 16 (over x, z), cols: 8 (over y, core).
Axes of the slice: x: 4, y: 4, z: 4, core: 2. Of those that a mesh axis runs over, the one named last changes fastest.
Arguments:
- offsets: float32 [65536, 2, 256], P(('rows', 'cols')), may hold values from 0 to 16
- lens_weight: float32 [65536, 256], P(('rows', 'cols')), may hold values from 0.25 to 4
- counts: int32 [65536], P(('rows', 'cols')), may hold values from 1 to 256, as said below
- owners: int32 [65536], P(('rows', 'cols')), may hold values from 0 to 127, as said below
- brick_slot: int32 [65536], P(('rows', 'cols')), may hold values from 0 to 511
Outputs:
- leaders_fine: float32 [2048, 2048], P('rows', 'cols')
- leaders_second: float32 [1024, 1024], P('rows', 'cols')
- leaders_third: float32 [512, 512], P('rows', 'cols')
- leaders_coarse: float32 [256, 256], P('rows', 'cols')
- approx_coarse: float32 [256, 256], P('rows', 'cols')
The draws below stay inside these ranges and needn't reach their ends.
Inputs may be any that keep to these rules, and one draw needn't show every extreme that they name: `owners`: the bricks of one device name any device at most 8 times; one device, drawn from the seed, is named exactly 8 times by the bricks of every device. `counts`: each device holds a brick with exactly 256 particles.
All inputs are finite; a program needn't handle non-finite values.
Results may differ from the reference program's by a relative error of at most 0.0026.
Values sent between devices are 32-bit elements; how exact they have to be, the bound alone decides.
No kernel may reach another device: no remote copies, remote signals or barrier semaphores. Data moves between devices by JAX's collectives and lax.ppermute only.
A program may use at most 64 MiB of HBM per device.

```python
import math
import jax
import jax.numpy as jnp
from jax import lax

R_DEV = 256
C_DEV = 512
PMAX = 256
LEVELS = 4
BT = 512
BRICKS_DEV = 512
CAP = 8
BRICKS_ALL = 65536
N_ROWS = 16
N_COLS = 8


def draw_counts(key, part):
    devices = BRICKS_ALL // BRICKS_DEV
    base = jax.random.randint(jax.random.fold_in(key, 11), (devices, BRICKS_DEV), 1, PMAX + 1)
    chosen = jax.random.randint(jax.random.fold_in(key, 12), (devices, 1), 0, BRICKS_DEV)
    filled = jnp.arange(BRICKS_DEV)[None, :] == chosen
    return jnp.where(filled, PMAX, base).reshape(BRICKS_ALL).astype(jnp.int32)


def draw_owners(key, part):
    devices = BRICKS_ALL // BRICKS_DEV
    busiest = jax.random.randint(jax.random.fold_in(key, 21), (), 0, devices)
    pool_keys = jax.random.split(jax.random.fold_in(key, 22), devices)

    def pool_draw(single):
        return jax.random.permutation(single, (devices - 1) * CAP)
    pooled = jax.vmap(pool_draw)(pool_keys)
    others = (busiest + 1 + pooled[:, :BRICKS_DEV - CAP] // CAP) % devices
    target = jnp.concatenate([jnp.full((devices, CAP), busiest), others], axis=1)
    order_keys = jax.random.split(jax.random.fold_in(key, 23), devices)

    def order_draw(single):
        return jax.random.permutation(single, BRICKS_DEV)
    shuffled = jax.vmap(order_draw)(order_keys)
    return jnp.take_along_axis(target, shuffled, axis=1).reshape(BRICKS_ALL).astype(jnp.int32)


def with_ends(values, own_key, smallest, high):
    dims = values.shape
    place = [jax.random.randint(jax.random.fold_in(own_key, axis), (), 0, dims[axis]) for axis in range(len(dims))]
    values = values.at[tuple(place)].set(smallest)
    longest = dims.index(max(dims))
    place[longest] = (place[longest] + 1) % dims[longest]
    return values.at[tuple(place)].set(high)


def block_scale(own_key, shape, shards, low, high):
    gain, own = 1.0, jax.random.fold_in(own_key, 6)
    for dim, shards_of in shards:
        steps = jnp.exp(jax.random.uniform(jax.random.fold_in(own, dim), (shards_of,), jnp.float32, low / len(shards), high / len(shards)))
        gain = gain * jnp.repeat(steps, shape[dim] // shards_of).reshape([-1 if axis == dim else 1 for axis in range(len(shape))])
    return gain


def setup_inputs(seed: int = 0) -> dict:
    splits = jax.random.split(jax.random.key(seed), 6)
    return {
        "offsets": jnp.clip(16.0 * jax.random.uniform(splits[0], (BRICKS_ALL, 2, PMAX), jnp.float32) ** block_scale(splits[0], (BRICKS_ALL, 2, PMAX), ((0, 128),), -0.2, 0.2), 0.0, 16.0),
        "lens_weight": jnp.clip(jnp.exp(math.log(4.0) - 2.7725887 * jax.random.uniform(splits[1], (BRICKS_ALL, PMAX), jnp.float32) ** block_scale(splits[1], (BRICKS_ALL, PMAX), ((0, 128),), -0.2, 0.2)), 0.25, 4.0),
        "counts": draw_counts(jax.random.fold_in(splits[5], 71), 0),
        "owners": draw_owners(jax.random.fold_in(splits[5], 71), 0),
        "brick_slot": with_ends(jax.random.randint(splits[4], (BRICKS_ALL,), 0, BT), jax.random.fold_in(splits[4], 1), 0, BT - 1).astype(jnp.int32),
    }


taps_low = (0.33267055295008263, 0.8068915093110925, 0.4598775021184915, -0.13501102001025458, -0.08544127388202666, 0.035226291885709536)
taps_high = tuple(((-1.0) ** index) * taps_low[5 - index] for index in range(6))


def deposit_block(offsets, weights, counts):
    slot_count = offsets.shape[-1]
    occupied = jnp.arange(slot_count, dtype=jnp.int32)[None, :] < counts[:, None]
    scaled = jnp.where(occupied, weights, 0.0)
    centres = jnp.arange(17).astype(offsets.dtype)
    row_hat = jnp.maximum(0.0, 1.0 - jnp.abs(offsets[:, 0, None, :] - centres[None, :, None]))
    col_hat = jnp.maximum(0.0, 1.0 - jnp.abs(offsets[:, 1, None, :] - centres[None, :, None]))
    row_part = (row_hat * scaled[:, None, :]).astype(jnp.bfloat16)
    col_part = col_hat.astype(jnp.bfloat16)
    deposit = jnp.einsum("gip,gjp->gij", row_part.astype(jnp.float32), col_part.astype(jnp.float32), precision=lax.Precision.HIGHEST)
    return deposit.reshape(deposit.shape[0], 289)


def fold_wrap(values):
    spilled = jnp.roll(values[:, 16], 1, axis=0)
    interior = values[:, :16].at[:, 0].add(spilled)
    return interior.reshape((values.shape[0] * 16,) + values.shape[2:])


def split_pair(values, along):
    half_len = (values.shape[along] - 4) // 2
    low_sum = 0.0
    high_sum = 0.0
    for tap_index in range(6):
        strided = lax.slice_in_dim(values, tap_index, tap_index + 2 * half_len - 1, 2, along)
        low_sum = low_sum + taps_low[tap_index] * strided
        high_sum = high_sum + taps_high[tap_index] * strided
    return low_sum, high_sum


def pool_pairs(values):
    rows_n, cols_n = values.shape
    return jnp.max(values.reshape(rows_n // 2, 2, cols_n // 2, 2), axis=(1, 3))


def neighbourhood_max(values):
    largest = values
    for shift_row in (-1, 0, 1):
        for shift_col in (-1, 0, 1):
            largest = jnp.maximum(largest, jnp.roll(values, (shift_row, shift_col), (0, 1)))
    return largest


def reference(offsets, lens_weight, counts, owners, brick_slot):
    devices = N_ROWS * N_COLS
    tile_rows = R_DEV // 16
    tile_cols = C_DEV // 16

    def one_device(members):
        return deposit_block(members[0], members[1], members[2])

    patches = lax.map(one_device, (offsets.reshape(devices, BRICKS_DEV, 2, PMAX), lens_weight.reshape(devices, BRICKS_DEV, PMAX), counts.reshape(devices, BRICKS_DEV)))
    patches = patches.reshape(devices * BRICKS_DEV, 289)
    brick_row = (owners // N_COLS) * tile_rows + brick_slot // tile_cols
    brick_col = (owners % N_COLS) * tile_cols + brick_slot % tile_cols
    all_rows = tile_rows * N_ROWS
    all_cols = tile_cols * N_COLS
    position = (brick_row * all_cols + brick_col).astype(jnp.int32)
    brick_grid = jax.ops.segment_sum(patches, position, num_segments=all_rows * all_cols)
    brick_grid = brick_grid.reshape(all_rows, all_cols, 17, 17)
    across = fold_wrap(brick_grid.transpose(1, 3, 0, 2))
    current = fold_wrap(across.transpose(1, 2, 0))
    previous = None
    leader_maps = []
    for level_index in range(LEVELS):
        widened = jnp.concatenate([current, current[:, :4]], axis=1)
        low_cols, high_cols = split_pair(widened, 1)
        stacked = jnp.stack([low_cols, high_cols])
        low_rows, high_rows = split_pair(jnp.concatenate([stacked, stacked[:, :4]], axis=1), 1)
        current = low_rows[0]
        peak_now = jnp.maximum(jnp.maximum(jnp.abs(low_rows[1]), jnp.abs(high_rows[0])), jnp.abs(high_rows[1]))
        if previous is not None:
            peak_now = jnp.maximum(peak_now, pool_pairs(previous))
        previous = peak_now
        leader_maps.append(neighbourhood_max(peak_now))
    return leader_maps[0], leader_maps[1], leader_maps[2], leader_maps[3], current
```

```python
import functools

import jax
import jax.numpy as jnp
import numpy as np
from jax import lax
from jax.experimental import pallas as pl
from jax.experimental.pallas import tpu as pltpu
from jax.sharding import PartitionSpec as P

R_DEV = 256
C_DEV = 512
PMAX = 256
CAP = 8
N_DEST = 128
BRICKS = 512
SLOTS = N_DEST * CAP

TILE_ROWS = 272
UP_ROWS = 80
DOWN_ROWS = 24
DOWN_FROM = 240
ROW_ROOM = (192, 96, 48, 24)
COL_ROOM = (384, 256, 128, 128)

taps_low = (
    0.33267055295008263,
    0.8068915093110925,
    0.4598775021184915,
    -0.13501102001025458,
    -0.08544127388202666,
    0.03522629188570953,
)
taps_high = tuple(((-1.0) ** index * taps_low[5 - index] for index in range(6)))

f32 = jnp.float32
bf16 = jnp.bfloat16


def spans(size):
    out = []
    for level in range(1, 5):
        n = size >> level
        before = 8 >> (level - 1)
        after = (36, 16, 6, 1)[level - 1]
        out.append((-before, n + after, -before, n + before))
    return out


def level_table(sources, room, span):
    low_from, low_to, high_from, high_to = span
    table = np.zeros((len(sources), 2 * room), np.float64)
    for position, index in enumerate(sources):
        if index is None:
            continue
        for half, (lo, hi, taps) in enumerate(
            ((low_from, low_to, taps_low), (high_from, high_to, taps_high))
        ):
            for tap in range(6):
                if (index - tap) % 2 == 0:
                    k = (index - tap) // 2
                    if lo <= k < hi:
                        table[position, half * room + (k % room)] += taps[tap]
    return table


def room_sources(room, low_from, low_to):
    out = [None] * room
    for k in range(low_from, low_to):
        out[k % room] = k
    return out


def split(table):
    table = np.asarray(table, np.float32)
    high = table.astype(jnp.bfloat16)
    low = (table - high.astype(np.float32)).astype(jnp.bfloat16)
    return np.stack([high, low])


@functools.lru_cache(maxsize=1)
def tables():
    col_spans = spans(C_DEV)
    row_spans = spans(R_DEV)
    col_src = list(range(C_DEV))
    col_src += [C_DEV + j if j < 76 else None for j in range(128)]
    col_src += [0, C_DEV] + [None] * 110 + [j - 16 for j in range(16)]
    row_src = [i if i < 257 else None for i in range(TILE_ROWS)]
    row_src += [R_DEV + i if i < 76 else None for i in range(UP_ROWS)]
    row_src += [i - 16 if i < 17 else None for i in range(DOWN_ROWS)]
    cols, rows = [], []
    for level in range(4):
        cols.append(level_table(col_src, COL_ROOM[level], col_spans[level]))
        rows.append(level_table(row_src, ROW_ROOM[level], row_spans[level]).T)
        col_src = room_sources(COL_ROOM[level], col_spans[level][0], col_spans[level][1])
        row_src = room_sources(ROW_ROOM[level], row_spans[level][0], row_spans[level][1])
    picks = []
    for level in range(3):
        _, _, high_from, high_to = col_spans[level + 1]
        pick = np.zeros((COL_ROOM[level], COL_ROOM[level + 1]), np.float64)
        for k in range(high_from, high_to):
            pick[(2 * k) % COL_ROOM[level], k % COL_ROOM[level + 1]] = 1.0
        picks.append(pick.astype(jnp.bfloat16))
    return [split(t) for t in cols], [split(t) for t in rows], picks


def hi_lo(x):
    high = x.astype(bf16)
    low = (x - high.astype(f32)).astype(bf16)
    return high, low


def mm(a, b):
    return jnp.dot(a, b, preferred_element_type=f32)


def mm_nt(a, b):
    return lax.dot_general(a, b, (((1,), (1,)), ((), ())), preferred_element_type=f32)


def iota(shape, dim):
    return lax.broadcasted_iota(jnp.int32, shape, dim)


GROUPS_PER_STEP = 4


def deposit_kernel(off_ref, w_ref, counts_ref, owners_ref, slot_ref, out_ref, cnt_ref, patch_ref, edge_ref):
    owners = owners_ref[...]
    dest = (iota((N_DEST, BRICKS), 0) == owners).astype(f32)
    before = (iota((BRICKS, BRICKS), 0) < iota((BRICKS, BRICKS), 1)).astype(bf16)
    ranks = jnp.sum(mm(dest.astype(bf16), before) * dest, axis=0, keepdims=True)
    position = owners * CAP + ranks.astype(jnp.int32)

    slot = slot_ref[...]
    grid_row = slot // 32
    grid_col = slot % 32
    coarse = (grid_col % 8) * 4 + grid_col // 8
    row_id = iota((256, BRICKS), 0)
    spread = jnp.where(
        row_id < 128,
        counts_ref[...],
        jnp.where(row_id == 168, coarse, jnp.where(row_id == 169, grid_row, 0)),
    )
    eye = (iota((BRICKS, BRICKS), 0) == iota((BRICKS, BRICKS), 1)).astype(bf16)
    cnt_ref[...] = mm_nt(eye, spread.astype(f32).astype(bf16))

    lane = iota((8, 128), 1)
    sub = iota((8, 128), 0)
    particle = iota((8, PMAX), 1).astype(f32)
    cell = iota((16, PMAX), 0).astype(f32)

    def hat(x, at):
        return jnp.maximum(0.0, 1.0 - jnp.abs(x - at))

    def one_group(start):
        rows_at = off_ref[pl.ds(start, 8), 0:PMAX]
        cols_at = off_ref[pl.ds(start, 8), PMAX : 2 * PMAX]
        count = cnt_ref[pl.ds(start, 8), 0:128]
        count = jnp.concatenate([count, count], axis=1)
        weight = jnp.where(particle < count, w_ref[pl.ds(start, 8), :], 0.0)
        left = jnp.concatenate([hat(rows_at, float(i)) * weight for i in range(17)], axis=0).astype(bf16)
        right = [hat(cols_at[(8 - g) % 8 : (8 - g) % 8 + 1, :], cell) for g in range(8)]
        last = hat(cols_at, 16.0)
        right = jnp.concatenate(right + [last] * 16, axis=0).astype(bf16)
        full = mm_nt(left, right)
        halves = []
        for half in range(2):
            acc = None
            for pair in range(4):
                at = (half * 8 + pair * 2) * 8
                even = pltpu.roll(full[at : at + 8, 0:128], 0, 1, stride=16, stride_axis=0)
                odd = pltpu.roll(full[at + 8 : at + 16, 0:128], 16, 1, stride=16, stride_axis=0)
                both = jnp.where(lane // 16 == 0, even, odd)
                acc = both if pair == 0 else jnp.where(lane // 32 == pair, pltpu.roll(both, 32 * pair, 1), acc)
            halves.append(acc)
        bottom = pltpu.roll(full[128:136, 0:128], 0, 1, stride=16, stride_axis=0)
        corner = jnp.sum(jnp.where(lane == sub, full[128:136, 128:256], 0.0), axis=1, keepdims=True)
        third = jnp.where(lane < 16, bottom, jnp.where(lane == 32, corner, 0.0))
        edge = jnp.zeros((8, 128), f32)
        for i in range(16):
            edge = jnp.where(lane == 8 * i + sub, full[8 * i : 8 * i + 8, 128:256], edge)
        patch_ref[pl.ds(start, 8), 0:128] = halves[0]
        patch_ref[pl.ds(start, 8), 128:256] = halves[1]
        patch_ref[pl.ds(start, 8), 256:384] = third + cnt_ref[pl.ds(start, 8), 128:256]
        edge_ref[pl.ds(start, 8), :] = edge

    def step(index, carry):
        for sub_group in range(GROUPS_PER_STEP):
            one_group(pl.multiple_of((index * GROUPS_PER_STEP + sub_group) * 8, 8))
        return carry

    lax.fori_loop(0, BRICKS // 8 // GROUPS_PER_STEP, step, 0)

    gather = (iota((128, 128), 1) == iota((128, 128), 0) // 8 + 16).astype(bf16)
    edge_high, edge_low = hi_lo(edge_ref[...])
    patch_ref[:, 256:384] = patch_ref[:, 256:384] + (mm(edge_high, gather) + mm(edge_low, gather))

    high, low = hi_lo(patch_ref[...])
    for chunk in range(4):
        rows = SLOTS // 4
        pick = (iota((rows, BRICKS), 0) + chunk * rows == position).astype(bf16)
        out_ref[chunk * rows : (chunk + 1) * rows, :] = mm(pick, high) + mm(pick, low)


def deposit_and_pack(offsets, weights, counts, owners, slots):
    return pl.pallas_call(
        deposit_kernel,
        out_shape=jax.ShapeDtypeStruct((SLOTS, 384), f32),
        scratch_shapes=[
            pltpu.VMEM((BRICKS, 256), f32),
            pltpu.VMEM((BRICKS, 384), f32),
            pltpu.VMEM((BRICKS, 128), f32),
        ],
        compiler_params=pltpu.CompilerParams(vmem_limit_bytes=40 << 20),
        name="deposit",
    )(
        offsets.reshape(BRICKS, 2 * PMAX),
        weights,
        counts.reshape(1, BRICKS),
        owners.reshape(1, BRICKS),
        slots.reshape(1, BRICKS),
    )


def place_kernel(x_ref, raw_ref, left_ref, right_ref, grid_ref):
    lane8 = iota((8, 128), 1)
    weigh = jnp.where(lane8 == 40, 16.0, jnp.where(lane8 == 41, 1.0, 0.0)).astype(bf16)
    slot = mm_nt(weigh, x_ref[:, 256:384].astype(bf16))[0:1, :].astype(jnp.int32)
    high, low = hi_lo(x_ref[...])
    for chunk in range(4):
        pick = (iota((128, SLOTS), 0) + chunk * 128 == slot).astype(bf16)
        grid_ref[chunk * 128 : (chunk + 1) * 128, :] = mm(pick, high) + mm(pick, low)

    group = lane8 // 16
    masks = {d: (group // d) % 2 == 0 for d in (1, 2, 4)}

    def swap_groups(tiles):
        for d in (1, 2, 4):
            new = list(tiles)
            for a in range(8):
                if (a // d) % 2 == 0:
                    one, two = tiles[a], tiles[a + d]
                    new[a] = jnp.where(masks[d], one, pltpu.roll(two, 16 * d, 1))
                    new[a + d] = jnp.where(masks[d], pltpu.roll(one, 128 - 16 * d, 1), two)
            tiles = new
        return tiles

    def tiles_of(third, across, half):
        at = across * 16 + half * 8
        return swap_groups(
            [grid_ref[low_col * 64 + at : low_col * 64 + at + 8, third * 128 : (third + 1) * 128] for low_col in range(8)]
        )

    first_lane = lane8 == 0
    group_start = lane8 % 16 == 0
    for across in range(4):
        raw_ref[across * TILE_ROWS + 256 : (across + 1) * TILE_ROWS, :] = jnp.zeros((TILE_ROWS - 256, 128), f32)
    right_ref[256:TILE_ROWS, :] = jnp.zeros((TILE_ROWS - 256, 128), f32)
    left_ref[256:TILE_ROWS, :] = jnp.zeros((TILE_ROWS - 256, 128), f32)

    previous = None
    for across in range(4):
        rows = [[None, None] for _ in range(17)]
        turned = [[None, None] for _ in range(17)]
        for half in range(2):
            upper = tiles_of(0, across, half)
            lower = tiles_of(1, across, half)
            edges = tiles_of(2, across, half)
            for i in range(8):
                rows[i][half] = upper[i]
                rows[8 + i][half] = lower[i]
            rows[16][half] = edges[0]
            for i in range(16):
                turned[i][half] = pltpu.roll(edges[1], 16 - i, 1)
            turned[16][half] = pltpu.roll(edges[2], 16, 1)
            for i in range(17):
                before = jnp.zeros((8, 128), f32) if previous is None else previous[i][half]
                spill = jnp.where(first_lane, before, jnp.where(group_start, turned[i][half], 0.0))
                rows[i][half] = rows[i][half] + spill
        previous = turned
        def finish(parts, i, ref, top):
            if i == 0:
                down_low = pltpu.roll(parts[16][0], 1, 0)
                down_high = pltpu.roll(parts[16][1], 1, 0)
                sub = iota((8, 128), 0)
                low = parts[0][0] + jnp.where(sub == 0, 0.0, down_low)
                high_part = parts[0][1] + jnp.where(sub == 0, down_low, down_high)
                both = (low, high_part)
                ref[top + 256 : top + 257, :] = parts[16][1][7:8, :]
            else:
                both = (parts[i][0], parts[i][1])
            ref[pl.ds(top + i, 8, stride=16), :] = both[0]
            ref[pl.ds(top + 128 + i, 8, stride=16), :] = both[1]

        for i in range(16):
            finish(rows, i, raw_ref, across * TILE_ROWS)
        if across == 0:
            for i in range(16):
                finish(rows, i, left_ref, 0)
        if across == 3:
            with_spill = [
                [jnp.where(first_lane, turned[i][half], rows[i][half]) for half in range(2)] for i in range(17)
            ]
            for i in range(16):
                finish(with_spill, i, right_ref, 0)


def place_and_fold(arrived):
    return pl.pallas_call(
        place_kernel,
        out_shape=(
            jax.ShapeDtypeStruct((4 * TILE_ROWS, 128), f32),
            jax.ShapeDtypeStruct((TILE_ROWS, 128), f32),
            jax.ShapeDtypeStruct((TILE_ROWS, 128), f32),
        ),
        scratch_shapes=[pltpu.VMEM((BRICKS, 384), f32)],
        compiler_params=pltpu.CompilerParams(vmem_limit_bytes=40 << 20),
        name="place",
    )(arrived)


def mm3(data, table_ref):
    high, low = hi_lo(data)
    return mm(high, table_ref[0]) + (mm(low, table_ref[0]) + mm(high, table_ref[1]))


def mm3_left(table_ref, data):
    high, low = hi_lo(data)
    return mm(table_ref[0], high) + (mm(table_ref[0], low) + mm(table_ref[1], high))


def columns_kernel(raw_ref, to_right_ref, from_right_ref, from_left_ref, table_ref, out_ref, up_ref, down_ref):
    lane = iota((TILE_ROWS, 128), 1)
    from_left = jnp.where(lane == 1, pltpu.roll(to_right_ref[...], 1, 1), from_left_ref[...])
    data = jnp.concatenate(
        [raw_ref[across * TILE_ROWS : (across + 1) * TILE_ROWS, :] for across in range(4)]
        + [from_right_ref[...], from_left],
        axis=1,
    )
    out_ref[...] = mm3(data, table_ref)
    up_ref[...] = out_ref[0:UP_ROWS, :]
    down_ref[...] = out_ref[DOWN_FROM : DOWN_FROM + DOWN_ROWS, :]


def first_columns(raw, to_right, from_right, from_left, table):
    width = 2 * COL_ROOM[0]
    return pl.pallas_call(
        columns_kernel,
        out_shape=(
            jax.ShapeDtypeStruct((TILE_ROWS, width), f32),
            jax.ShapeDtypeStruct((UP_ROWS, width), f32),
            jax.ShapeDtypeStruct((DOWN_ROWS, width), f32),
        ),
        compiler_params=pltpu.CompilerParams(vmem_limit_bytes=40 << 20),
        name="columns",
    )(raw, to_right, from_right, from_left, table)


def levels_kernel(own_ref, below_ref, above_ref, *refs):
    col_refs = (None,) + refs[0:3]
    row_refs = refs[3:7]
    pick_refs = refs[7:10]
    leader_refs = refs[10:14]
    approx_ref = refs[14]
    peak_ref = refs[15]
    current = jnp.concatenate([own_ref[...], below_ref[...], above_ref[...]], axis=0)
    peak = None
    for level in range(4):
        room_r = ROW_ROOM[level]
        room_c = COL_ROOM[level]
        if level:
            current = mm3(current, col_refs[level])
        both = mm3_left(row_refs[level], current)
        current = both[:room_r, :room_c]
        detail_a = both[:room_r, room_c:]
        detail_b = both[room_r:, :room_c]
        detail_c = both[room_r:, room_c:]
        now = jnp.maximum(jnp.maximum(jnp.abs(detail_a), jnp.abs(detail_b)), jnp.abs(detail_c))
        if peak is not None:
            now = jnp.maximum(now, peak)
        wide = jnp.maximum(now, jnp.maximum(pltpu.roll(now, 1, 1), pltpu.roll(now, room_c - 1, 1)))
        wide = jnp.maximum(wide, jnp.maximum(pltpu.roll(wide, 1, 0), pltpu.roll(wide, room_r - 1, 0)))
        n_r = R_DEV >> (level + 1)
        n_c = C_DEV >> (level + 1)
        leader_refs[level][...] = wide[:n_r, :n_c]
        if level < 3:
            pairs = jnp.maximum(now, pltpu.roll(now, room_c - 1, 1))
            pooled = []
            for across in range(room_c // 128):
                top = across * ROW_ROOM[0]
                peak_ref[top : top + room_r, :] = pairs[:, across * 128 : (across + 1) * 128]
                pooled.append(
                    jnp.maximum(
                        peak_ref[pl.ds(top, room_r // 2, stride=2), :],
                        peak_ref[pl.ds(top + 1, room_r // 2, stride=2), :],
                    )
                )
            high, low = hi_lo(jnp.concatenate(pooled, axis=1) if len(pooled) > 1 else pooled[0])
            pick = pick_refs[level][...]
            peak = mm(high, pick) + mm(low, pick)
    approx_ref[...] = current[: R_DEV >> 4, : C_DEV >> 4]


def all_levels(own, below, above, cols, rows, picks):
    shapes = [(R_DEV >> level, C_DEV >> level) for level in (1, 2, 3, 4, 4)]
    return pl.pallas_call(
        levels_kernel,
        out_shape=tuple(jax.ShapeDtypeStruct(shape, f32) for shape in shapes),
        scratch_shapes=[pltpu.VMEM((3 * ROW_ROOM[0], 128), f32)],
        compiler_params=pltpu.CompilerParams(vmem_limit_bytes=48 << 20),
        name="levels",
    )(own, below, above, *cols[1:], *rows, *picks)


def shifted(x, axis, by):
    size = lax.axis_size(axis)
    return lax.ppermute(x, axis, [(i, (i + by) % size) for i in range(size)])


def on_device(offsets, lens_weight, counts, owners, brick_slot):
    cols, rows, picks = tables()
    cols = [jnp.asarray(t) for t in cols]
    rows = [jnp.asarray(t) for t in rows]
    picks = [jnp.asarray(t) for t in picks]
    packed = deposit_and_pack(offsets, lens_weight, counts, owners, brick_slot)
    arrived = lax.all_to_all(
        packed.reshape(N_DEST, CAP, 384), ("rows", "cols"), split_axis=0, concat_axis=0, tiled=True
    )
    raw, to_left, to_right = place_and_fold(arrived.reshape(SLOTS, 384))
    from_right = shifted(to_left, "cols", -1)
    from_left = shifted(to_right, "cols", 1)
    own, to_up, to_down = first_columns(raw, to_right, from_right, from_left, cols[0])
    below = shifted(to_up, "rows", -1)
    above = shifted(to_down, "rows", 1)
    return all_levels(own, below, above, cols, rows, picks)


def solution(mesh):
    placed = (
        P(("rows", "cols"), None, None),
        P(("rows", "cols"), None),
        P(("rows", "cols")),
        P(("rows", "cols")),
        P(("rows", "cols")),
    )
    return jax.shard_map(
        on_device,
        mesh=mesh,
        in_specs=placed,
        out_specs=(P("rows", "cols"),) * 5,
        check_vma=False,
    )
```

```python
import functools

import jax
import jax.numpy as jnp
import numpy as np
from jax import lax
from jax.experimental import pallas as pl
from jax.experimental.pallas import tpu as pltpu
from jax.sharding import PartitionSpec as P

R_DEV = 256
C_DEV = 512
PMAX = 256
CAP = 8
N_DEST = 128
BRICKS = 512
SLOTS = N_DEST * CAP

TILE_ROWS = 272
UP_ROWS = 80
DOWN_ROWS = 24
DOWN_FROM = 240
ROW_ROOM = (192, 96, 48, 24)
COL_ROOM = (384, 256, 128, 128)

taps_low = (
    0.33267055295008263,
    0.8068915093110925,
    0.4598775021184915,
    -0.13501102001025458,
    -0.08544127388202666,
    0.03522629188570953,
)
taps_high = tuple(((-1.0) ** index * taps_low[5 - index] for index in range(6)))

f32 = jnp.float32
bf16 = jnp.bfloat16


def spans(size):
    out = []
    for level in range(1, 5):
        n = size >> level
        before = 8 >> (level - 1)
        after = (36, 16, 6, 1)[level - 1]
        out.append((-before, n + after, -before, n + before))
    return out


def level_table(sources, room, span):
    low_from, low_to, high_from, high_to = span
    table = np.zeros((len(sources), 2 * room), np.float64)
    for position, index in enumerate(sources):
        if index is None:
            continue
        for half, (lo, hi, taps) in enumerate(
            ((low_from, low_to, taps_low), (high_from, high_to, taps_high))
        ):
            for tap in range(6):
                if (index - tap) % 2 == 0:
                    k = (index - tap) // 2
                    if lo <= k < hi:
                        table[position, half * room + (k % room)] += taps[tap]
    return table


def room_sources(room, low_from, low_to):
    out = [None] * room
    for k in range(low_from, low_to):
        out[k % room] = k
    return out


def split(table):
    table = np.asarray(table, np.float32)
    high = table.astype(jnp.bfloat16)
    low = (table - high.astype(np.float32)).astype(jnp.bfloat16)
    return np.stack([high, low])


@functools.lru_cache(maxsize=1)
def tables():
    col_spans = spans(C_DEV)
    row_spans = spans(R_DEV)
    col_src = list(range(C_DEV))
    col_src += [C_DEV + j if j < 76 else None for j in range(128)]
    col_src += [0, C_DEV] + [None] * 110 + [j - 16 for j in range(16)]
    row_src = [i if i < 257 else None for i in range(TILE_ROWS)]
    row_src += [R_DEV + i if i < 76 else None for i in range(UP_ROWS)]
    row_src += [i - 16 if i < 17 else None for i in range(DOWN_ROWS)]
    cols, rows = [], []
    for level in range(4):
        cols.append(level_table(col_src, COL_ROOM[level], col_spans[level]))
        rows.append(level_table(row_src, ROW_ROOM[level], row_spans[level]).T)
        col_src = room_sources(COL_ROOM[level], col_spans[level][0], col_spans[level][1])
        row_src = room_sources(ROW_ROOM[level], row_spans[level][0], row_spans[level][1])
    picks = []
    for level in range(3):
        _, _, high_from, high_to = col_spans[level + 1]
        pick = np.zeros((COL_ROOM[level], COL_ROOM[level + 1]), np.float64)
        for k in range(high_from, high_to):
            pick[(2 * k) % COL_ROOM[level], k % COL_ROOM[level + 1]] = 1.0
        picks.append(pick.astype(jnp.bfloat16))
    return [split(t) for t in cols], [split(t) for t in rows], picks


def hi_lo(x):
    high = x.astype(bf16)
    low = (x - high.astype(f32)).astype(bf16)
    return high, low


def mm(a, b):
    return jnp.dot(a, b, preferred_element_type=f32)


def mm_nt(a, b):
    return lax.dot_general(a, b, (((1,), (1,)), ((), ())), preferred_element_type=f32)


def iota(shape, dim):
    return lax.broadcasted_iota(jnp.int32, shape, dim)


GROUPS_PER_STEP = 16
STEPS = BRICKS // 8 // GROUPS_PER_STEP
STEP_BRICKS = BRICKS // STEPS
MESSAGE = 20


def deposit_kernel(
    off_hbm,
    w_hbm,
    counts_hbm,
    owners_hbm,
    slot_hbm,
    out_ref,
    off_ref,
    w_ref,
    counts_ref,
    owners_ref,
    slot_ref,
    cnt_ref,
    patch_ref,
    edge_ref,
    small_sem,
    off_sem,
    w_sem,
):
    small = [
        pltpu.make_async_copy(src, dst, small_sem.at[n])
        for n, (src, dst) in enumerate(
            ((owners_hbm, owners_ref), (slot_hbm, slot_ref), (counts_hbm, counts_ref))
        )
    ]
    for copy in small:
        copy.start()

    def fetch(index):
        off_rows = pl.ds(index * 4 * STEP_BRICKS, 4 * STEP_BRICKS)
        w_rows = pl.ds(index * STEP_BRICKS, STEP_BRICKS)
        return (
            pltpu.make_async_copy(off_hbm.at[off_rows], off_ref.at[off_rows], off_sem.at[index]),
            pltpu.make_async_copy(w_hbm.at[w_rows], w_ref.at[w_rows], w_sem.at[index]),
        )

    for index in range(STEPS):
        for copy in fetch(index):
            copy.start()
    for copy in small:
        copy.wait()

    owners = owners_ref[...]
    dest = (iota((N_DEST, BRICKS), 0) == owners).astype(f32)
    before = (iota((BRICKS, BRICKS), 0) < iota((BRICKS, BRICKS), 1)).astype(bf16)
    ranks = jnp.sum(mm(dest.astype(bf16), before) * dest, axis=0, keepdims=True)
    position = ranks.astype(jnp.int32) * N_DEST + owners

    slot = slot_ref[...]
    grid_row = slot // 32
    grid_col = slot % 32
    coarse = (grid_col % 8) * 4 + grid_col // 8
    row_id = iota((256, BRICKS), 0)
    spread = jnp.where(
        row_id < 128,
        counts_ref[...],
        jnp.where(row_id == 168, coarse, jnp.where(row_id == 169, grid_row, 0)),
    )
    eye = (iota((BRICKS, BRICKS), 0) == iota((BRICKS, BRICKS), 1)).astype(bf16)
    cnt_ref[...] = mm_nt(eye, spread.astype(f32).astype(bf16))

    lane = iota((8, 128), 1)
    sub = iota((8, 128), 0)
    particle = iota((8, PMAX), 1).astype(f32)
    cell = iota((16, PMAX), 0).astype(f32)

    def hat(x, at):
        return jnp.maximum(0.0, 1.0 - jnp.abs(x - at))

    def one_group(start):
        first = pl.multiple_of(start * 4, 32)
        rows_at = jnp.concatenate([off_ref[pl.ds(first + 2 * half, 8, stride=4), :] for half in range(2)], axis=1)
        cols_at = jnp.concatenate([off_ref[pl.ds(first + 2 * half + 1, 8, stride=4), :] for half in range(2)], axis=1)
        count = cnt_ref[pl.ds(start, 8), 0:128]
        count = jnp.concatenate([count, count], axis=1)
        weight = jnp.where(particle < count, w_ref[pl.ds(start, 8), :], 0.0)
        left = jnp.concatenate([hat(rows_at, float(i)) * weight for i in range(17)], axis=0).astype(bf16)
        right = [hat(cols_at[(8 - g) % 8 : (8 - g) % 8 + 1, :], cell) for g in range(8)]
        last = hat(cols_at, 16.0)
        right = jnp.concatenate(right + [last] * 16, axis=0).astype(bf16)
        full = mm_nt(left, right)
        halves = []
        for half in range(2):
            acc = None
            for pair in range(4):
                at = (half * 8 + pair * 2) * 8
                even = pltpu.roll(full[at : at + 8, 0:128], 0, 1, stride=16, stride_axis=0)
                odd = pltpu.roll(full[at + 8 : at + 16, 0:128], 16, 1, stride=16, stride_axis=0)
                both = jnp.where(lane // 16 == 0, even, odd)
                acc = both if pair == 0 else jnp.where(lane // 32 == pair, pltpu.roll(both, 32 * pair, 1), acc)
            halves.append(acc)
        bottom = pltpu.roll(full[128:136, 0:128], 0, 1, stride=16, stride_axis=0)
        corner = jnp.sum(jnp.where(lane == sub, full[128:136, 128:256], 0.0), axis=1, keepdims=True)
        third = jnp.where(lane < 16, bottom, jnp.where(lane == 32, corner, 0.0))
        edge = jnp.zeros((8, 128), f32)
        for i in range(16):
            edge = jnp.where(lane == 8 * i + sub, full[8 * i : 8 * i + 8, 128:256], edge)
        patch_ref[pl.ds(start, 8), 0:128] = halves[0]
        patch_ref[pl.ds(start, 8), 128:256] = halves[1]
        patch_ref[pl.ds(start, 8), 256:384] = third + cnt_ref[pl.ds(start, 8), 128:256]
        edge_ref[pl.ds(start, 8), :] = edge

    def step(index, carry):
        for copy in fetch(index):
            copy.wait()
        for sub_group in range(GROUPS_PER_STEP):
            one_group(pl.multiple_of((index * GROUPS_PER_STEP + sub_group) * 8, 8))
        return carry

    lax.fori_loop(0, STEPS, step, 0)

    gather = (iota((128, 128), 1) == iota((128, 128), 0) // 8 + 16).astype(bf16)
    edge_high, edge_low = hi_lo(edge_ref[...])
    third = patch_ref[:, 256:384] + (mm(edge_high, gather) + mm(edge_low, gather))

    high, low = hi_lo(patch_ref[:, 0:256])
    ends = jnp.concatenate(hi_lo(third), axis=1)
    lane_wide = iota((N_DEST, 128), 1)
    for pair in range(4):
        edges = []
        for rank in (2 * pair, 2 * pair + 1):
            pick = (iota((N_DEST, BRICKS), 0) + rank * N_DEST == position).astype(bf16)
            inner = mm(pick, high) + mm(pick, low)
            out_ref[pl.ds(rank, N_DEST, stride=MESSAGE), :] = inner[:, 0:128]
            out_ref[pl.ds(8 + rank, N_DEST, stride=MESSAGE), :] = inner[:, 128:256]
            both = mm(pick, ends)
            edges.append(both[:, 0:128] + both[:, 128:256])
        joined = jnp.where(lane_wide < 64, edges[0], pltpu.roll(edges[1], 64, 1))
        out_ref[pl.ds(16 + pair, N_DEST, stride=MESSAGE), :] = joined


def deposit_and_pack(offsets, weights, counts, owners, slots):
    flat = offsets.reshape(BRICKS, 2, 2, 128).transpose(0, 2, 1, 3).reshape(4 * BRICKS, 128)
    return pl.pallas_call(
        deposit_kernel,
        out_shape=jax.ShapeDtypeStruct((N_DEST * MESSAGE, 128), f32),
        in_specs=[pl.BlockSpec(memory_space=pltpu.MemorySpace.HBM)] * 5,
        scratch_shapes=[
            pltpu.VMEM((4 * BRICKS, 128), f32),
            pltpu.VMEM((BRICKS, PMAX), f32),
            pltpu.VMEM((1, BRICKS), jnp.int32),
            pltpu.VMEM((1, BRICKS), jnp.int32),
            pltpu.VMEM((1, BRICKS), jnp.int32),
            pltpu.VMEM((BRICKS, 256), f32),
            pltpu.VMEM((BRICKS, 384), f32),
            pltpu.VMEM((BRICKS, 128), f32),
            pltpu.SemaphoreType.DMA((3,)),
            pltpu.SemaphoreType.DMA((STEPS,)),
            pltpu.SemaphoreType.DMA((STEPS,)),
        ],
        compiler_params=pltpu.CompilerParams(vmem_limit_bytes=40 << 20),
        name="deposit",
    )(
        flat,
        weights,
        counts.reshape(1, BRICKS),
        owners.reshape(1, BRICKS),
        slots.reshape(1, BRICKS),
    )


def place_kernel(x_ref, raw_ref, left_ref, right_ref, grid_ref):
    lane8 = iota((8, 128), 1)
    upper = jnp.concatenate([x_ref[pl.ds(rank, N_DEST, stride=MESSAGE), :] for rank in range(8)], axis=0)
    lower = jnp.concatenate([x_ref[pl.ds(8 + rank, N_DEST, stride=MESSAGE), :] for rank in range(8)], axis=0)
    ends = []
    for pair in range(4):
        joined = x_ref[pl.ds(16 + pair, N_DEST, stride=MESSAGE), :]
        ends += [joined, pltpu.roll(joined, 64, 1)]
    ends_high, ends_low = hi_lo(jnp.concatenate(ends, axis=0))
    weigh = jnp.where(lane8 == 40, 16.0, jnp.where(lane8 == 41, 1.0, 0.0)).astype(bf16)
    slot = mm_nt(weigh, ends_high)[0:1, :].astype(jnp.int32)
    high, low = hi_lo(jnp.concatenate([upper, lower], axis=1))
    ends = jnp.concatenate([ends_high, ends_low], axis=1)
    for chunk in range(4):
        rows = slice(chunk * 128, (chunk + 1) * 128)
        pick = (iota((128, SLOTS), 0) + chunk * 128 == slot).astype(bf16)
        grid_ref[rows, 0:256] = mm(pick, high) + mm(pick, low)
        both = mm(pick, ends)
        grid_ref[rows, 256:384] = both[:, 0:128] + both[:, 128:256]

    group = lane8 // 16
    masks = {d: (group // d) % 2 == 0 for d in (1, 2, 4)}

    def swap_groups(tiles):
        for d in (1, 2, 4):
            new = list(tiles)
            for a in range(8):
                if (a // d) % 2 == 0:
                    one, two = tiles[a], tiles[a + d]
                    new[a] = jnp.where(masks[d], one, pltpu.roll(two, 16 * d, 1))
                    new[a + d] = jnp.where(masks[d], pltpu.roll(one, 128 - 16 * d, 1), two)
            tiles = new
        return tiles

    def tiles_of(third, across, half):
        at = across * 16 + half * 8
        return swap_groups(
            [grid_ref[low_col * 64 + at : low_col * 64 + at + 8, third * 128 : (third + 1) * 128] for low_col in range(8)]
        )

    first_lane = lane8 == 0
    group_start = lane8 % 16 == 0
    for across in range(4):
        raw_ref[across * TILE_ROWS + 256 : (across + 1) * TILE_ROWS, :] = jnp.zeros((TILE_ROWS - 256, 128), f32)
    right_ref[256:TILE_ROWS, :] = jnp.zeros((TILE_ROWS - 256, 128), f32)
    left_ref[256:TILE_ROWS, :] = jnp.zeros((TILE_ROWS - 256, 128), f32)

    previous = None
    for across in range(4):
        rows = [[None, None] for _ in range(17)]
        turned = [[None, None] for _ in range(17)]
        for half in range(2):
            upper = tiles_of(0, across, half)
            lower = tiles_of(1, across, half)
            edges = tiles_of(2, across, half)
            for i in range(8):
                rows[i][half] = upper[i]
                rows[8 + i][half] = lower[i]
            rows[16][half] = edges[0]
            for i in range(16):
                turned[i][half] = pltpu.roll(edges[1], 16 - i, 1)
            turned[16][half] = pltpu.roll(edges[2], 16, 1)
            for i in range(17):
                before = jnp.zeros((8, 128), f32) if previous is None else previous[i][half]
                spill = jnp.where(first_lane, before, jnp.where(group_start, turned[i][half], 0.0))
                rows[i][half] = rows[i][half] + spill
        previous = turned
        def finish(parts, i, ref, top):
            if i == 0:
                down_low = pltpu.roll(parts[16][0], 1, 0)
                down_high = pltpu.roll(parts[16][1], 1, 0)
                sub = iota((8, 128), 0)
                low = parts[0][0] + jnp.where(sub == 0, 0.0, down_low)
                high_part = parts[0][1] + jnp.where(sub == 0, down_low, down_high)
                both = (low, high_part)
                ref[top + 256 : top + 257, :] = parts[16][1][7:8, :]
            else:
                both = (parts[i][0], parts[i][1])
            ref[pl.ds(top + i, 8, stride=16), :] = both[0]
            ref[pl.ds(top + 128 + i, 8, stride=16), :] = both[1]

        for i in range(16):
            finish(rows, i, raw_ref, across * TILE_ROWS)
        if across == 0:
            for i in range(16):
                finish(rows, i, left_ref, 0)
        if across == 3:
            with_spill = [
                [jnp.where(first_lane, turned[i][half], rows[i][half]) for half in range(2)] for i in range(17)
            ]
            for i in range(16):
                finish(with_spill, i, right_ref, 0)


def place_and_fold(arrived):
    return pl.pallas_call(
        place_kernel,
        out_shape=(
            jax.ShapeDtypeStruct((4 * TILE_ROWS, 128), f32),
            jax.ShapeDtypeStruct((TILE_ROWS, 128), f32),
            jax.ShapeDtypeStruct((TILE_ROWS, 128), f32),
        ),
        scratch_shapes=[pltpu.VMEM((BRICKS, 384), f32)],
        compiler_params=pltpu.CompilerParams(vmem_limit_bytes=40 << 20),
        name="place",
    )(arrived)


def mm3(data, table_ref):
    high, low = hi_lo(data)
    return mm(high, table_ref[0]) + (mm(low, table_ref[0]) + mm(high, table_ref[1]))


def mm3_left(table_ref, data):
    high, low = hi_lo(data)
    return mm(table_ref[0], high) + (mm(table_ref[0], low) + mm(table_ref[1], high))


def columns_kernel(raw_ref, to_right_ref, from_right_ref, from_left_ref, table_ref, out_ref, up_ref, down_ref):
    lane = iota((TILE_ROWS, 128), 1)
    from_left = jnp.where(lane == 1, pltpu.roll(to_right_ref[...], 1, 1), from_left_ref[...])
    data = jnp.concatenate(
        [raw_ref[across * TILE_ROWS : (across + 1) * TILE_ROWS, :] for across in range(4)]
        + [from_right_ref[...], from_left],
        axis=1,
    )
    out_ref[...] = mm3(data, table_ref)
    up_ref[...] = out_ref[0:UP_ROWS, :]
    down_ref[...] = out_ref[DOWN_FROM : DOWN_FROM + DOWN_ROWS, :]


def first_columns(raw, to_right, from_right, from_left, table):
    width = 2 * COL_ROOM[0]
    return pl.pallas_call(
        columns_kernel,
        out_shape=(
            jax.ShapeDtypeStruct((TILE_ROWS, width), f32),
            jax.ShapeDtypeStruct((UP_ROWS, width), f32),
            jax.ShapeDtypeStruct((DOWN_ROWS, width), f32),
        ),
        compiler_params=pltpu.CompilerParams(vmem_limit_bytes=40 << 20),
        name="columns",
    )(raw, to_right, from_right, from_left, table)


def levels_kernel(own_ref, below_ref, above_ref, *refs):
    col_refs = (None,) + refs[0:3]
    row_refs = refs[3:7]
    pick_refs = refs[7:10]
    leader_refs = refs[10:14]
    approx_ref = refs[14]
    peak_ref = refs[15]
    current = jnp.concatenate([own_ref[...], below_ref[...], above_ref[...]], axis=0)
    peak = None
    for level in range(4):
        room_r = ROW_ROOM[level]
        room_c = COL_ROOM[level]
        if level:
            current = mm3(current, col_refs[level])
        both = mm3_left(row_refs[level], current)
        current = both[:room_r, :room_c]
        detail_a = both[:room_r, room_c:]
        detail_b = both[room_r:, :room_c]
        detail_c = both[room_r:, room_c:]
        now = jnp.maximum(jnp.maximum(jnp.abs(detail_a), jnp.abs(detail_b)), jnp.abs(detail_c))
        if peak is not None:
            now = jnp.maximum(now, peak)
        wide = jnp.maximum(now, jnp.maximum(pltpu.roll(now, 1, 1), pltpu.roll(now, room_c - 1, 1)))
        wide = jnp.maximum(wide, jnp.maximum(pltpu.roll(wide, 1, 0), pltpu.roll(wide, room_r - 1, 0)))
        n_r = R_DEV >> (level + 1)
        n_c = C_DEV >> (level + 1)
        leader_refs[level][...] = wide[:n_r, :n_c]
        if level < 3:
            pairs = jnp.maximum(now, pltpu.roll(now, room_c - 1, 1))
            pooled = []
            for across in range(room_c // 128):
                top = across * ROW_ROOM[0]
                peak_ref[top : top + room_r, :] = pairs[:, across * 128 : (across + 1) * 128]
                pooled.append(
                    jnp.maximum(
                        peak_ref[pl.ds(top, room_r // 2, stride=2), :],
                        peak_ref[pl.ds(top + 1, room_r // 2, stride=2), :],
                    )
                )
            high, low = hi_lo(jnp.concatenate(pooled, axis=1) if len(pooled) > 1 else pooled[0])
            pick = pick_refs[level][...]
            peak = mm(high, pick) + mm(low, pick)
    approx_ref[...] = current[: R_DEV >> 4, : C_DEV >> 4]


def all_levels(own, below, above, cols, rows, picks):
    shapes = [(R_DEV >> level, C_DEV >> level) for level in (1, 2, 3, 4, 4)]
    return pl.pallas_call(
        levels_kernel,
        out_shape=tuple(jax.ShapeDtypeStruct(shape, f32) for shape in shapes),
        scratch_shapes=[pltpu.VMEM((3 * ROW_ROOM[0], 128), f32)],
        compiler_params=pltpu.CompilerParams(vmem_limit_bytes=48 << 20),
        name="levels",
    )(own, below, above, *cols[1:], *rows, *picks)


def shifted(x, axis, by):
    size = lax.axis_size(axis)
    return lax.ppermute(x, axis, [(i, (i + by) % size) for i in range(size)])


def on_device(offsets, lens_weight, counts, owners, brick_slot):
    cols, rows, picks = tables()
    cols = [jnp.asarray(t) for t in cols]
    rows = [jnp.asarray(t) for t in rows]
    picks = [jnp.asarray(t) for t in picks]
    packed = deposit_and_pack(offsets, lens_weight, counts, owners, brick_slot)
    arrived = lax.all_to_all(
        packed.reshape(N_DEST, MESSAGE // 4, 4, 128), ("rows", "cols"), split_axis=0, concat_axis=0, tiled=True
    )
    raw, to_left, to_right = place_and_fold(arrived.reshape(N_DEST * MESSAGE, 128))
    from_right = shifted(to_left, "cols", -1)
    from_left = shifted(to_right, "cols", 1)
    own, to_up, to_down = first_columns(raw, to_right, from_right, from_left, cols[0])
    below = shifted(to_up, "rows", -1)
    above = shifted(to_down, "rows", 1)
    return all_levels(own, below, above, cols, rows, picks)


def solution(mesh):
    placed = (
        P(("rows", "cols"), None, None),
        P(("rows", "cols"), None),
        P(("rows", "cols")),
        P(("rows", "cols")),
        P(("rows", "cols")),
    )
    return jax.shard_map(
        on_device,
        mesh=mesh,
        in_specs=placed,
        out_specs=(P("rows", "cols"),) * 5,
        check_vma=False,
    )
```

```python
import functools

import jax
import jax.numpy as jnp
import numpy as np
from jax import lax
from jax.experimental import pallas as pl
from jax.experimental.pallas import tpu as pltpu
from jax.sharding import PartitionSpec as P

R_DEV = 256
C_DEV = 512
PMAX = 256
CAP = 8
N_DEST = 128
BRICKS = 512
SLOTS = N_DEST * CAP

TILE_ROWS = 272
UP_ROWS = 80
DOWN_ROWS = 24
DOWN_FROM = 240
ROW_ROOM = (192, 96, 48, 24)
COL_ROOM = (384, 256, 128, 128)

taps_low = (
    0.33267055295008263,
    0.8068915093110925,
    0.4598775021184915,
    -0.13501102001025458,
    -0.08544127388202666,
    0.03522629188570953,
)
taps_high = tuple(((-1.0) ** index * taps_low[5 - index] for index in range(6)))

f32 = jnp.float32
bf16 = jnp.bfloat16


def spans(size):
    out = []
    for level in range(1, 5):
        n = size >> level
        before = 8 >> (level - 1)
        after = (36, 16, 6, 1)[level - 1]
        out.append((-before, n + after, -before, n + before))
    return out


def level_table(sources, room, span):
    low_from, low_to, high_from, high_to = span
    table = np.zeros((len(sources), 2 * room), np.float64)
    for position, index in enumerate(sources):
        if index is None:
            continue
        for half, (lo, hi, taps) in enumerate(
            ((low_from, low_to, taps_low), (high_from, high_to, taps_high))
        ):
            for tap in range(6):
                if (index - tap) % 2 == 0:
                    k = (index - tap) // 2
                    if lo <= k < hi:
                        table[position, half * room + (k % room)] += taps[tap]
    return table


def room_sources(room, low_from, low_to):
    out = [None] * room
    for k in range(low_from, low_to):
        out[k % room] = k
    return out


def split(table):
    table = np.asarray(table, np.float32)
    high = table.astype(jnp.bfloat16)
    low = (table - high.astype(np.float32)).astype(jnp.bfloat16)
    return np.stack([high, low])


HALO_ROWS = ((0, 8), (120, 168), (184, 192), (192, 200), (312, 328), (376, 384))


@functools.lru_cache(maxsize=1)
def tables():
    col_spans = spans(C_DEV)
    row_spans = spans(R_DEV)
    inner = level_table(list(range(384)), 128, (0, 128, 0, 128))
    right = [C_DEV + j if j < 76 else None for j in range(128)] + [None] * 128
    mixed = [None] * 128 + list(range(8)) + [None] * 104 + [j - 16 for j in range(16)]
    room = COL_ROOM[0]
    beyond = level_table(right, room, (256, 292, 256, 264)) + level_table(mixed, room, (-8, 0, -8, 0))
    partial = level_table(right, room, (254, 256, 254, 256))
    outer = np.concatenate(
        [
            beyond[:, 256:384],
            beyond[:, room + 256 : room + 384],
            partial[:, 128:256],
            partial[:, room + 128 : room + 256],
        ],
        axis=1,
    )
    row_src = [i if i < 257 else None for i in range(TILE_ROWS)]
    row_src += [R_DEV + i if i < 76 else None for i in range(UP_ROWS)]
    row_src += [i - 16 if i < 17 else None for i in range(DOWN_ROWS)]
    cols, rows = [], []
    for level in range(4):
        if level:
            cols.append(level_table(col_src, COL_ROOM[level], col_spans[level]))
        rows.append(level_table(row_src, ROW_ROOM[level], row_spans[level]).T)
        col_src = room_sources(COL_ROOM[level], col_spans[level][0], col_spans[level][1])
        row_src = room_sources(ROW_ROOM[level], row_spans[level][0], row_spans[level][1])
    first = rows[0]
    near = np.concatenate([first[start:stop, TILE_ROWS:] for start, stop in HALO_ROWS], axis=0)
    rest = np.ones(first.shape[0], bool)
    for start, stop in HALO_ROWS:
        rest[start:stop] = False
    assert not first[rest, TILE_ROWS:].any()
    return {
        "inner": split(inner),
        "outer": split(outer),
        "own": split(first[:, :TILE_ROWS]),
        "near": split(near),
        "cols": [split(t) for t in cols],
        "rows": [split(t) for t in rows[1:]],
    }


def hi_lo(x):
    high = x.astype(bf16)
    low = (x - high.astype(f32)).astype(bf16)
    return high, low


def mm(a, b):
    return jnp.dot(a, b, preferred_element_type=f32)


def mm_nt(a, b):
    return lax.dot_general(a, b, (((1,), (1,)), ((), ())), preferred_element_type=f32)


def iota(shape, dim):
    return lax.broadcasted_iota(jnp.int32, shape, dim)


GROUPS_PER_STEP = 16
STEPS = BRICKS // 8 // GROUPS_PER_STEP
STEP_BRICKS = BRICKS // STEPS
MESSAGE = 20


def deposit_kernel(
    off_hbm,
    w_hbm,
    counts_hbm,
    owners_hbm,
    slot_hbm,
    out_ref,
    off_ref,
    w_ref,
    counts_ref,
    owners_ref,
    slot_ref,
    cnt_ref,
    patch_ref,
    edge_ref,
    small_sem,
    off_sem,
    w_sem,
):
    small = [
        pltpu.make_async_copy(src, dst, small_sem.at[n])
        for n, (src, dst) in enumerate(
            ((owners_hbm, owners_ref), (slot_hbm, slot_ref), (counts_hbm, counts_ref))
        )
    ]
    for copy in small:
        copy.start()

    def fetch(index):
        off_rows = pl.ds(index * 4 * STEP_BRICKS, 4 * STEP_BRICKS)
        w_rows = pl.ds(index * STEP_BRICKS, STEP_BRICKS)
        return (
            pltpu.make_async_copy(off_hbm.at[off_rows], off_ref.at[off_rows], off_sem.at[index]),
            pltpu.make_async_copy(w_hbm.at[w_rows], w_ref.at[w_rows], w_sem.at[index]),
        )

    for index in range(STEPS):
        for copy in fetch(index):
            copy.start()
    for copy in small:
        copy.wait()

    owners = owners_ref[...]
    dest = (iota((N_DEST, BRICKS), 0) == owners).astype(f32)
    before = (iota((BRICKS, BRICKS), 0) < iota((BRICKS, BRICKS), 1)).astype(bf16)
    ranks = jnp.sum(mm(dest.astype(bf16), before) * dest, axis=0, keepdims=True)
    position = ranks.astype(jnp.int32) * N_DEST + owners

    slot = slot_ref[...]
    grid_row = slot // 32
    grid_col = slot % 32
    coarse = (grid_col % 8) * 4 + grid_col // 8
    row_id = iota((256, BRICKS), 0)
    spread = jnp.where(
        row_id < 128,
        counts_ref[...],
        jnp.where(row_id == 168, coarse, jnp.where(row_id == 169, grid_row, 0)),
    )
    eye = (iota((BRICKS, BRICKS), 0) == iota((BRICKS, BRICKS), 1)).astype(bf16)
    cnt_ref[...] = mm_nt(eye, spread.astype(f32).astype(bf16))

    lane = iota((8, 128), 1)
    sub = iota((8, 128), 0)
    particle = iota((8, PMAX), 1).astype(f32)
    cell = iota((16, PMAX), 0).astype(f32)

    def hat(x, at):
        return jnp.maximum(0.0, 1.0 - jnp.abs(x - at))

    def one_group(start):
        first = pl.multiple_of(start * 4, 32)
        rows_at = jnp.concatenate([off_ref[pl.ds(first + 2 * half, 8, stride=4), :] for half in range(2)], axis=1)
        cols_at = jnp.concatenate([off_ref[pl.ds(first + 2 * half + 1, 8, stride=4), :] for half in range(2)], axis=1)
        count = cnt_ref[pl.ds(start, 8), 0:128]
        count = jnp.concatenate([count, count], axis=1)
        weight = jnp.where(particle < count, w_ref[pl.ds(start, 8), :], 0.0)
        left = jnp.concatenate([hat(rows_at, float(i)) * weight for i in range(17)], axis=0).astype(bf16)
        right = [hat(cols_at[(8 - g) % 8 : (8 - g) % 8 + 1, :], cell) for g in range(8)]
        last = hat(cols_at, 16.0)
        right = jnp.concatenate(right + [last] * 16, axis=0).astype(bf16)
        full = mm_nt(left, right)
        halves = []
        for half in range(2):
            acc = None
            for pair in range(4):
                at = (half * 8 + pair * 2) * 8
                even = pltpu.roll(full[at : at + 8, 0:128], 0, 1, stride=16, stride_axis=0)
                odd = pltpu.roll(full[at + 8 : at + 16, 0:128], 16, 1, stride=16, stride_axis=0)
                both = jnp.where(lane // 16 == 0, even, odd)
                acc = both if pair == 0 else jnp.where(lane // 32 == pair, pltpu.roll(both, 32 * pair, 1), acc)
            halves.append(acc)
        bottom = pltpu.roll(full[128:136, 0:128], 0, 1, stride=16, stride_axis=0)
        corner = jnp.sum(jnp.where(lane == sub, full[128:136, 128:256], 0.0), axis=1, keepdims=True)
        third = jnp.where(lane < 16, bottom, jnp.where(lane == 32, corner, 0.0))
        edge = jnp.zeros((8, 128), f32)
        for i in range(16):
            edge = jnp.where(lane == 8 * i + sub, full[8 * i : 8 * i + 8, 128:256], edge)
        patch_ref[pl.ds(start, 8), 0:128] = halves[0]
        patch_ref[pl.ds(start, 8), 128:256] = halves[1]
        patch_ref[pl.ds(start, 8), 256:384] = third + cnt_ref[pl.ds(start, 8), 128:256]
        edge_ref[pl.ds(start, 8), :] = edge

    def step(index, carry):
        for copy in fetch(index):
            copy.wait()
        for sub_group in range(GROUPS_PER_STEP):
            one_group(pl.multiple_of((index * GROUPS_PER_STEP + sub_group) * 8, 8))
        return carry

    lax.fori_loop(0, STEPS, step, 0)

    gather = (iota((128, 128), 1) == iota((128, 128), 0) // 8 + 16).astype(bf16)
    edge_high, edge_low = hi_lo(edge_ref[...])
    third = patch_ref[:, 256:384] + (mm(edge_high, gather) + mm(edge_low, gather))

    high, low = hi_lo(patch_ref[:, 0:256])
    ends = jnp.concatenate(hi_lo(third), axis=1)
    lane_wide = iota((N_DEST, 128), 1)
    for pair in range(4):
        edges = []
        for rank in (2 * pair, 2 * pair + 1):
            pick = (iota((N_DEST, BRICKS), 0) + rank * N_DEST == position).astype(bf16)
            inner = mm(pick, high) + mm(pick, low)
            out_ref[pl.ds(rank, N_DEST, stride=MESSAGE), :] = inner[:, 0:128]
            out_ref[pl.ds(8 + rank, N_DEST, stride=MESSAGE), :] = inner[:, 128:256]
            both = mm(pick, ends)
            edges.append(both[:, 0:128] + both[:, 128:256])
        joined = jnp.where(lane_wide < 64, edges[0], pltpu.roll(edges[1], 64, 1))
        out_ref[pl.ds(16 + pair, N_DEST, stride=MESSAGE), :] = joined


def deposit_and_pack(offsets, weights, counts, owners, slots):
    flat = offsets.reshape(BRICKS, 2, 2, 128).transpose(0, 2, 1, 3).reshape(4 * BRICKS, 128)
    return pl.pallas_call(
        deposit_kernel,
        out_shape=jax.ShapeDtypeStruct((N_DEST * MESSAGE, 128), f32),
        in_specs=[pl.BlockSpec(memory_space=pltpu.MemorySpace.HBM)] * 5,
        scratch_shapes=[
            pltpu.VMEM((4 * BRICKS, 128), f32),
            pltpu.VMEM((BRICKS, PMAX), f32),
            pltpu.VMEM((1, BRICKS), jnp.int32),
            pltpu.VMEM((1, BRICKS), jnp.int32),
            pltpu.VMEM((1, BRICKS), jnp.int32),
            pltpu.VMEM((BRICKS, 256), f32),
            pltpu.VMEM((BRICKS, 384), f32),
            pltpu.VMEM((BRICKS, 128), f32),
            pltpu.SemaphoreType.DMA((3,)),
            pltpu.SemaphoreType.DMA((STEPS,)),
            pltpu.SemaphoreType.DMA((STEPS,)),
        ],
        compiler_params=pltpu.CompilerParams(vmem_limit_bytes=40 << 20),
        name="deposit",
    )(*(pltpu.with_memory_space_constraint(x, pltpu.MemorySpace.HBM) for x in (
        flat,
        weights,
        counts.reshape(1, BRICKS),
        owners.reshape(1, BRICKS),
        slots.reshape(1, BRICKS),
    )))


def mm3(data, table):
    high, low = hi_lo(data)
    return mm(high, table[0]) + (mm(low, table[0]) + mm(high, table[1]))


def mm3_left(table, data):
    high, low = hi_lo(data)
    return mm(table[0], high) + (mm(table[0], low) + mm(table[1], high))


def place(x_ref, grid_ref, blocks):
    lane8 = iota((8, 128), 1)
    upper = jnp.concatenate([x_ref[pl.ds(rank, N_DEST, stride=MESSAGE), :] for rank in range(8)], axis=0)
    lower = jnp.concatenate([x_ref[pl.ds(8 + rank, N_DEST, stride=MESSAGE), :] for rank in range(8)], axis=0)
    ends = []
    for pair in range(4):
        joined = x_ref[pl.ds(16 + pair, N_DEST, stride=MESSAGE), :]
        ends += [joined, pltpu.roll(joined, 64, 1)]
    ends_high, ends_low = hi_lo(jnp.concatenate(ends, axis=0))
    weigh = jnp.where(lane8 == 40, 16.0, jnp.where(lane8 == 41, 1.0, 0.0)).astype(bf16)
    slot = mm_nt(weigh, ends_high)[0:1, :].astype(jnp.int32)
    high, low = hi_lo(jnp.concatenate([upper, lower], axis=1))
    ends = jnp.concatenate([ends_high, ends_low], axis=1)
    row = iota((128, SLOTS), 0)
    for at, block in enumerate(blocks):
        rows = slice(at * 128, (at + 1) * 128)
        pick = ((row // 16) * 64 + row % 16 + block * 16 == slot).astype(bf16)
        grid_ref[rows, 0:256] = mm(pick, high) + mm(pick, low)
        both = mm(pick, ends)
        grid_ref[rows, 256:384] = both[:, 0:128] + both[:, 128:256]


def swap_groups(tiles):
    group = iota((8, 128), 1) // 16
    for d in (1, 2, 4):
        mask = (group // d) % 2 == 0
        new = list(tiles)
        for a in range(8):
            if (a // d) % 2 == 0:
                one, two = tiles[a], tiles[a + d]
                new[a] = jnp.where(mask, one, pltpu.roll(two, 16 * d, 1))
                new[a + d] = jnp.where(mask, pltpu.roll(one, 128 - 16 * d, 1), two)
        tiles = new
    return tiles


def turn(side, corner):
    turned = [[pltpu.roll(side[half], 16 - i, 1) for half in range(2)] for i in range(16)]
    return turned + [[pltpu.roll(corner[half], 16, 1) for half in range(2)]]


def unpack_block(grid_ref, at):
    rows = [[None, None] for _ in range(17)]
    side, corner = [None, None], [None, None]
    for half in range(2):
        parts = []
        for third in range(3):
            parts.append(
                swap_groups(
                    [
                        grid_ref[at * 128 + col * 16 + half * 8 : at * 128 + col * 16 + half * 8 + 8, third * 128 : (third + 1) * 128]
                        for col in range(8)
                    ]
                )
            )
        for i in range(8):
            rows[i][half] = parts[0][i]
            rows[8 + i][half] = parts[1][i]
        rows[16][half] = parts[2][0]
        side[half] = parts[2][1]
        corner[half] = parts[2][2]
    return rows, side, corner


def add_spills(rows, turned, previous):
    lane8 = iota((8, 128), 1)
    out = []
    for i in range(17):
        pair = []
        for half in range(2):
            spill = jnp.where(lane8 % 16 == 0, turned[i][half], 0.0)
            first = 0.0 if previous is None else previous[i][half]
            pair.append(rows[i][half] + jnp.where(lane8 == 0, first, spill))
        out.append(pair)
    return out


def store_block(rows, ref):
    sub = iota((8, 128), 0)
    down = [pltpu.roll(rows[16][half], 1, 0) for half in range(2)]
    for i in range(16):
        low, high = rows[i]
        if i == 0:
            low = low + jnp.where(sub == 0, 0.0, down[0])
            high = high + jnp.where(sub == 0, down[0], down[1])
        ref[pl.ds(i, 8, stride=16), :] = low
        ref[pl.ds(128 + i, 8, stride=16), :] = high
    ref[256:264, :] = jnp.where(sub == 0, down[1], 0.0)
    ref[264:TILE_ROWS, :] = jnp.zeros((8, 128), f32)


def place_edges_kernel(x_ref, first_ref, last_ref, right_ref, carry_ref, grid_ref):
    place(x_ref, grid_ref, (0, 3))
    lane8 = iota((8, 128), 1)
    rows, side, corner = unpack_block(grid_ref, 0)
    store_block(add_spills(rows, turn(side, corner), None), first_ref)
    for half in range(2):
        carry_ref[half * 8 : half * 8 + 8, :] = side[half]
        carry_ref[16 + half * 8 : 24 + half * 8, :] = corner[half]
    rows, side, corner = unpack_block(grid_ref, 1)
    turned = turn(side, corner)
    rows = add_spills(rows, turned, None)
    store_block(rows, last_ref)
    store_block(
        [[jnp.where(lane8 == 0, turned[i][half], rows[i][half]) for half in range(2)] for i in range(17)], right_ref
    )


def place_edges(arrived):
    tile = jax.ShapeDtypeStruct((TILE_ROWS, 128), f32)
    return pl.pallas_call(
        place_edges_kernel,
        out_shape=(tile, tile, tile, jax.ShapeDtypeStruct((32, 128), f32)),
        scratch_shapes=[pltpu.VMEM((256, 384), f32)],
        compiler_params=pltpu.CompilerParams(vmem_limit_bytes=32 << 20),
        cost_estimate=pl.CostEstimate(flops=600_000_000, bytes_accessed=2_000_000, transcendentals=0),
        name="place_edges",
    )(arrived)


def place_inner_kernel(x_ref, carry_ref, first_ref, last_ref, inner_ref, own_ref, grid_ref, second_ref, third_ref, fix_ref):
    place(x_ref, grid_ref, (1, 2))
    lane8 = iota((8, 128), 1)
    previous = turn(
        [carry_ref[half * 8 : half * 8 + 8, :] for half in range(2)],
        [carry_ref[16 + half * 8 : 24 + half * 8, :] for half in range(2)],
    )
    for at, ref in enumerate((second_ref, third_ref)):
        rows, side, corner = unpack_block(grid_ref, at)
        turned = turn(side, corner)
        store_block(add_spills(rows, turned, previous), ref)
        previous = turned
    store_block([[jnp.where(lane8 == 0, previous[i][half], 0.0) for half in range(2)] for i in range(17)], fix_ref)
    left = jnp.concatenate([first_ref[...], second_ref[...], third_ref[...]], axis=1)
    right = jnp.concatenate([third_ref[...], last_ref[...] + fix_ref[...]], axis=1)
    own_ref[:, 0:256] = mm3(left, inner_ref)
    own_ref[:, 256:512] = mm3(right, inner_ref[:, 0:256, :])


def place_inner(arrived, carry, first, last, inner):
    tile = pltpu.VMEM((TILE_ROWS, 128), f32)
    return pl.pallas_call(
        place_inner_kernel,
        out_shape=jax.ShapeDtypeStruct((TILE_ROWS, 512), f32),
        scratch_shapes=[pltpu.VMEM((256, 384), f32), tile, tile, tile],
        compiler_params=pltpu.CompilerParams(vmem_limit_bytes=32 << 20),
        cost_estimate=pl.CostEstimate(flops=800_000_000, bytes_accessed=3_000_000, transcendentals=0),
        name="place_inner",
    )(arrived, carry, first, last, inner)


def columns_kernel(own_ref, first_ref, to_right_ref, from_right_ref, from_left_ref, outer_ref, out_ref, up_ref, down_ref):
    lane = iota((TILE_ROWS, 128), 1)
    from_left = from_left_ref[...]
    spill = jnp.where(lane == 0, from_left, 0.0)
    right = from_right_ref[...] + jnp.where(lane == 0, to_right_ref[...], 0.0)
    mixed = jnp.where(lane < 8, first_ref[...] + spill, jnp.where(lane >= 112, from_left, 0.0))
    outer = mm3(jnp.concatenate([right, mixed], axis=1), outer_ref)
    pieces = [
        own_ref[:, 0:128] + taps_low[0] * spill,
        own_ref[:, 256:384] + outer[:, 256:384],
        outer[:, 0:128],
        own_ref[:, 128:256] + taps_high[0] * spill,
        own_ref[:, 384:512] + outer[:, 384:512],
        outer[:, 128:256],
    ]
    for at, piece in enumerate(pieces):
        cols = slice(at * 128, (at + 1) * 128)
        out_ref[:, cols] = piece
        up_ref[:, cols] = piece[0:UP_ROWS]
        down_ref[:, cols] = piece[DOWN_FROM : DOWN_FROM + DOWN_ROWS]


def outer_columns(own, first, to_right, from_right, from_left, outer):
    width = 2 * COL_ROOM[0]
    return pl.pallas_call(
        columns_kernel,
        out_shape=(
            jax.ShapeDtypeStruct((TILE_ROWS, width), f32),
            jax.ShapeDtypeStruct((UP_ROWS, width), f32),
            jax.ShapeDtypeStruct((DOWN_ROWS, width), f32),
        ),
        compiler_params=pltpu.CompilerParams(vmem_limit_bytes=32 << 20),
        cost_estimate=pl.CostEstimate(flops=220_000_000, bytes_accessed=2_000_000, transcendentals=0),
        name="columns",
    )(own, first, to_right, from_right, from_left, outer)


def own_rows_kernel(own_ref, table_ref, out_ref):
    for at in range(3):
        cols = slice(at * 256, (at + 1) * 256)
        out_ref[:, cols] = mm3_left(table_ref, own_ref[:, cols])


def own_rows(own, table):
    return pl.pallas_call(
        own_rows_kernel,
        out_shape=jax.ShapeDtypeStruct((2 * ROW_ROOM[0], 2 * COL_ROOM[0]), f32),
        compiler_params=pltpu.CompilerParams(vmem_limit_bytes=32 << 20),
        cost_estimate=pl.CostEstimate(flops=480_000_000, bytes_accessed=2_000_000, transcendentals=0),
        name="own_rows",
    )(own, table)


def levels_kernel(part_ref, below_ref, above_ref, near_ref, *refs):
    col_refs = (None,) + refs[0:3]
    row_refs = (None,) + refs[3:6]
    leader_refs = refs[6:10]
    approx_ref = refs[10]
    peak_ref = refs[11]
    near = mm3_left(near_ref, jnp.concatenate([below_ref[...], above_ref[...]], axis=0))
    pieces = []
    at, done = 0, 0
    for start, stop in HALO_ROWS:
        if start > done:
            pieces.append(part_ref[done:start, :])
        pieces.append(part_ref[start:stop, :] + near[at : at + stop - start])
        at += stop - start
        done = stop
    both = jnp.concatenate(pieces, axis=0)
    peak = None
    for level in range(4):
        room_r = ROW_ROOM[level]
        room_c = COL_ROOM[level]
        if level:
            both = mm3_left(row_refs[level], mm3(current, col_refs[level]))
        current = both[:room_r, :room_c]
        detail_a = both[:room_r, room_c:]
        detail_b = both[room_r:, :room_c]
        detail_c = both[room_r:, room_c:]
        now = jnp.maximum(jnp.maximum(jnp.abs(detail_a), jnp.abs(detail_b)), jnp.abs(detail_c))
        if peak is not None:
            now = jnp.maximum(now, peak)
        wide = jnp.maximum(now, jnp.maximum(pltpu.roll(now, 1, 1), pltpu.roll(now, room_c - 1, 1)))
        wide = jnp.maximum(wide, jnp.maximum(pltpu.roll(wide, 1, 0), pltpu.roll(wide, room_r - 1, 0)))
        n_r = R_DEV >> (level + 1)
        n_c = C_DEV >> (level + 1)
        leader_refs[level][...] = wide[:n_r, :n_c]
        if level < 3:
            pairs = jnp.maximum(now, pltpu.roll(now, room_c - 1, 1))
            pooled = []
            for across in range(room_c // 128):
                top = across * ROW_ROOM[0]
                peak_ref[top : top + room_r, :] = pairs[:, across * 128 : (across + 1) * 128]
                pooled.append(
                    jnp.maximum(
                        peak_ref[pl.ds(top, room_r // 2, stride=2), :],
                        peak_ref[pl.ds(top + 1, room_r // 2, stride=2), :],
                    )
                )
            high, low = hi_lo(jnp.concatenate(pooled, axis=1) if len(pooled) > 1 else pooled[0])
            room_n = COL_ROOM[level + 1]
            out = iota((room_c, room_n), 1)
            source = 2 * out + jnp.where(out < 3 * room_n // 4, 0, room_c - 2 * room_n)
            pick = (iota((room_c, room_n), 0) == source).astype(bf16)
            peak = mm(high, pick) + mm(low, pick)
    approx_ref[...] = current[: R_DEV >> 4, : C_DEV >> 4]


def all_levels(part, below, above, near, cols, rows):
    shapes = [(R_DEV >> level, C_DEV >> level) for level in (1, 2, 3, 4, 4)]
    return pl.pallas_call(
        levels_kernel,
        out_shape=tuple(jax.ShapeDtypeStruct(shape, f32) for shape in shapes),
        scratch_shapes=[pltpu.VMEM((3 * ROW_ROOM[0], 128), f32)],
        compiler_params=pltpu.CompilerParams(vmem_limit_bytes=32 << 20),
        name="levels",
    )(part, below, above, near, *cols, *rows)


def shifted(x, axis, by):
    size = lax.axis_size(axis)
    return lax.ppermute(x, axis, [(i, (i + by) % size) for i in range(size)])


def transform(arrived):
    table = jax.tree.map(jnp.asarray, tables())
    first, last, to_right, carry = place_edges(arrived)
    from_right = shifted(first, "cols", -1)
    from_left = shifted(to_right, "cols", 1)
    inner = place_inner(arrived, carry, first, last, table["inner"])
    own, to_up, to_down = outer_columns(inner, first, to_right, from_right, from_left, table["outer"])
    below = shifted(to_up, "rows", -1)
    above = shifted(to_down, "rows", 1)
    part = own_rows(own, table["own"])
    return all_levels(part, below, above, table["near"], table["cols"], table["rows"])


def on_device(offsets, lens_weight, counts, owners, brick_slot):
    packed = deposit_and_pack(offsets, lens_weight, counts, owners, brick_slot)
    arrived = lax.all_to_all(
        packed.reshape(N_DEST, MESSAGE // 4, 4, 128), ("rows", "cols"), split_axis=0, concat_axis=0, tiled=True
    )
    return transform(arrived.reshape(N_DEST * MESSAGE, 128))


def solution(mesh):
    placed = (
        P(("rows", "cols"), None, None),
        P(("rows", "cols"), None),
        P(("rows", "cols")),
        P(("rows", "cols")),
        P(("rows", "cols")),
    )
    return jax.shard_map(
        on_device,
        mesh=mesh,
        in_specs=placed,
        out_specs=(P("rows", "cols"),) * 5,
        check_vma=False,
    )
```

```python
import functools

import jax
import jax.numpy as jnp
import numpy as np
from jax import lax
from jax.experimental import pallas as pl
from jax.experimental.pallas import tpu as pltpu
from jax.sharding import PartitionSpec as P

R_DEV = 256
C_DEV = 512
PMAX = 256
CAP = 8
N_DEST = 128
BRICKS = 512
SLOTS = N_DEST * CAP

TILE_ROWS = 272
UP_ROWS = 80
DOWN_ROWS = 24
DOWN_FROM = 240
ROW_ROOM = (192, 96, 48, 24)
COL_ROOM = (384, 256, 128, 128)

taps_low = (
    0.33267055295008263,
    0.8068915093110925,
    0.4598775021184915,
    -0.13501102001025458,
    -0.08544127388202666,
    0.03522629188570953,
)
taps_high = tuple(((-1.0) ** index * taps_low[5 - index] for index in range(6)))

f32 = jnp.float32
bf16 = jnp.bfloat16


def spans(size):
    out = []
    for level in range(1, 5):
        n = size >> level
        before = 8 >> (level - 1)
        after = (36, 16, 6, 1)[level - 1]
        out.append((-before, n + after, -before, n + before))
    return out


def level_table(sources, room, span):
    low_from, low_to, high_from, high_to = span
    table = np.zeros((len(sources), 2 * room), np.float64)
    for position, index in enumerate(sources):
        if index is None:
            continue
        for half, (lo, hi, taps) in enumerate(
            ((low_from, low_to, taps_low), (high_from, high_to, taps_high))
        ):
            for tap in range(6):
                if (index - tap) % 2 == 0:
                    k = (index - tap) // 2
                    if lo <= k < hi:
                        table[position, half * room + (k % room)] += taps[tap]
    return table


def room_sources(room, low_from, low_to):
    out = [None] * room
    for k in range(low_from, low_to):
        out[k % room] = k
    return out


def split(table):
    table = np.asarray(table, np.float32)
    high = table.astype(jnp.bfloat16)
    low = (table - high.astype(np.float32)).astype(jnp.bfloat16)
    return np.stack([high, low])


HALO_ROWS = ((0, 8), (120, 168), (184, 192), (192, 200), (312, 328), (376, 384))


@functools.lru_cache(maxsize=1)
def tables():
    col_spans = spans(C_DEV)
    row_spans = spans(R_DEV)
    inner = level_table(list(range(384)), 128, (0, 128, 0, 128))
    right = [C_DEV + j if j < 76 else None for j in range(128)] + [None] * 128
    mixed = [None] * 128 + list(range(8)) + [None] * 104 + [j - 16 for j in range(16)]
    room = COL_ROOM[0]
    beyond = level_table(right, room, (256, 292, 256, 264)) + level_table(mixed, room, (-8, 0, -8, 0))
    partial = level_table(right, room, (254, 256, 254, 256))
    outer = np.concatenate(
        [
            beyond[:, 256:384],
            beyond[:, room + 256 : room + 384],
            partial[:, 128:256],
            partial[:, room + 128 : room + 256],
        ],
        axis=1,
    )
    row_src = [i if i < 257 else None for i in range(TILE_ROWS)]
    row_src += [R_DEV + i if i < 76 else None for i in range(UP_ROWS)]
    row_src += [i - 16 if i < 17 else None for i in range(DOWN_ROWS)]
    third = [256 + j if j < 36 else j - 128 if j >= 120 else None for j in range(128)] + [None] * 128
    room = COL_ROOM[1]
    rest = level_table(third, room, col_spans[1])
    rest += level_table([None] * 128 + list(range(8)) + [None] * 120, room, (-4, 0, -4, 0))
    rest = np.concatenate([rest[:, 128:256], rest[:, room + 128 : room + 256]], axis=1)
    cols, rows = [rest], []
    for level in range(4):
        if level > 1:
            cols.append(level_table(col_src, COL_ROOM[level], col_spans[level]))
        rows.append(level_table(row_src, ROW_ROOM[level], row_spans[level]).T)
        col_src = room_sources(COL_ROOM[level], col_spans[level][0], col_spans[level][1])
        row_src = room_sources(ROW_ROOM[level], row_spans[level][0], row_spans[level][1])
    first = rows[0]
    near = np.concatenate([first[start:stop, TILE_ROWS:] for start, stop in HALO_ROWS], axis=0)
    far = np.ones(first.shape[0], bool)
    for start, stop in HALO_ROWS:
        far[start:stop] = False
    assert not first[far, TILE_ROWS:].any()
    return {
        "inner": split(inner),
        "outer": split(outer),
        "own": split(first[:, :TILE_ROWS]),
        "near": split(near),
        "cols": [split(t) for t in cols],
        "rows": [split(t) for t in rows[1:]],
    }


def hi_lo(x):
    high = x.astype(bf16)
    low = (x - high.astype(f32)).astype(bf16)
    return high, low


def mm(a, b):
    return jnp.dot(a, b, preferred_element_type=f32)


def mm_nt(a, b):
    return lax.dot_general(a, b, (((1,), (1,)), ((), ())), preferred_element_type=f32)


def iota(shape, dim):
    return lax.broadcasted_iota(jnp.int32, shape, dim)


STEPS = 4
STEP_BRICKS = BRICKS // STEPS
MESSAGE = 20


def deposit_kernel(
    off_hbm,
    w_hbm,
    counts_hbm,
    owners_hbm,
    slot_hbm,
    out_ref,
    off_ref,
    w_ref,
    counts_ref,
    owners_ref,
    slot_ref,
    cnt_ref,
    patch_ref,
    edge_ref,
    small_sem,
    off_sem,
    w_sem,
):
    small = [
        pltpu.make_async_copy(src, dst, small_sem.at[n])
        for n, (src, dst) in enumerate(
            ((owners_hbm, owners_ref), (slot_hbm, slot_ref), (counts_hbm, counts_ref))
        )
    ]
    for copy in small:
        copy.start()

    def fetch(index):
        off_rows = pl.ds(index * 4 * STEP_BRICKS, 4 * STEP_BRICKS)
        w_rows = pl.ds(index * STEP_BRICKS, STEP_BRICKS)
        return (
            pltpu.make_async_copy(off_hbm.at[off_rows], off_ref.at[off_rows], off_sem.at[index]),
            pltpu.make_async_copy(w_hbm.at[w_rows], w_ref.at[w_rows], w_sem.at[index]),
        )

    for index in range(STEPS):
        for copy in fetch(index):
            copy.start()
    for copy in small:
        copy.wait()

    owners = owners_ref[...]
    dest = (iota((N_DEST, BRICKS), 0) == owners).astype(f32)
    before = (iota((BRICKS, BRICKS), 0) < iota((BRICKS, BRICKS), 1)).astype(bf16)
    ranks = jnp.sum(mm(dest.astype(bf16), before) * dest, axis=0, keepdims=True)
    position = ranks.astype(jnp.int32) * N_DEST + owners

    slot = slot_ref[...]
    grid_row = slot // 32
    grid_col = slot % 32
    coarse = (grid_col % 8) * 4 + grid_col // 8
    row_id = iota((256, BRICKS), 0)
    spread = jnp.where(
        row_id < 128,
        counts_ref[...],
        jnp.where(row_id == 168, coarse, jnp.where(row_id == 169, grid_row, 0)),
    )
    eye = (iota((BRICKS, BRICKS), 0) == iota((BRICKS, BRICKS), 1)).astype(bf16)
    cnt_ref[...] = mm_nt(eye, spread.astype(f32).astype(bf16))

    lane = iota((8, 128), 1)
    sub = iota((8, 128), 0)
    particle = iota((8, PMAX), 1).astype(f32)
    cell = iota((16, PMAX), 0).astype(f32)

    zero = jnp.zeros((), bf16)
    bit = {at: (lane >> at) % 2 == 1 for at in (3, 4, 5, 6)}

    def choose(tiles, mask):
        return [jnp.where(mask, odd, even) for even, odd in zip(tiles[0::2], tiles[1::2])]

    def one_group(start):
        first = start * 4
        rows_at = jnp.concatenate([off_ref[pl.ds(first + 2 * half, 8, stride=4), :] for half in range(2)], axis=1)
        cols_at = jnp.concatenate([off_ref[pl.ds(first + 2 * half + 1, 8, stride=4), :] for half in range(2)], axis=1)
        count = cnt_ref[pl.ds(start, 8), 0:128]
        count = jnp.concatenate([count, count], axis=1)
        weight = jnp.where(particle < count, w_ref[pl.ds(start, 8), :], 0.0)
        lag = rows_at * weight
        left = []
        for i in range(17):
            left.append(weight - jnp.abs(lag))
            lag = lag - weight
        left = jnp.maximum(jnp.concatenate(left, axis=0).astype(bf16), zero)
        right = []
        for g in range(8):
            at = first + 4 * ((8 - g) % 8) + 1
            column = jnp.concatenate([off_ref[pl.ds(at + 2 * half, 8, stride=0), :] for half in range(2)], axis=1)
            right += [1.0 - jnp.abs(column - cell[0:8]), 1.0 - jnp.abs(column - cell[8:16])]
        last = cols_at - 15.0
        right = [jnp.maximum(jnp.concatenate(right, axis=0).astype(bf16), zero)]
        right += [jnp.maximum(jnp.concatenate([last, last], axis=0).astype(bf16), zero)] * 8
        full = mm_nt(left, jnp.concatenate(right, axis=0))
        halves = []
        for half in range(2):
            pairs = []
            for pair in range(4):
                at = (half * 8 + pair * 2) * 8
                even = pltpu.roll(full[at : at + 8, 0:128], 0, 1, stride=16, stride_axis=0)
                odd = pltpu.roll(full[at + 8 : at + 16, 0:128], 16, 1, stride=16, stride_axis=0)
                both = jnp.where(bit[4], odd, even)
                pairs.append(pltpu.roll(both, 32 * pair, 1) if pair else both)
            halves.append(choose(choose(pairs, bit[5]), bit[6])[0])
        bottom = pltpu.roll(full[128:136, 0:128], 0, 1, stride=16, stride_axis=0)
        corner = jnp.sum(jnp.where(lane == sub, full[128:136, 128:256], 0.0), axis=1, keepdims=True)
        third = jnp.where(lane < 16, bottom, jnp.where(lane == 32, corner, 0.0))
        edge = [full[8 * i : 8 * i + 8, 128:256] for i in range(16)]
        for at in range(3, 7):
            edge = choose(edge, bit[at])
        edge = jnp.where(lane % 8 == sub, edge[0], 0.0)
        patch_ref[pl.ds(start, 8), 0:128] = halves[0]
        patch_ref[pl.ds(start, 8), 128:256] = halves[1]
        patch_ref[pl.ds(start, 8), 256:384] = third + cnt_ref[pl.ds(start, 8), 128:256]
        edge_ref[pl.ds(start, 8), :] = edge

    for index in range(STEPS):
        for copy in fetch(index):
            copy.wait()
    for group in range(BRICKS // 8):
        one_group(group * 8)

    gather = (iota((128, 128), 1) == iota((128, 128), 0) // 8 + 16).astype(bf16)
    edge_high, edge_low = hi_lo(edge_ref[...])
    third = patch_ref[:, 256:384] + (mm(edge_high, gather) + mm(edge_low, gather))

    high, low = hi_lo(patch_ref[:, 0:256])
    ends = jnp.concatenate(hi_lo(third), axis=1)
    lane_wide = iota((N_DEST, 128), 1)
    for pair in range(4):
        edges = []
        for rank in (2 * pair, 2 * pair + 1):
            pick = (iota((N_DEST, BRICKS), 0) + rank * N_DEST == position).astype(bf16)
            inner = mm(pick, high) + mm(pick, low)
            out_ref[pl.ds(rank, N_DEST, stride=MESSAGE), :] = inner[:, 0:128]
            out_ref[pl.ds(8 + rank, N_DEST, stride=MESSAGE), :] = inner[:, 128:256]
            both = mm(pick, ends)
            edges.append(both[:, 0:128] + both[:, 128:256])
        joined = jnp.where(lane_wide < 64, edges[0], pltpu.roll(edges[1], 64, 1))
        out_ref[pl.ds(16 + pair, N_DEST, stride=MESSAGE), :] = joined


def deposit_and_pack(offsets, weights, counts, owners, slots):
    flat = offsets.reshape(BRICKS, 2, 2, 128).transpose(0, 2, 1, 3).reshape(4 * BRICKS, 128)
    return pl.pallas_call(
        deposit_kernel,
        out_shape=jax.ShapeDtypeStruct((N_DEST * MESSAGE, 128), f32),
        in_specs=[pl.BlockSpec(memory_space=pltpu.MemorySpace.HBM)] * 5,
        scratch_shapes=[
            pltpu.VMEM((4 * BRICKS, 128), f32),
            pltpu.VMEM((BRICKS, PMAX), f32),
            pltpu.VMEM((1, BRICKS), jnp.int32),
            pltpu.VMEM((1, BRICKS), jnp.int32),
            pltpu.VMEM((1, BRICKS), jnp.int32),
            pltpu.VMEM((BRICKS, 256), f32),
            pltpu.VMEM((BRICKS, 384), f32),
            pltpu.VMEM((BRICKS, 128), f32),
            pltpu.SemaphoreType.DMA((3,)),
            pltpu.SemaphoreType.DMA((STEPS,)),
            pltpu.SemaphoreType.DMA((STEPS,)),
        ],
        compiler_params=pltpu.CompilerParams(vmem_limit_bytes=40 << 20),
        name="deposit",
    )(*(pltpu.with_memory_space_constraint(x, pltpu.MemorySpace.HBM) for x in (
        flat,
        weights,
        counts.reshape(1, BRICKS),
        owners.reshape(1, BRICKS),
        slots.reshape(1, BRICKS),
    )))


def mm3(data, table):
    high, low = hi_lo(data)
    return mm(high, table[0]) + (mm(low, table[0]) + mm(high, table[1]))


def mm3_left(table, data):
    high, low = hi_lo(data)
    return mm(table[0], high) + (mm(table[0], low) + mm(table[1], high))


def place(x_ref, grid_ref, blocks):
    lane8 = iota((8, 128), 1)
    upper = jnp.concatenate([x_ref[pl.ds(rank, N_DEST, stride=MESSAGE), :] for rank in range(8)], axis=0)
    lower = jnp.concatenate([x_ref[pl.ds(8 + rank, N_DEST, stride=MESSAGE), :] for rank in range(8)], axis=0)
    ends = []
    for pair in range(4):
        joined = x_ref[pl.ds(16 + pair, N_DEST, stride=MESSAGE), :]
        ends += [joined, pltpu.roll(joined, 64, 1)]
    ends_high, ends_low = hi_lo(jnp.concatenate(ends, axis=0))
    weigh = jnp.where(lane8 == 40, 16.0, jnp.where(lane8 == 41, 1.0, 0.0)).astype(bf16)
    slot = mm_nt(weigh, ends_high)[0:1, :].astype(jnp.int32)
    high, low = hi_lo(jnp.concatenate([upper, lower], axis=1))
    ends = jnp.concatenate([ends_high, ends_low], axis=1)
    row = iota((128, SLOTS), 0)
    for at, block in enumerate(blocks):
        rows = slice(at * 128, (at + 1) * 128)
        pick = ((row // 16) * 64 + row % 16 + block * 16 == slot).astype(bf16)
        grid_ref[rows, 0:256] = mm(pick, high) + mm(pick, low)
        both = mm(pick, ends)
        grid_ref[rows, 256:384] = both[:, 0:128] + both[:, 128:256]


def swap_groups(tiles):
    group = iota((8, 128), 1) // 16
    for d in (1, 2, 4):
        mask = (group // d) % 2 == 0
        new = list(tiles)
        for a in range(8):
            if (a // d) % 2 == 0:
                one, two = tiles[a], tiles[a + d]
                new[a] = jnp.where(mask, one, pltpu.roll(two, 16 * d, 1))
                new[a + d] = jnp.where(mask, pltpu.roll(one, 128 - 16 * d, 1), two)
        tiles = new
    return tiles


def turn(side, corner):
    turned = [[pltpu.roll(side[half], 16 - i, 1) for half in range(2)] for i in range(16)]
    return turned + [[pltpu.roll(corner[half], 16, 1) for half in range(2)]]


def unpack_block(grid_ref, at):
    rows = [[None, None] for _ in range(17)]
    side, corner = [None, None], [None, None]
    for half in range(2):
        parts = []
        for third in range(3):
            parts.append(
                swap_groups(
                    [
                        grid_ref[at * 128 + col * 16 + half * 8 : at * 128 + col * 16 + half * 8 + 8, third * 128 : (third + 1) * 128]
                        for col in range(8)
                    ]
                )
            )
        for i in range(8):
            rows[i][half] = parts[0][i]
            rows[8 + i][half] = parts[1][i]
        rows[16][half] = parts[2][0]
        side[half] = parts[2][1]
        corner[half] = parts[2][2]
    return rows, side, corner


def add_spills(rows, turned, previous):
    lane8 = iota((8, 128), 1)
    out = []
    for i in range(17):
        pair = []
        for half in range(2):
            spill = jnp.where(lane8 % 16 == 0, turned[i][half], 0.0)
            first = 0.0 if previous is None else previous[i][half]
            pair.append(rows[i][half] + jnp.where(lane8 == 0, first, spill))
        out.append(pair)
    return out


def store_block(rows, ref):
    sub = iota((8, 128), 0)
    down = [pltpu.roll(rows[16][half], 1, 0) for half in range(2)]
    for i in range(16):
        low, high = rows[i]
        if i == 0:
            low = low + jnp.where(sub == 0, 0.0, down[0])
            high = high + jnp.where(sub == 0, down[0], down[1])
        ref[pl.ds(i, 8, stride=16), :] = low
        ref[pl.ds(128 + i, 8, stride=16), :] = high
    ref[256:264, :] = jnp.where(sub == 0, down[1], 0.0)
    ref[264:TILE_ROWS, :] = jnp.zeros((8, 128), f32)


def place_edges_kernel(x_ref, first_ref, last_ref, right_ref, carry_ref, grid_ref):
    place(x_ref, grid_ref, (0, 3))
    lane8 = iota((8, 128), 1)
    rows, side, corner = unpack_block(grid_ref, 0)
    store_block(add_spills(rows, turn(side, corner), None), first_ref)
    for half in range(2):
        carry_ref[half * 8 : half * 8 + 8, :] = side[half]
        carry_ref[16 + half * 8 : 24 + half * 8, :] = corner[half]
    rows, side, corner = unpack_block(grid_ref, 1)
    turned = turn(side, corner)
    rows = add_spills(rows, turned, None)
    store_block(rows, last_ref)
    store_block(
        [[jnp.where(lane8 == 0, turned[i][half], rows[i][half]) for half in range(2)] for i in range(17)], right_ref
    )


def place_edges(arrived):
    tile = jax.ShapeDtypeStruct((TILE_ROWS, 128), f32)
    return pl.pallas_call(
        place_edges_kernel,
        out_shape=(tile, tile, tile, jax.ShapeDtypeStruct((32, 128), f32)),
        scratch_shapes=[pltpu.VMEM((256, 384), f32)],
        compiler_params=pltpu.CompilerParams(vmem_limit_bytes=32 << 20),
        cost_estimate=pl.CostEstimate(flops=600_000_000, bytes_accessed=2_000_000, transcendentals=0),
        name="place_edges",
    )(arrived)


def place_inner_kernel(x_ref, carry_ref, first_ref, last_ref, inner_ref, own_ref, grid_ref, second_ref, third_ref, fix_ref):
    place(x_ref, grid_ref, (1, 2))
    lane8 = iota((8, 128), 1)
    previous = turn(
        [carry_ref[half * 8 : half * 8 + 8, :] for half in range(2)],
        [carry_ref[16 + half * 8 : 24 + half * 8, :] for half in range(2)],
    )
    for at, ref in enumerate((second_ref, third_ref)):
        rows, side, corner = unpack_block(grid_ref, at)
        turned = turn(side, corner)
        store_block(add_spills(rows, turned, previous), ref)
        previous = turned
    store_block([[jnp.where(lane8 == 0, previous[i][half], 0.0) for half in range(2)] for i in range(17)], fix_ref)
    left = jnp.concatenate([first_ref[...], second_ref[...], third_ref[...]], axis=1)
    right = jnp.concatenate([third_ref[...], last_ref[...] + fix_ref[...]], axis=1)
    own_ref[:, 0:256] = mm3(left, inner_ref)
    own_ref[:, 256:512] = mm3(right, inner_ref[:, 0:256, :])


def place_inner(arrived, carry, first, last, inner):
    tile = pltpu.VMEM((TILE_ROWS, 128), f32)
    return pl.pallas_call(
        place_inner_kernel,
        out_shape=jax.ShapeDtypeStruct((TILE_ROWS, 512), f32),
        scratch_shapes=[pltpu.VMEM((256, 384), f32), tile, tile, tile],
        compiler_params=pltpu.CompilerParams(vmem_limit_bytes=32 << 20),
        cost_estimate=pl.CostEstimate(flops=800_000_000, bytes_accessed=3_000_000, transcendentals=0),
        name="place_inner",
    )(arrived, carry, first, last, inner)


def columns_kernel(own_ref, first_ref, to_right_ref, from_right_ref, from_left_ref, outer_ref, out_ref, up_ref, down_ref):
    lane = iota((TILE_ROWS, 128), 1)
    from_left = from_left_ref[...]
    spill = jnp.where(lane == 0, from_left, 0.0)
    right = from_right_ref[...] + jnp.where(lane == 0, to_right_ref[...], 0.0)
    mixed = jnp.where(lane < 8, first_ref[...] + spill, jnp.where(lane >= 112, from_left, 0.0))
    outer = mm3(jnp.concatenate([right, mixed], axis=1), outer_ref)
    pieces = [
        own_ref[:, 0:128] + taps_low[0] * spill,
        own_ref[:, 256:384] + outer[:, 256:384],
        outer[:, 0:128],
        own_ref[:, 128:256] + taps_high[0] * spill,
        own_ref[:, 384:512] + outer[:, 384:512],
        outer[:, 128:256],
    ]
    for at, piece in enumerate(pieces):
        cols = slice(at * 128, (at + 1) * 128)
        out_ref[:, cols] = piece
        up_ref[:, cols] = piece[0:UP_ROWS]
        down_ref[:, cols] = piece[DOWN_FROM : DOWN_FROM + DOWN_ROWS]


def outer_columns(own, first, to_right, from_right, from_left, outer):
    width = 2 * COL_ROOM[0]
    return pl.pallas_call(
        columns_kernel,
        out_shape=(
            jax.ShapeDtypeStruct((TILE_ROWS, width), f32),
            jax.ShapeDtypeStruct((UP_ROWS, width), f32),
            jax.ShapeDtypeStruct((DOWN_ROWS, width), f32),
        ),
        compiler_params=pltpu.CompilerParams(vmem_limit_bytes=32 << 20),
        cost_estimate=pl.CostEstimate(flops=220_000_000, bytes_accessed=2_000_000, transcendentals=0),
        name="columns",
    )(own, first, to_right, from_right, from_left, outer)


def own_rows_kernel(own_ref, table_ref, out_ref):
    for at in range(3):
        cols = slice(at * 256, (at + 1) * 256)
        out_ref[:, cols] = mm3_left(table_ref, own_ref[:, cols])


def own_rows(own, table):
    return pl.pallas_call(
        own_rows_kernel,
        out_shape=jax.ShapeDtypeStruct((2 * ROW_ROOM[0], 2 * COL_ROOM[0]), f32),
        compiler_params=pltpu.CompilerParams(vmem_limit_bytes=32 << 20),
        cost_estimate=pl.CostEstimate(flops=480_000_000, bytes_accessed=2_000_000, transcendentals=0),
        name="own_rows",
    )(own, table)


def levels_kernel(part_ref, below_ref, above_ref, near_ref, inner_ref, *refs):
    col_refs = (None,) + refs[0:3]
    row_refs = (None,) + refs[3:6]
    leader_refs = refs[6:10]
    approx_ref = refs[10]
    peak_ref = refs[11]
    near = mm3_left(near_ref, jnp.concatenate([below_ref[...], above_ref[...]], axis=0))
    pieces = []
    at, done = 0, 0
    for start, stop in HALO_ROWS:
        if start > done:
            pieces.append(part_ref[done:start, :])
        pieces.append(part_ref[start:stop, :] + near[at : at + stop - start])
        at += stop - start
        done = stop
    both = jnp.concatenate(pieces, axis=0)
    peak = None
    for level in range(4):
        room_r = ROW_ROOM[level]
        room_c = COL_ROOM[level]
        if level == 1:
            main = mm3(current, inner_ref)
            rest = mm3(jnp.concatenate([current[:, 256:384], current[:, 0:128]], axis=1), col_refs[1])
            parts = (main[:, 0:128], rest[:, 0:128], main[:, 128:256], rest[:, 128:256])
            both = mm3_left(row_refs[1], jnp.concatenate(parts, axis=1))
        elif level:
            both = mm3_left(row_refs[level], mm3(current, col_refs[level]))
        current = both[:room_r, :room_c]
        detail_a = both[:room_r, room_c:]
        detail_b = both[room_r:, :room_c]
        detail_c = both[room_r:, room_c:]
        now = jnp.maximum(jnp.maximum(jnp.abs(detail_a), jnp.abs(detail_b)), jnp.abs(detail_c))
        if peak is not None:
            now = jnp.maximum(now, peak)
        wide = jnp.maximum(now, jnp.maximum(pltpu.roll(now, 1, 1), pltpu.roll(now, room_c - 1, 1)))
        wide = jnp.maximum(wide, jnp.maximum(pltpu.roll(wide, 1, 0), pltpu.roll(wide, room_r - 1, 0)))
        n_r = R_DEV >> (level + 1)
        n_c = C_DEV >> (level + 1)
        leader_refs[level][...] = wide[:n_r, :n_c]
        if level < 3:
            pairs = jnp.maximum(now, pltpu.roll(now, room_c - 1, 1))
            pooled = []
            for across in range(room_c // 128):
                top = across * ROW_ROOM[0]
                peak_ref[top : top + room_r, :] = pairs[:, across * 128 : (across + 1) * 128]
                pooled.append(
                    jnp.maximum(
                        peak_ref[pl.ds(top, room_r // 2, stride=2), :],
                        peak_ref[pl.ds(top + 1, room_r // 2, stride=2), :],
                    )
                )
            high, low = hi_lo(jnp.concatenate(pooled, axis=1) if len(pooled) > 1 else pooled[0])
            room_n = COL_ROOM[level + 1]
            out = iota((room_c, room_n), 1)
            source = 2 * out + jnp.where(out < 3 * room_n // 4, 0, room_c - 2 * room_n)
            pick = (iota((room_c, room_n), 0) == source).astype(bf16)
            peak = mm(high, pick) + mm(low, pick)
    approx_ref[...] = current[: R_DEV >> 4, : C_DEV >> 4]


def all_levels(part, below, above, near, inner, cols, rows):
    shapes = [(R_DEV >> level, C_DEV >> level) for level in (1, 2, 3, 4, 4)]
    return pl.pallas_call(
        levels_kernel,
        out_shape=tuple(jax.ShapeDtypeStruct(shape, f32) for shape in shapes),
        scratch_shapes=[pltpu.VMEM((3 * ROW_ROOM[0], 128), f32)],
        compiler_params=pltpu.CompilerParams(vmem_limit_bytes=32 << 20),
        name="levels",
    )(part, below, above, near, inner, *cols, *rows)


def shifted(x, axis, by):
    size = lax.axis_size(axis)
    return lax.ppermute(x, axis, [(i, (i + by) % size) for i in range(size)])


def transform(arrived):
    table = jax.tree.map(jnp.asarray, tables())
    first, last, to_right, carry = place_edges(arrived)
    from_right = shifted(first, "cols", -1)
    from_left = shifted(to_right, "cols", 1)
    inner = place_inner(arrived, carry, first, last, table["inner"])
    own, to_up, to_down = outer_columns(inner, first, to_right, from_right, from_left, table["outer"])
    below = shifted(to_up, "rows", -1)
    above = shifted(to_down, "rows", 1)
    part = own_rows(own, table["own"])
    return all_levels(part, below, above, table["near"], table["inner"], table["cols"], table["rows"])


def on_device(offsets, lens_weight, counts, owners, brick_slot):
    packed = deposit_and_pack(offsets, lens_weight, counts, owners, brick_slot)
    arrived = lax.all_to_all(
        packed.reshape(N_DEST, MESSAGE // 4, 4, 128), ("rows", "cols"), split_axis=0, concat_axis=0, tiled=True
    )
    return transform(arrived.reshape(N_DEST * MESSAGE, 128))


def solution(mesh):
    placed = (
        P(("rows", "cols"), None, None),
        P(("rows", "cols"), None),
        P(("rows", "cols")),
        P(("rows", "cols")),
        P(("rows", "cols")),
    )
    return jax.shard_map(
        on_device,
        mesh=mesh,
        in_specs=placed,
        out_specs=(P("rows", "cols"),) * 5,
        check_vma=False,
    )
```

```python
import functools

import jax
import jax.numpy as jnp
import numpy as np
from jax import lax
from jax.experimental import pallas as pl
from jax.experimental.pallas import tpu as pltpu
from jax.sharding import PartitionSpec as P

R_DEV = 256
C_DEV = 512
PMAX = 256
CAP = 8
N_DEST = 128
BRICKS = 512
SLOTS = N_DEST * CAP

TILE_ROWS = 272
UP_ROWS = 80
DOWN_ROWS = 24
DOWN_FROM = 240
ROW_ROOM = (192, 96, 48, 24)
COL_ROOM = (384, 256, 128, 128)

taps_low = (
    0.33267055295008263,
    0.8068915093110925,
    0.4598775021184915,
    -0.13501102001025458,
    -0.08544127388202666,
    0.03522629188570953,
)
taps_high = tuple(((-1.0) ** index * taps_low[5 - index] for index in range(6)))

f32 = jnp.float32
bf16 = jnp.bfloat16


def spans(size):
    out = []
    for level in range(1, 5):
        n = size >> level
        before = 8 >> (level - 1)
        after = (36, 16, 6, 1)[level - 1]
        out.append((-before, n + after, -before, n + before))
    return out


def level_table(sources, room, span):
    low_from, low_to, high_from, high_to = span
    table = np.zeros((len(sources), 2 * room), np.float64)
    for position, index in enumerate(sources):
        if index is None:
            continue
        for half, (lo, hi, taps) in enumerate(
            ((low_from, low_to, taps_low), (high_from, high_to, taps_high))
        ):
            for tap in range(6):
                if (index - tap) % 2 == 0:
                    k = (index - tap) // 2
                    if lo <= k < hi:
                        table[position, half * room + (k % room)] += taps[tap]
    return table


def room_sources(room, low_from, low_to):
    out = [None] * room
    for k in range(low_from, low_to):
        out[k % room] = k
    return out


def split(table):
    table = np.asarray(table, np.float32)
    high = table.astype(jnp.bfloat16)
    low = (table - high.astype(np.float32)).astype(jnp.bfloat16)
    return np.stack([high, low])


ABOVE_ROWS = ((0, 8), (184, 192), (192, 200), (376, 384))
BELOW_ROWS = ((120, 136), (312, 328), (136, 168))
UP_MESSAGE = 6 * 16 + 6 * 16 + 3 * 32
LEFT_MESSAGE = TILE_ROWS // 2 + 40


@functools.lru_cache(maxsize=1)
def tables():
    col_spans = spans(C_DEV)
    row_spans = spans(R_DEV)
    inner = level_table(list(range(384)), 128, (0, 128, 0, 128))
    right = [C_DEV + j if j < 76 else None for j in range(128)] + [None] * 128
    mixed = [None] * 128 + list(range(8)) + [None] * 104 + [j - 16 for j in range(16)]
    room = COL_ROOM[0]
    beyond = level_table(right, room, (256, 292, 256, 264)) + level_table(mixed, room, (-8, 0, -8, 0))
    partial = level_table(right, room, (254, 256, 254, 256))
    outer = np.concatenate(
        [
            beyond[:, 256:384],
            beyond[:, room + 256 : room + 384],
            partial[:, 128:256],
            partial[:, room + 128 : room + 256],
        ],
        axis=1,
    )
    row_src = [i if i < 257 else None for i in range(TILE_ROWS)]
    row_src += [R_DEV + i if i < 76 else None for i in range(UP_ROWS)]
    row_src += [i - 16 if i < 17 else None for i in range(DOWN_ROWS)]
    third = [256 + j if j < 36 else j - 128 if j >= 120 else None for j in range(128)] + [None] * 128
    room = COL_ROOM[1]
    rest = level_table(third, room, col_spans[1])
    rest += level_table([None] * 128 + list(range(8)) + [None] * 120, room, (-4, 0, -4, 0))
    rest = np.concatenate([rest[:, 128:256], rest[:, room + 128 : room + 256]], axis=1)
    cols, rows = [rest], []
    for level in range(4):
        if level > 1:
            cols.append(level_table(col_src, COL_ROOM[level], col_spans[level]))
        rows.append(level_table(row_src, ROW_ROOM[level], row_spans[level]).T)
        col_src = room_sources(COL_ROOM[level], col_spans[level][0], col_spans[level][1])
        row_src = room_sources(ROW_ROOM[level], row_spans[level][0], row_spans[level][1])
    first = rows[0]
    below = first[:, TILE_ROWS : TILE_ROWS + UP_ROWS]
    above = first[:, TILE_ROWS + UP_ROWS :]
    for part, kept in ((below, BELOW_ROWS), (above, ABOVE_ROWS)):
        far = np.ones(first.shape[0], bool)
        for start, stop in kept:
            far[start:stop] = False
        assert not part[far].any()
    below = np.concatenate([below[start:stop] for start, stop in BELOW_ROWS], axis=0)
    above = np.concatenate([above[start:stop] for start, stop in ABOVE_ROWS], axis=0)
    return {
        "inner": split(inner),
        "outer": split(outer),
        "own": split(first[:, :TILE_ROWS]),
        "below": split(below),
        "above": split(above),
        "cols": [split(t) for t in cols],
        "rows": [split(t) for t in rows[1:]],
    }


def hi_lo(x):
    high = x.astype(bf16)
    low = (x - high.astype(f32)).astype(bf16)
    return high, low


def mm(a, b):
    return jnp.dot(a, b, preferred_element_type=f32)


def mm_nt(a, b):
    return lax.dot_general(a, b, (((1,), (1,)), ((), ())), preferred_element_type=f32)


def iota(shape, dim):
    return lax.broadcasted_iota(jnp.int32, shape, dim)


STEPS = 4
STEP_BRICKS = BRICKS // STEPS
MESSAGE = 20


def deposit_kernel(
    off_hbm,
    w_hbm,
    counts_hbm,
    owners_hbm,
    slot_hbm,
    out_ref,
    off_ref,
    w_ref,
    counts_ref,
    owners_ref,
    slot_ref,
    cnt_ref,
    patch_ref,
    edge_ref,
    small_sem,
    off_sem,
    w_sem,
):
    small = [
        pltpu.make_async_copy(src, dst, small_sem.at[n])
        for n, (src, dst) in enumerate(
            ((owners_hbm, owners_ref), (slot_hbm, slot_ref), (counts_hbm, counts_ref))
        )
    ]
    for copy in small:
        copy.start()

    def fetch(index):
        off_rows = pl.ds(index * 4 * STEP_BRICKS, 4 * STEP_BRICKS)
        w_rows = pl.ds(index * STEP_BRICKS, STEP_BRICKS)
        return (
            pltpu.make_async_copy(off_hbm.at[off_rows], off_ref.at[off_rows], off_sem.at[index]),
            pltpu.make_async_copy(w_hbm.at[w_rows], w_ref.at[w_rows], w_sem.at[index]),
        )

    for index in range(STEPS):
        for copy in fetch(index):
            copy.start()
    for copy in small:
        copy.wait()

    owners = owners_ref[...]
    dest = (iota((N_DEST, BRICKS), 0) == owners).astype(f32)
    before = (iota((BRICKS, BRICKS), 0) < iota((BRICKS, BRICKS), 1)).astype(bf16)
    ranks = jnp.sum(mm(dest.astype(bf16), before) * dest, axis=0, keepdims=True)
    position = ranks.astype(jnp.int32) * N_DEST + owners

    slot = slot_ref[...]
    grid_row = slot // 32
    grid_col = slot % 32
    coarse = (grid_col % 8) * 4 + grid_col // 8
    row_id = iota((256, BRICKS), 0)
    spread = jnp.where(
        row_id < 128,
        counts_ref[...],
        jnp.where(row_id == 168, coarse, jnp.where(row_id == 169, grid_row, 0)),
    )
    eye = (iota((BRICKS, BRICKS), 0) == iota((BRICKS, BRICKS), 1)).astype(bf16)
    cnt_ref[...] = mm_nt(eye, spread.astype(f32).astype(bf16))

    lane = iota((8, 128), 1)
    sub = iota((8, 128), 0)
    particle = iota((8, PMAX), 1).astype(f32)
    cell = iota((16, PMAX), 0).astype(f32)

    zero = jnp.zeros((), bf16)
    bit = {at: (lane >> at) % 2 == 1 for at in (3, 4, 5, 6)}

    def choose(tiles, mask):
        return [jnp.where(mask, odd, even) for even, odd in zip(tiles[0::2], tiles[1::2])]

    def one_group(start):
        first = start * 4
        rows_at = jnp.concatenate([off_ref[pl.ds(first + 2 * half, 8, stride=4), :] for half in range(2)], axis=1)
        cols_at = jnp.concatenate([off_ref[pl.ds(first + 2 * half + 1, 8, stride=4), :] for half in range(2)], axis=1)
        count = cnt_ref[pl.ds(start, 8), 0:128]
        count = jnp.concatenate([count, count], axis=1)
        weight = jnp.where(particle < count, w_ref[pl.ds(start, 8), :], 0.0)
        lag = rows_at * weight
        left = []
        for i in range(17):
            left.append(weight - jnp.abs(lag))
            lag = lag - weight
        left = jnp.maximum(jnp.concatenate(left, axis=0).astype(bf16), zero)
        right = []
        for g in range(8):
            at = first + 4 * ((8 - g) % 8) + 1
            column = jnp.concatenate([off_ref[pl.ds(at + 2 * half, 8, stride=0), :] for half in range(2)], axis=1)
            right += [1.0 - jnp.abs(column - cell[0:8]), 1.0 - jnp.abs(column - cell[8:16])]
        last = cols_at - 15.0
        right = [jnp.maximum(jnp.concatenate(right, axis=0).astype(bf16), zero)]
        right += [jnp.maximum(jnp.concatenate([last, last], axis=0).astype(bf16), zero)] * 8
        full = mm_nt(left, jnp.concatenate(right, axis=0))
        halves = []
        for half in range(2):
            pairs = []
            for pair in range(4):
                at = (half * 8 + pair * 2) * 8
                even = pltpu.roll(full[at : at + 8, 0:128], 0, 1, stride=16, stride_axis=0)
                odd = pltpu.roll(full[at + 8 : at + 16, 0:128], 16, 1, stride=16, stride_axis=0)
                both = jnp.where(bit[4], odd, even)
                pairs.append(pltpu.roll(both, 32 * pair, 1) if pair else both)
            halves.append(choose(choose(pairs, bit[5]), bit[6])[0])
        bottom = pltpu.roll(full[128:136, 0:128], 0, 1, stride=16, stride_axis=0)
        corner = jnp.sum(jnp.where(lane == sub, full[128:136, 128:256], 0.0), axis=1, keepdims=True)
        third = jnp.where(lane < 16, bottom, jnp.where(lane == 32, corner, 0.0))
        edge = [full[8 * i : 8 * i + 8, 128:256] for i in range(16)]
        for at in range(3, 7):
            edge = choose(edge, bit[at])
        edge = jnp.where(lane % 8 == sub, edge[0], 0.0)
        patch_ref[pl.ds(start, 8), 0:128] = halves[0]
        patch_ref[pl.ds(start, 8), 128:256] = halves[1]
        patch_ref[pl.ds(start, 8), 256:384] = third + cnt_ref[pl.ds(start, 8), 128:256]
        edge_ref[pl.ds(start, 8), :] = edge

    for index in range(STEPS):
        for copy in fetch(index):
            copy.wait()
    for group in range(BRICKS // 8):
        one_group(group * 8)

    gather = (iota((128, 128), 1) == iota((128, 128), 0) // 8 + 16).astype(bf16)
    edge_high, edge_low = hi_lo(edge_ref[...])
    third = patch_ref[:, 256:384] + (mm(edge_high, gather) + mm(edge_low, gather))

    high, low = hi_lo(patch_ref[:, 0:256])
    ends = jnp.concatenate(hi_lo(third), axis=1)
    lane_wide = iota((N_DEST, 128), 1)
    for pair in range(4):
        edges = []
        for rank in (2 * pair, 2 * pair + 1):
            pick = (iota((N_DEST, BRICKS), 0) + rank * N_DEST == position).astype(bf16)
            inner = mm(pick, high) + mm(pick, low)
            out_ref[pl.ds(rank, N_DEST, stride=MESSAGE), :] = inner[:, 0:128]
            out_ref[pl.ds(8 + rank, N_DEST, stride=MESSAGE), :] = inner[:, 128:256]
            both = mm(pick, ends)
            edges.append(both[:, 0:128] + both[:, 128:256])
        joined = jnp.where(lane_wide < 64, edges[0], pltpu.roll(edges[1], 64, 1))
        out_ref[pl.ds(16 + pair, N_DEST, stride=MESSAGE), :] = joined


def deposit_and_pack(offsets, weights, counts, owners, slots):
    flat = offsets.reshape(BRICKS, 2, 2, 128).transpose(0, 2, 1, 3).reshape(4 * BRICKS, 128)
    return pl.pallas_call(
        deposit_kernel,
        out_shape=jax.ShapeDtypeStruct((N_DEST * MESSAGE, 128), f32),
        in_specs=[pl.BlockSpec(memory_space=pltpu.MemorySpace.HBM)] * 5,
        scratch_shapes=[
            pltpu.VMEM((4 * BRICKS, 128), f32),
            pltpu.VMEM((BRICKS, PMAX), f32),
            pltpu.VMEM((1, BRICKS), jnp.int32),
            pltpu.VMEM((1, BRICKS), jnp.int32),
            pltpu.VMEM((1, BRICKS), jnp.int32),
            pltpu.VMEM((BRICKS, 256), f32),
            pltpu.VMEM((BRICKS, 384), f32),
            pltpu.VMEM((BRICKS, 128), f32),
            pltpu.SemaphoreType.DMA((3,)),
            pltpu.SemaphoreType.DMA((STEPS,)),
            pltpu.SemaphoreType.DMA((STEPS,)),
        ],
        compiler_params=pltpu.CompilerParams(vmem_limit_bytes=40 << 20),
        name="deposit",
    )(*(pltpu.with_memory_space_constraint(x, pltpu.MemorySpace.HBM) for x in (
        flat,
        weights,
        counts.reshape(1, BRICKS),
        owners.reshape(1, BRICKS),
        slots.reshape(1, BRICKS),
    )))


def mm3(data, table):
    high, low = hi_lo(data)
    return mm(high, table[0]) + (mm(low, table[0]) + mm(high, table[1]))


def mm3_left(table, data):
    high, low = hi_lo(data)
    return mm(table[0], high) + (mm(table[0], low) + mm(table[1], high))


def place(x_ref, grid_ref, blocks):
    lane8 = iota((8, 128), 1)
    upper = jnp.concatenate([x_ref[pl.ds(rank, N_DEST, stride=MESSAGE), :] for rank in range(8)], axis=0)
    lower = jnp.concatenate([x_ref[pl.ds(8 + rank, N_DEST, stride=MESSAGE), :] for rank in range(8)], axis=0)
    ends = []
    for pair in range(4):
        joined = x_ref[pl.ds(16 + pair, N_DEST, stride=MESSAGE), :]
        ends += [joined, pltpu.roll(joined, 64, 1)]
    ends_high, ends_low = hi_lo(jnp.concatenate(ends, axis=0))
    weigh = jnp.where(lane8 == 40, 16.0, jnp.where(lane8 == 41, 1.0, 0.0)).astype(bf16)
    slot = mm_nt(weigh, ends_high)[0:1, :].astype(jnp.int32)
    high, low = hi_lo(jnp.concatenate([upper, lower], axis=1))
    ends = jnp.concatenate([ends_high, ends_low], axis=1)
    row = iota((128, SLOTS), 0)
    for at, block in enumerate(blocks):
        rows = slice(at * 128, (at + 1) * 128)
        pick = ((row // 16) * 64 + row % 16 + block * 16 == slot).astype(bf16)
        grid_ref[rows, 0:256] = mm(pick, high) + mm(pick, low)
        both = mm(pick, ends)
        grid_ref[rows, 256:384] = both[:, 0:128] + both[:, 128:256]


def swap_groups(tiles):
    group = iota((8, 128), 1) // 16
    for d in (1, 2, 4):
        mask = (group // d) % 2 == 0
        new = list(tiles)
        for a in range(8):
            if (a // d) % 2 == 0:
                one, two = tiles[a], tiles[a + d]
                new[a] = jnp.where(mask, one, pltpu.roll(two, 16 * d, 1))
                new[a + d] = jnp.where(mask, pltpu.roll(one, 128 - 16 * d, 1), two)
        tiles = new
    return tiles


def turn(side, corner):
    turned = [[pltpu.roll(side[half], 16 - i, 1) for half in range(2)] for i in range(16)]
    return turned + [[pltpu.roll(corner[half], 16, 1) for half in range(2)]]


def unpack_block(grid_ref, at):
    rows = [[None, None] for _ in range(17)]
    side, corner = [None, None], [None, None]
    for half in range(2):
        parts = []
        for third in range(3):
            parts.append(
                swap_groups(
                    [
                        grid_ref[at * 128 + col * 16 + half * 8 : at * 128 + col * 16 + half * 8 + 8, third * 128 : (third + 1) * 128]
                        for col in range(8)
                    ]
                )
            )
        for i in range(8):
            rows[i][half] = parts[0][i]
            rows[8 + i][half] = parts[1][i]
        rows[16][half] = parts[2][0]
        side[half] = parts[2][1]
        corner[half] = parts[2][2]
    return rows, side, corner


def add_spills(rows, turned, previous):
    lane8 = iota((8, 128), 1)
    out = []
    for i in range(17):
        pair = []
        for half in range(2):
            spill = jnp.where(lane8 % 16 == 0, turned[i][half], 0.0)
            first = 0.0 if previous is None else previous[i][half]
            pair.append(rows[i][half] + jnp.where(lane8 == 0, first, spill))
        out.append(pair)
    return out


def store_block(rows, ref):
    sub = iota((8, 128), 0)
    down = [pltpu.roll(rows[16][half], 1, 0) for half in range(2)]
    for i in range(16):
        low, high = rows[i]
        if i == 0:
            low = low + jnp.where(sub == 0, 0.0, down[0])
            high = high + jnp.where(sub == 0, down[0], down[1])
        ref[pl.ds(i, 8, stride=16), :] = low
        ref[pl.ds(128 + i, 8, stride=16), :] = high
    ref[256:264, :] = jnp.where(sub == 0, down[1], 0.0)
    ref[264:TILE_ROWS, :] = jnp.zeros((8, 128), f32)


def place_edges_kernel(x_ref, first_ref, last_ref, left_ref, right_ref, carry_ref, grid_ref, side_ref):
    place(x_ref, grid_ref, (0, 3))
    lane8 = iota((8, 128), 1)
    rows, side, corner = unpack_block(grid_ref, 0)
    store_block(add_spills(rows, turn(side, corner), None), first_ref)
    for half in range(2):
        carry_ref[half * 8 : half * 8 + 8, :] = side[half]
        carry_ref[16 + half * 8 : 24 + half * 8, :] = corner[half]
    rows, side, corner = unpack_block(grid_ref, 1)
    turned = turn(side, corner)
    rows = add_spills(rows, turned, None)
    store_block(rows, last_ref)
    store_block(
        [[jnp.where(lane8 == 0, turned[i][half], rows[i][half]) for half in range(2)] for i in range(17)], side_ref
    )
    right = [jnp.zeros((8, 128), f32)] * 5
    left = [jnp.zeros((8, 128), f32)] * 5
    for tile in range(33):
        group, at = divmod(tile, 5)
        rows8 = slice(tile * 8, tile * 8 + 8)
        both = side_ref[rows8, :]
        moved = jnp.where(lane8 == 112 + group, pltpu.roll(both, 112 + group, 1), right[at])
        right[at] = jnp.where(lane8 // 16 == group, pltpu.roll(both, 16 * group + 16, 1), moved)
        turned64 = pltpu.roll(first_ref[rows8, :], (64 + 16 * group) % 128, 1) if group != 4 else first_ref[rows8, :]
        left[at] = jnp.where(lane8 // 16 == group, turned64, left[at])
    for at in range(5):
        right_ref[at * 8 : at * 8 + 8, :] = right[at]
        left_ref[136 + at * 8 : 144 + at * 8, :] = left[at]
    lane = iota((136, 128), 1)
    left_ref[0:136, :] = jnp.where(lane < 64, first_ref[0:136, :], pltpu.roll(first_ref[136:272, :], 64, 1))


def place_edges(arrived):
    tile = jax.ShapeDtypeStruct((TILE_ROWS, 128), f32)
    return pl.pallas_call(
        place_edges_kernel,
        out_shape=(
            tile,
            tile,
            jax.ShapeDtypeStruct((LEFT_MESSAGE, 128), f32),
            jax.ShapeDtypeStruct((40, 128), f32),
            jax.ShapeDtypeStruct((32, 128), f32),
        ),
        scratch_shapes=[pltpu.VMEM((256, 384), f32), pltpu.VMEM((TILE_ROWS, 128), f32)],
        compiler_params=pltpu.CompilerParams(vmem_limit_bytes=32 << 20),
        cost_estimate=pl.CostEstimate(flops=600_000_000, bytes_accessed=2_000_000, transcendentals=0),
        name="place_edges",
    )(arrived)


def place_inner_kernel(x_ref, carry_ref, first_ref, last_ref, inner_ref, own_ref, grid_ref, second_ref, third_ref, fix_ref):
    place(x_ref, grid_ref, (1, 2))
    lane8 = iota((8, 128), 1)
    previous = turn(
        [carry_ref[half * 8 : half * 8 + 8, :] for half in range(2)],
        [carry_ref[16 + half * 8 : 24 + half * 8, :] for half in range(2)],
    )
    for at, ref in enumerate((second_ref, third_ref)):
        rows, side, corner = unpack_block(grid_ref, at)
        turned = turn(side, corner)
        store_block(add_spills(rows, turned, previous), ref)
        previous = turned
    store_block([[jnp.where(lane8 == 0, previous[i][half], 0.0) for half in range(2)] for i in range(17)], fix_ref)
    left = jnp.concatenate([first_ref[...], second_ref[...], third_ref[...]], axis=1)
    right = jnp.concatenate([third_ref[...], last_ref[...] + fix_ref[...]], axis=1)
    own_ref[:, 0:256] = mm3(left, inner_ref)
    own_ref[:, 256:512] = mm3(right, inner_ref[:, 0:256, :])


def place_inner(arrived, carry, first, last, inner):
    tile = pltpu.VMEM((TILE_ROWS, 128), f32)
    return pl.pallas_call(
        place_inner_kernel,
        out_shape=jax.ShapeDtypeStruct((TILE_ROWS, 512), f32),
        scratch_shapes=[pltpu.VMEM((256, 384), f32), tile, tile, tile],
        compiler_params=pltpu.CompilerParams(vmem_limit_bytes=32 << 20),
        cost_estimate=pl.CostEstimate(flops=800_000_000, bytes_accessed=3_000_000, transcendentals=0),
        name="place_inner",
    )(arrived, carry, first, last, inner)


def columns_kernel(
    own_ref, first_ref, to_right_ref, from_right_ref, from_left_ref, outer_ref, below_ref, out_ref, up_ref, down_ref
):
    lane8 = iota((8, 128), 1)
    none = jnp.zeros((8, 128), f32)
    spills, rows = [], []
    for tile in range(TILE_ROWS // 8):
        group, at = divmod(tile, 5)
        own = first_ref[tile * 8 : tile * 8 + 8, :]
        if tile == 33:
            spills.append(none)
            rows.append(jnp.concatenate([none, jnp.where(lane8 < 8, own, 0.0)], axis=1))
            continue
        packed = from_left_ref[at * 8 : at * 8 + 8, :]
        spill = jnp.where(lane8 == 0, pltpu.roll(packed, 16 - group, 1), 0.0)
        near = pltpu.roll(packed, 112 - 16 * group, 1)
        spills.append(spill)
        mixed = jnp.where(lane8 < 8, own + spill, jnp.where(lane8 >= 112, near, 0.0))
        wide = from_right_ref[(tile % 17) * 8 : (tile % 17) * 8 + 8, :]
        if tile >= 17:
            wide = pltpu.roll(wide, 64, 1)
        rest = from_right_ref[136 + at * 8 : 144 + at * 8, :]
        if group != 4:
            rest = pltpu.roll(rest, (64 - 16 * group) % 128, 1)
        over = jnp.where(lane8 == 0, pltpu.roll(to_right_ref[at * 8 : at * 8 + 8, :], 16 - group, 1), 0.0)
        right = jnp.where(lane8 < 64, wide, jnp.where(lane8 < 80, rest, 0.0)) + over
        rows.append(jnp.concatenate([right, mixed], axis=1))
    spill = jnp.concatenate(spills, axis=0)
    outer = mm3(jnp.concatenate(rows, axis=0), outer_ref)
    pieces = [
        own_ref[:, 0:128] + taps_low[0] * spill,
        own_ref[:, 256:384] + outer[:, 256:384],
        outer[:, 0:128],
        own_ref[:, 128:256] + taps_high[0] * spill,
        own_ref[:, 384:512] + outer[:, 384:512],
        outer[:, 128:256],
    ]
    low = mm3_left(below_ref, jnp.concatenate([piece[0:UP_ROWS] for piece in pieces[0:3]], axis=1))
    high = mm3_left(below_ref[:, 0:32, :], jnp.concatenate([piece[0:UP_ROWS] for piece in pieces[3:6]], axis=1))
    for at in range(3):
        cols = slice(at * 128, (at + 1) * 128)
        for part in range(2):
            rows16 = slice(part * 16, part * 16 + 16)
            up_ref[part * 96 + at * 16 : part * 96 + at * 16 + 16, :] = low[rows16, cols]
            up_ref[part * 96 + 48 + at * 16 : part * 96 + 64 + at * 16, :] = high[rows16, cols]
        up_ref[192 + at * 32 : 224 + at * 32, :] = low[32:64, cols]
    for at, piece in enumerate(pieces):
        cols = slice(at * 128, (at + 1) * 128)
        out_ref[:, cols] = piece
        down_ref[:, cols] = piece[DOWN_FROM : DOWN_FROM + DOWN_ROWS]


def outer_columns(own, first, to_right, from_right, from_left, outer, below):
    width = 2 * COL_ROOM[0]
    return pl.pallas_call(
        columns_kernel,
        out_shape=(
            jax.ShapeDtypeStruct((TILE_ROWS, width), f32),
            jax.ShapeDtypeStruct((UP_MESSAGE, 128), f32),
            jax.ShapeDtypeStruct((DOWN_ROWS, width), f32),
        ),
        compiler_params=pltpu.CompilerParams(vmem_limit_bytes=32 << 20),
        cost_estimate=pl.CostEstimate(flops=220_000_000, bytes_accessed=2_000_000, transcendentals=0),
        name="columns",
    )(own, first, to_right, from_right, from_left, outer, below)


def own_rows_kernel(own_ref, table_ref, out_ref):
    for at in range(3):
        cols = slice(at * 256, (at + 1) * 256)
        out_ref[:, cols] = mm3_left(table_ref, own_ref[:, cols])


def own_rows(own, table):
    return pl.pallas_call(
        own_rows_kernel,
        out_shape=jax.ShapeDtypeStruct((2 * ROW_ROOM[0], 2 * COL_ROOM[0]), f32),
        compiler_params=pltpu.CompilerParams(vmem_limit_bytes=32 << 20),
        cost_estimate=pl.CostEstimate(flops=480_000_000, bytes_accessed=2_000_000, transcendentals=0),
        name="own_rows",
    )(own, table)


def levels_kernel(part_ref, below_ref, above_ref, table_ref, inner_ref, *refs):
    col_refs = (None,) + refs[0:3]
    row_refs = (None,) + refs[3:6]
    leader_refs = refs[6:10]
    approx_ref = refs[10]
    peak_ref = refs[11]
    near = mm3_left(table_ref, above_ref[...])
    half = COL_ROOM[0]
    sixes = [
        jnp.concatenate([below_ref[part * 96 + at * 16 : part * 96 + at * 16 + 16, :] for at in range(6)], axis=1)
        for part in range(2)
    ]
    threes = jnp.concatenate([below_ref[192 + at * 32 : 224 + at * 32, :] for at in range(3)], axis=1)
    threes = jnp.concatenate([threes, jnp.zeros((32, half), f32)], axis=1)
    added = {0: near[0:8], 184: near[8:16], 192: near[16:24], 376: near[24:32]}
    added.update({120: sixes[0], 136: threes, 312: sixes[1]})
    cuts = sorted({0, 8, 120, 136, 168, 184, 192, 200, 312, 328, 376, 384})
    both = jnp.concatenate(
        [
            part_ref[start:stop, :] + added[start] if start in added else part_ref[start:stop, :]
            for start, stop in zip(cuts, cuts[1:])
        ],
        axis=0,
    )
    peak = None
    for level in range(4):
        room_r = ROW_ROOM[level]
        room_c = COL_ROOM[level]
        if level == 1:
            main = mm3(current, inner_ref)
            rest = mm3(jnp.concatenate([current[:, 256:384], current[:, 0:128]], axis=1), col_refs[1])
            parts = (main[:, 0:128], rest[:, 0:128], main[:, 128:256], rest[:, 128:256])
            both = mm3_left(row_refs[1], jnp.concatenate(parts, axis=1))
        elif level:
            both = mm3_left(row_refs[level], mm3(current, col_refs[level]))
        current = both[:room_r, :room_c]
        detail_a = both[:room_r, room_c:]
        detail_b = both[room_r:, :room_c]
        detail_c = both[room_r:, room_c:]
        now = jnp.maximum(jnp.maximum(jnp.abs(detail_a), jnp.abs(detail_b)), jnp.abs(detail_c))
        if peak is not None:
            now = jnp.maximum(now, peak)
        wide = jnp.maximum(now, jnp.maximum(pltpu.roll(now, 1, 1), pltpu.roll(now, room_c - 1, 1)))
        wide = jnp.maximum(wide, jnp.maximum(pltpu.roll(wide, 1, 0), pltpu.roll(wide, room_r - 1, 0)))
        n_r = R_DEV >> (level + 1)
        n_c = C_DEV >> (level + 1)
        leader_refs[level][...] = wide[:n_r, :n_c]
        if level < 3:
            pairs = jnp.maximum(now, pltpu.roll(now, room_c - 1, 1))
            pooled = []
            for across in range(room_c // 128):
                top = across * ROW_ROOM[0]
                peak_ref[top : top + room_r, :] = pairs[:, across * 128 : (across + 1) * 128]
                pooled.append(
                    jnp.maximum(
                        peak_ref[pl.ds(top, room_r // 2, stride=2), :],
                        peak_ref[pl.ds(top + 1, room_r // 2, stride=2), :],
                    )
                )
            high, low = hi_lo(jnp.concatenate(pooled, axis=1) if len(pooled) > 1 else pooled[0])
            room_n = COL_ROOM[level + 1]
            out = iota((room_c, room_n), 1)
            source = 2 * out + jnp.where(out < 3 * room_n // 4, 0, room_c - 2 * room_n)
            pick = (iota((room_c, room_n), 0) == source).astype(bf16)
            peak = mm(high, pick) + mm(low, pick)
    approx_ref[...] = current[: R_DEV >> 4, : C_DEV >> 4]


def all_levels(part, below, above, near, inner, cols, rows):
    shapes = [(R_DEV >> level, C_DEV >> level) for level in (1, 2, 3, 4, 4)]
    return pl.pallas_call(
        levels_kernel,
        out_shape=tuple(jax.ShapeDtypeStruct(shape, f32) for shape in shapes),
        scratch_shapes=[pltpu.VMEM((3 * ROW_ROOM[0], 128), f32)],
        compiler_params=pltpu.CompilerParams(vmem_limit_bytes=32 << 20),
        name="levels",
    )(part, below, above, near, inner, *cols, *rows)


def shifted(x, axis, by):
    size = lax.axis_size(axis)
    return lax.ppermute(x, axis, [(i, (i + by) % size) for i in range(size)])


def transform(arrived):
    table = jax.tree.map(jnp.asarray, tables())
    first, last, to_left, to_right, carry = place_edges(arrived)
    from_right = shifted(to_left, "cols", -1)
    from_left = shifted(to_right, "cols", 1)
    inner = place_inner(arrived, carry, first, last, table["inner"])
    own, to_up, to_down = outer_columns(
        inner, first, to_right, from_right, from_left, table["outer"], table["below"]
    )
    below = shifted(to_up, "rows", -1)
    above = shifted(to_down, "rows", 1)
    part = own_rows(own, table["own"])
    return all_levels(part, below, above, table["above"], table["inner"], table["cols"], table["rows"])


def on_device(offsets, lens_weight, counts, owners, brick_slot):
    packed = deposit_and_pack(offsets, lens_weight, counts, owners, brick_slot)
    arrived = lax.all_to_all(
        packed.reshape(N_DEST, MESSAGE // 4, 4, 128), ("rows", "cols"), split_axis=0, concat_axis=0, tiled=True
    )
    return transform(arrived.reshape(N_DEST * MESSAGE, 128))


def solution(mesh):
    placed = (
        P(("rows", "cols"), None, None),
        P(("rows", "cols"), None),
        P(("rows", "cols")),
        P(("rows", "cols")),
        P(("rows", "cols")),
    )
    return jax.shard_map(
        on_device,
        mesh=mesh,
        in_specs=placed,
        out_specs=(P("rows", "cols"),) * 5,
        check_vma=False,
    )
```

```python
import functools

import jax
import jax.numpy as jnp
import numpy as np
from jax import lax
from jax.experimental import pallas as pl
from jax.experimental.pallas import tpu as pltpu
from jax.sharding import PartitionSpec as P

R_DEV = 256
C_DEV = 512
PMAX = 256
CAP = 8
N_DEST = 128
BRICKS = 512
SLOTS = N_DEST * CAP

TILE_ROWS = 272
UP_ROWS = 80
DOWN_ROWS = 24
DOWN_FROM = 240
ROW_ROOM = (192, 96, 48, 24)
COL_ROOM = (384, 256, 128, 128)

taps_low = (
    0.33267055295008263,
    0.8068915093110925,
    0.4598775021184915,
    -0.13501102001025458,
    -0.08544127388202666,
    0.03522629188570953,
)
taps_high = tuple(((-1.0) ** index * taps_low[5 - index] for index in range(6)))

f32 = jnp.float32
bf16 = jnp.bfloat16


def spans(size):
    out = []
    for level in range(1, 5):
        n = size >> level
        before = 8 >> (level - 1)
        after = (36, 16, 6, 1)[level - 1]
        out.append((-before, n + after, -before, n + before))
    return out


def level_table(sources, room, span):
    low_from, low_to, high_from, high_to = span
    table = np.zeros((len(sources), 2 * room), np.float64)
    for position, index in enumerate(sources):
        if index is None:
            continue
        for half, (lo, hi, taps) in enumerate(
            ((low_from, low_to, taps_low), (high_from, high_to, taps_high))
        ):
            for tap in range(6):
                if (index - tap) % 2 == 0:
                    k = (index - tap) // 2
                    if lo <= k < hi:
                        table[position, half * room + (k % room)] += taps[tap]
    return table


def room_sources(room, low_from, low_to):
    out = [None] * room
    for k in range(low_from, low_to):
        out[k % room] = k
    return out


def split(table):
    table = np.asarray(table, np.float32)
    high = table.astype(jnp.bfloat16)
    low = (table - high.astype(np.float32)).astype(jnp.bfloat16)
    return np.stack([high, low])


ABOVE_ROWS = ((0, 8), (184, 192), (192, 200), (376, 384))
BELOW_ROWS = ((120, 136), (312, 328), (136, 168))
UP_MESSAGE = 5 * 16 + 5 * 16 + 3 * 32
DOWN_MESSAGE = 5 * 16 + 8
LEFT_MESSAGE = TILE_ROWS // 2 + 40


@functools.lru_cache(maxsize=1)
def tables():
    col_spans = spans(C_DEV)
    row_spans = spans(R_DEV)
    inner = level_table(list(range(384)), 128, (0, 128, 0, 128))
    right = [C_DEV + j if j < 76 else None for j in range(128)] + [None] * 128
    mixed = [None] * 128 + list(range(8)) + [None] * 104 + [j - 16 for j in range(16)]
    room = COL_ROOM[0]
    beyond = level_table(right, room, (256, 292, 256, 264)) + level_table(mixed, room, (-8, 0, -8, 0))
    partial = level_table(right, room, (254, 256, 254, 256))
    outer = np.concatenate(
        [
            beyond[:, 256:384],
            beyond[:, room + 256 : room + 384],
            partial[:, 128:256],
            partial[:, room + 128 : room + 256],
        ],
        axis=1,
    )
    row_src = [i if i < 257 else None for i in range(TILE_ROWS)]
    row_src += [R_DEV + i if i < 76 else None for i in range(UP_ROWS)]
    row_src += [i - 16 if i < 17 else None for i in range(DOWN_ROWS)]
    third = [256 + j if j < 36 else j - 128 if j >= 120 else None for j in range(128)] + [None] * 128
    room = COL_ROOM[1]
    rest = level_table(third, room, col_spans[1])
    rest += level_table([None] * 128 + list(range(8)) + [None] * 120, room, (-4, 0, -4, 0))
    rest = np.concatenate([rest[:, 128:256], rest[:, room + 128 : room + 256]], axis=1)
    cols, rows = [rest], []
    for level in range(4):
        if level > 1:
            cols.append(level_table(col_src, COL_ROOM[level], col_spans[level]))
        rows.append(level_table(row_src, ROW_ROOM[level], row_spans[level]).T)
        col_src = room_sources(COL_ROOM[level], col_spans[level][0], col_spans[level][1])
        row_src = room_sources(ROW_ROOM[level], row_spans[level][0], row_spans[level][1])
    first = rows[0]
    below = first[:, TILE_ROWS : TILE_ROWS + UP_ROWS]
    above = first[:, TILE_ROWS + UP_ROWS :]
    for part, kept in ((below, BELOW_ROWS), (above, ABOVE_ROWS)):
        far = np.ones(first.shape[0], bool)
        for start, stop in kept:
            far[start:stop] = False
        assert not part[far].any()
    below = np.concatenate([below[start:stop] for start, stop in BELOW_ROWS], axis=0)
    above = np.concatenate([above[start:stop] for start, stop in ABOVE_ROWS], axis=0)
    return {
        "inner": split(inner),
        "outer": split(outer),
        "own": split(first[:, :TILE_ROWS]),
        "below": split(below),
        "above": split(above),
        "cols": [split(t) for t in cols],
        "rows": [split(t) for t in rows[1:]],
    }


def hi_lo(x):
    high = x.astype(bf16)
    low = (x - high.astype(f32)).astype(bf16)
    return high, low


def mm(a, b):
    return jnp.dot(a, b, preferred_element_type=f32)


def mm_nt(a, b):
    return lax.dot_general(a, b, (((1,), (1,)), ((), ())), preferred_element_type=f32)


def iota(shape, dim):
    return lax.broadcasted_iota(jnp.int32, shape, dim)


STEPS = 4
STEP_BRICKS = BRICKS // STEPS
MESSAGE = 20


def deposit_kernel(
    off_hbm,
    w_hbm,
    counts_hbm,
    owners_hbm,
    slot_hbm,
    out_ref,
    off_ref,
    w_ref,
    counts_ref,
    owners_ref,
    slot_ref,
    cnt_ref,
    patch_ref,
    edge_ref,
    small_sem,
    off_sem,
    w_sem,
):
    small = [
        pltpu.make_async_copy(src, dst, small_sem.at[n])
        for n, (src, dst) in enumerate(
            ((owners_hbm, owners_ref), (slot_hbm, slot_ref), (counts_hbm, counts_ref))
        )
    ]
    for copy in small:
        copy.start()

    def fetch(index):
        off_rows = pl.ds(index * 4 * STEP_BRICKS, 4 * STEP_BRICKS)
        w_rows = pl.ds(index * STEP_BRICKS, STEP_BRICKS)
        return (
            pltpu.make_async_copy(off_hbm.at[off_rows], off_ref.at[off_rows], off_sem.at[index]),
            pltpu.make_async_copy(w_hbm.at[w_rows], w_ref.at[w_rows], w_sem.at[index]),
        )

    for index in range(STEPS):
        for copy in fetch(index):
            copy.start()
    for copy in small:
        copy.wait()

    owners = owners_ref[...]
    dest = (iota((N_DEST, BRICKS), 0) == owners).astype(f32)
    before = (iota((BRICKS, BRICKS), 0) < iota((BRICKS, BRICKS), 1)).astype(bf16)
    ranks = jnp.sum(mm(dest.astype(bf16), before) * dest, axis=0, keepdims=True)
    position = ranks.astype(jnp.int32) * N_DEST + owners

    slot = slot_ref[...]
    grid_row = slot // 32
    grid_col = slot % 32
    coarse = (grid_col % 8) * 4 + grid_col // 8
    row_id = iota((256, BRICKS), 0)
    spread = jnp.where(
        row_id < 128,
        counts_ref[...],
        jnp.where(row_id == 168, coarse, jnp.where(row_id == 169, grid_row, 0)),
    )
    eye = (iota((BRICKS, BRICKS), 0) == iota((BRICKS, BRICKS), 1)).astype(bf16)
    cnt_ref[...] = mm_nt(eye, spread.astype(f32).astype(bf16))

    lane = iota((8, 128), 1)
    sub = iota((8, 128), 0)
    particle = iota((8, PMAX), 1).astype(f32)
    cell = iota((16, PMAX), 0).astype(f32)

    zero = jnp.zeros((), bf16)
    bit = {at: (lane >> at) % 2 == 1 for at in (3, 4, 5, 6)}

    def choose(tiles, mask):
        return [jnp.where(mask, odd, even) for even, odd in zip(tiles[0::2], tiles[1::2])]

    def one_group(start):
        first = start * 4
        rows_at = jnp.concatenate([off_ref[pl.ds(first + 2 * half, 8, stride=4), :] for half in range(2)], axis=1)
        cols_at = jnp.concatenate([off_ref[pl.ds(first + 2 * half + 1, 8, stride=4), :] for half in range(2)], axis=1)
        count = cnt_ref[pl.ds(start, 8), 0:128]
        count = jnp.concatenate([count, count], axis=1)
        weight = jnp.where(particle < count, w_ref[pl.ds(start, 8), :], 0.0)
        lag = rows_at * weight
        left = []
        for i in range(17):
            left.append(weight - jnp.abs(lag))
            lag = lag - weight
        left = jnp.maximum(jnp.concatenate(left, axis=0).astype(bf16), zero)
        right = []
        for g in range(8):
            at = first + 4 * ((8 - g) % 8) + 1
            column = jnp.concatenate([off_ref[pl.ds(at + 2 * half, 8, stride=0), :] for half in range(2)], axis=1)
            right += [1.0 - jnp.abs(column - cell[0:8]), 1.0 - jnp.abs(column - cell[8:16])]
        last = cols_at - 15.0
        right = [jnp.maximum(jnp.concatenate(right, axis=0).astype(bf16), zero)]
        right += [jnp.maximum(jnp.concatenate([last, last], axis=0).astype(bf16), zero)] * 8
        full = mm_nt(left, jnp.concatenate(right, axis=0))
        halves = []
        for half in range(2):
            pairs = []
            for pair in range(4):
                at = (half * 8 + pair * 2) * 8
                even = pltpu.roll(full[at : at + 8, 0:128], 0, 1, stride=16, stride_axis=0)
                odd = pltpu.roll(full[at + 8 : at + 16, 0:128], 16, 1, stride=16, stride_axis=0)
                both = jnp.where(bit[4], odd, even)
                pairs.append(pltpu.roll(both, 32 * pair, 1) if pair else both)
            halves.append(choose(choose(pairs, bit[5]), bit[6])[0])
        bottom = pltpu.roll(full[128:136, 0:128], 0, 1, stride=16, stride_axis=0)
        corner = jnp.sum(jnp.where(lane == sub, full[128:136, 128:256], 0.0), axis=1, keepdims=True)
        third = jnp.where(lane < 16, bottom, jnp.where(lane == 32, corner, 0.0))
        edge = [full[8 * i : 8 * i + 8, 128:256] for i in range(16)]
        for at in range(3, 7):
            edge = choose(edge, bit[at])
        edge = jnp.where(lane % 8 == sub, edge[0], 0.0)
        patch_ref[pl.ds(start, 8), 0:128] = halves[0]
        patch_ref[pl.ds(start, 8), 128:256] = halves[1]
        patch_ref[pl.ds(start, 8), 256:384] = third + cnt_ref[pl.ds(start, 8), 128:256]
        edge_ref[pl.ds(start, 8), :] = edge

    for index in range(STEPS):
        for copy in fetch(index):
            copy.wait()
    for group in range(BRICKS // 8):
        one_group(group * 8)

    gather = (iota((128, 128), 1) == iota((128, 128), 0) // 8 + 16).astype(bf16)
    edge_high, edge_low = hi_lo(edge_ref[...])
    third = patch_ref[:, 256:384] + (mm(edge_high, gather) + mm(edge_low, gather))

    high, low = hi_lo(patch_ref[:, 0:256])
    ends = jnp.concatenate(hi_lo(third), axis=1)
    lane_wide = iota((N_DEST, 128), 1)
    for pair in range(4):
        edges = []
        for rank in (2 * pair, 2 * pair + 1):
            pick = (iota((N_DEST, BRICKS), 0) + rank * N_DEST == position).astype(bf16)
            inner = mm(pick, high) + mm(pick, low)
            out_ref[pl.ds(rank, N_DEST, stride=MESSAGE), :] = inner[:, 0:128]
            out_ref[pl.ds(8 + rank, N_DEST, stride=MESSAGE), :] = inner[:, 128:256]
            both = mm(pick, ends)
            edges.append(both[:, 0:128] + both[:, 128:256])
        joined = jnp.where(lane_wide < 64, edges[0], pltpu.roll(edges[1], 64, 1))
        out_ref[pl.ds(16 + pair, N_DEST, stride=MESSAGE), :] = joined


def deposit_and_pack(offsets, weights, counts, owners, slots):
    flat = offsets.reshape(BRICKS, 2, 2, 128).transpose(0, 2, 1, 3).reshape(4 * BRICKS, 128)
    return pl.pallas_call(
        deposit_kernel,
        out_shape=jax.ShapeDtypeStruct((N_DEST * MESSAGE, 128), f32),
        in_specs=[pl.BlockSpec(memory_space=pltpu.MemorySpace.HBM)] * 5,
        scratch_shapes=[
            pltpu.VMEM((4 * BRICKS, 128), f32),
            pltpu.VMEM((BRICKS, PMAX), f32),
            pltpu.VMEM((1, BRICKS), jnp.int32),
            pltpu.VMEM((1, BRICKS), jnp.int32),
            pltpu.VMEM((1, BRICKS), jnp.int32),
            pltpu.VMEM((BRICKS, 256), f32),
            pltpu.VMEM((BRICKS, 384), f32),
            pltpu.VMEM((BRICKS, 128), f32),
            pltpu.SemaphoreType.DMA((3,)),
            pltpu.SemaphoreType.DMA((STEPS,)),
            pltpu.SemaphoreType.DMA((STEPS,)),
        ],
        compiler_params=pltpu.CompilerParams(vmem_limit_bytes=40 << 20),
        name="deposit",
    )(*(pltpu.with_memory_space_constraint(x, pltpu.MemorySpace.HBM) for x in (
        flat,
        weights,
        counts.reshape(1, BRICKS),
        owners.reshape(1, BRICKS),
        slots.reshape(1, BRICKS),
    )))


def mm3(data, table):
    high, low = hi_lo(data)
    return mm(high, table[0]) + (mm(low, table[0]) + mm(high, table[1]))


def mm3_left(table, data):
    high, low = hi_lo(data)
    return mm(table[0], high) + (mm(table[0], low) + mm(table[1], high))


def place(x_ref, grid_ref, blocks):
    lane8 = iota((8, 128), 1)
    upper = jnp.concatenate([x_ref[pl.ds(rank, N_DEST, stride=MESSAGE), :] for rank in range(8)], axis=0)
    lower = jnp.concatenate([x_ref[pl.ds(8 + rank, N_DEST, stride=MESSAGE), :] for rank in range(8)], axis=0)
    ends = []
    for pair in range(4):
        joined = x_ref[pl.ds(16 + pair, N_DEST, stride=MESSAGE), :]
        ends += [joined, pltpu.roll(joined, 64, 1)]
    ends_high, ends_low = hi_lo(jnp.concatenate(ends, axis=0))
    weigh = jnp.where(lane8 == 40, 16.0, jnp.where(lane8 == 41, 1.0, 0.0)).astype(bf16)
    slot = mm_nt(weigh, ends_high)[0:1, :].astype(jnp.int32)
    high, low = hi_lo(jnp.concatenate([upper, lower], axis=1))
    ends = jnp.concatenate([ends_high, ends_low], axis=1)
    row = iota((128, SLOTS), 0)
    for at, block in enumerate(blocks):
        rows = slice(at * 128, (at + 1) * 128)
        pick = ((row // 16) * 64 + row % 16 + block * 16 == slot).astype(bf16)
        grid_ref[rows, 0:256] = mm(pick, high) + mm(pick, low)
        both = mm(pick, ends)
        grid_ref[rows, 256:384] = both[:, 0:128] + both[:, 128:256]


def swap_groups(tiles):
    group = iota((8, 128), 1) // 16
    for d in (1, 2, 4):
        mask = (group // d) % 2 == 0
        new = list(tiles)
        for a in range(8):
            if (a // d) % 2 == 0:
                one, two = tiles[a], tiles[a + d]
                new[a] = jnp.where(mask, one, pltpu.roll(two, 16 * d, 1))
                new[a + d] = jnp.where(mask, pltpu.roll(one, 128 - 16 * d, 1), two)
        tiles = new
    return tiles


def turn(side, corner):
    turned = [[pltpu.roll(side[half], 16 - i, 1) for half in range(2)] for i in range(16)]
    return turned + [[pltpu.roll(corner[half], 16, 1) for half in range(2)]]


def unpack_block(grid_ref, at):
    rows = [[None, None] for _ in range(17)]
    side, corner = [None, None], [None, None]
    for half in range(2):
        parts = []
        for third in range(3):
            parts.append(
                swap_groups(
                    [
                        grid_ref[at * 128 + col * 16 + half * 8 : at * 128 + col * 16 + half * 8 + 8, third * 128 : (third + 1) * 128]
                        for col in range(8)
                    ]
                )
            )
        for i in range(8):
            rows[i][half] = parts[0][i]
            rows[8 + i][half] = parts[1][i]
        rows[16][half] = parts[2][0]
        side[half] = parts[2][1]
        corner[half] = parts[2][2]
    return rows, side, corner


def add_spills(rows, turned, previous):
    lane8 = iota((8, 128), 1)
    out = []
    for i in range(17):
        pair = []
        for half in range(2):
            spill = jnp.where(lane8 % 16 == 0, turned[i][half], 0.0)
            first = 0.0 if previous is None else previous[i][half]
            pair.append(rows[i][half] + jnp.where(lane8 == 0, first, spill))
        out.append(pair)
    return out


def store_block(rows, ref):
    sub = iota((8, 128), 0)
    down = [pltpu.roll(rows[16][half], 1, 0) for half in range(2)]
    for i in range(16):
        low, high = rows[i]
        if i == 0:
            low = low + jnp.where(sub == 0, 0.0, down[0])
            high = high + jnp.where(sub == 0, down[0], down[1])
        ref[pl.ds(i, 8, stride=16), :] = low
        ref[pl.ds(128 + i, 8, stride=16), :] = high
    ref[256:264, :] = jnp.where(sub == 0, down[1], 0.0)
    ref[264:TILE_ROWS, :] = jnp.zeros((8, 128), f32)


def place_edges_kernel(x_ref, first_ref, last_ref, left_ref, right_ref, carry_ref, grid_ref, side_ref):
    place(x_ref, grid_ref, (0, 3))
    lane8 = iota((8, 128), 1)
    rows, side, corner = unpack_block(grid_ref, 0)
    store_block(add_spills(rows, turn(side, corner), None), first_ref)
    for half in range(2):
        carry_ref[half * 8 : half * 8 + 8, :] = side[half]
        carry_ref[16 + half * 8 : 24 + half * 8, :] = corner[half]
    rows, side, corner = unpack_block(grid_ref, 1)
    turned = turn(side, corner)
    rows = add_spills(rows, turned, None)
    store_block(rows, last_ref)
    store_block(
        [[jnp.where(lane8 == 0, turned[i][half], rows[i][half]) for half in range(2)] for i in range(17)], side_ref
    )
    right = [jnp.zeros((8, 128), f32)] * 5
    left = [jnp.zeros((8, 128), f32)] * 5
    for tile in range(33):
        group, at = divmod(tile, 5)
        rows8 = slice(tile * 8, tile * 8 + 8)
        both = side_ref[rows8, :]
        moved = jnp.where(lane8 == 112 + group, pltpu.roll(both, 112 + group, 1), right[at])
        right[at] = jnp.where(lane8 // 16 == group, pltpu.roll(both, 16 * group + 16, 1), moved)
        turned64 = pltpu.roll(first_ref[rows8, :], (64 + 16 * group) % 128, 1) if group != 4 else first_ref[rows8, :]
        left[at] = jnp.where(lane8 // 16 == group, turned64, left[at])
    for at in range(5):
        right_ref[at * 8 : at * 8 + 8, :] = right[at]
        left_ref[136 + at * 8 : 144 + at * 8, :] = left[at]
    lane = iota((136, 128), 1)
    left_ref[0:136, :] = jnp.where(lane < 64, first_ref[0:136, :], pltpu.roll(first_ref[136:272, :], 64, 1))


def place_edges(arrived):
    tile = jax.ShapeDtypeStruct((TILE_ROWS, 128), f32)
    return pl.pallas_call(
        place_edges_kernel,
        out_shape=(
            tile,
            tile,
            jax.ShapeDtypeStruct((LEFT_MESSAGE, 128), f32),
            jax.ShapeDtypeStruct((40, 128), f32),
            jax.ShapeDtypeStruct((32, 128), f32),
        ),
        scratch_shapes=[pltpu.VMEM((256, 384), f32), pltpu.VMEM((TILE_ROWS, 128), f32)],
        compiler_params=pltpu.CompilerParams(vmem_limit_bytes=32 << 20),
        cost_estimate=pl.CostEstimate(flops=600_000_000, bytes_accessed=2_000_000, transcendentals=0),
        name="place_edges",
    )(arrived)


def place_inner_kernel(x_ref, carry_ref, first_ref, last_ref, inner_ref, own_ref, grid_ref, second_ref, third_ref, fix_ref):
    place(x_ref, grid_ref, (1, 2))
    lane8 = iota((8, 128), 1)
    previous = turn(
        [carry_ref[half * 8 : half * 8 + 8, :] for half in range(2)],
        [carry_ref[16 + half * 8 : 24 + half * 8, :] for half in range(2)],
    )
    for at, ref in enumerate((second_ref, third_ref)):
        rows, side, corner = unpack_block(grid_ref, at)
        turned = turn(side, corner)
        store_block(add_spills(rows, turned, previous), ref)
        previous = turned
    store_block([[jnp.where(lane8 == 0, previous[i][half], 0.0) for half in range(2)] for i in range(17)], fix_ref)
    left = jnp.concatenate([first_ref[...], second_ref[...], third_ref[...]], axis=1)
    right = jnp.concatenate([third_ref[...], last_ref[...] + fix_ref[...]], axis=1)
    own_ref[:, 0:256] = mm3(left, inner_ref)
    own_ref[:, 256:512] = mm3(right, inner_ref[:, 0:256, :])


def place_inner(arrived, carry, first, last, inner):
    tile = pltpu.VMEM((TILE_ROWS, 128), f32)
    return pl.pallas_call(
        place_inner_kernel,
        out_shape=jax.ShapeDtypeStruct((TILE_ROWS, 512), f32),
        scratch_shapes=[pltpu.VMEM((256, 384), f32), tile, tile, tile],
        compiler_params=pltpu.CompilerParams(vmem_limit_bytes=32 << 20),
        cost_estimate=pl.CostEstimate(flops=800_000_000, bytes_accessed=3_000_000, transcendentals=0),
        name="place_inner",
    )(arrived, carry, first, last, inner)


def pack_tiles(tiles):
    lane = iota(tiles[0].shape, 1)
    shared = jnp.where((lane >= 56) & (lane < 72), pltpu.roll(tiles[5], 64, 1), tiles[2])
    return [tiles[0], tiles[1], shared, tiles[3], tiles[4]]


def unpack_tiles(tiles):
    return jnp.concatenate([*tiles, pltpu.roll(tiles[2], 64, 1)], axis=1)


def columns_kernel(
    own_ref, first_ref, to_right_ref, from_right_ref, from_left_ref, outer_ref, below_ref, out_ref, up_ref, down_ref
):
    lane8 = iota((8, 128), 1)
    none = jnp.zeros((8, 128), f32)
    spills, rows = [], []
    for tile in range(TILE_ROWS // 8):
        group, at = divmod(tile, 5)
        own = first_ref[tile * 8 : tile * 8 + 8, :]
        if tile == 33:
            spills.append(none)
            rows.append(jnp.concatenate([none, jnp.where(lane8 < 8, own, 0.0)], axis=1))
            continue
        packed = from_left_ref[at * 8 : at * 8 + 8, :]
        spill = jnp.where(lane8 == 0, pltpu.roll(packed, 16 - group, 1), 0.0)
        near = pltpu.roll(packed, 112 - 16 * group, 1)
        spills.append(spill)
        mixed = jnp.where(lane8 < 8, own + spill, jnp.where(lane8 >= 112, near, 0.0))
        wide = from_right_ref[(tile % 17) * 8 : (tile % 17) * 8 + 8, :]
        if tile >= 17:
            wide = pltpu.roll(wide, 64, 1)
        rest = from_right_ref[136 + at * 8 : 144 + at * 8, :]
        if group != 4:
            rest = pltpu.roll(rest, (64 - 16 * group) % 128, 1)
        over = jnp.where(lane8 == 0, pltpu.roll(to_right_ref[at * 8 : at * 8 + 8, :], 16 - group, 1), 0.0)
        right = jnp.where(lane8 < 64, wide, jnp.where(lane8 < 80, rest, 0.0)) + over
        rows.append(jnp.concatenate([right, mixed], axis=1))
    spill = jnp.concatenate(spills, axis=0)
    outer = mm3(jnp.concatenate(rows, axis=0), outer_ref)
    pieces = [
        own_ref[:, 0:128] + taps_low[0] * spill,
        own_ref[:, 256:384] + outer[:, 256:384],
        outer[:, 0:128],
        own_ref[:, 128:256] + taps_high[0] * spill,
        own_ref[:, 384:512] + outer[:, 384:512],
        outer[:, 128:256],
    ]
    low = mm3_left(below_ref, jnp.concatenate([piece[0:UP_ROWS] for piece in pieces[0:3]], axis=1))
    high = mm3_left(below_ref[:, 0:32, :], jnp.concatenate([piece[0:UP_ROWS] for piece in pieces[3:6]], axis=1))
    for part in range(2):
        rows16 = slice(part * 16, part * 16 + 16)
        fives = pack_tiles([half[rows16, at * 128 : (at + 1) * 128] for half in (low, high) for at in range(3)])
        for at, tile in enumerate(fives):
            up_ref[part * 80 + at * 16 : part * 80 + at * 16 + 16, :] = tile
    for at in range(3):
        up_ref[160 + at * 32 : 192 + at * 32, :] = low[32:64, at * 128 : (at + 1) * 128]
    for at, tile in enumerate(pack_tiles([piece[DOWN_FROM : DOWN_FROM + 24] for piece in pieces])):
        down_ref[at * 16 : at * 16 + 16, :] = tile[0:16]
        down_ref[80 + at : 81 + at, :] = tile[16:17]
    down_ref[85:88, :] = jnp.zeros((3, 128), f32)
    for at, piece in enumerate(pieces):
        out_ref[:, at * 128 : (at + 1) * 128] = piece


def outer_columns(own, first, to_right, from_right, from_left, outer, below):
    width = 2 * COL_ROOM[0]
    return pl.pallas_call(
        columns_kernel,
        out_shape=(
            jax.ShapeDtypeStruct((TILE_ROWS, width), f32),
            jax.ShapeDtypeStruct((UP_MESSAGE, 128), f32),
            jax.ShapeDtypeStruct((DOWN_MESSAGE, 128), f32),
        ),
        compiler_params=pltpu.CompilerParams(vmem_limit_bytes=32 << 20),
        cost_estimate=pl.CostEstimate(flops=220_000_000, bytes_accessed=2_000_000, transcendentals=0),
        name="columns",
    )(own, first, to_right, from_right, from_left, outer, below)


def own_rows_kernel(own_ref, table_ref, out_ref):
    for at in range(3):
        cols = slice(at * 256, (at + 1) * 256)
        out_ref[:, cols] = mm3_left(table_ref, own_ref[:, cols])


def own_rows(own, table):
    return pl.pallas_call(
        own_rows_kernel,
        out_shape=jax.ShapeDtypeStruct((2 * ROW_ROOM[0], 2 * COL_ROOM[0]), f32),
        compiler_params=pltpu.CompilerParams(vmem_limit_bytes=32 << 20),
        cost_estimate=pl.CostEstimate(flops=480_000_000, bytes_accessed=2_000_000, transcendentals=0),
        name="own_rows",
    )(own, table)


def levels_kernel(part_ref, below_ref, above_ref, table_ref, inner_ref, *refs):
    col_refs = (None,) + refs[0:3]
    row_refs = (None,) + refs[3:6]
    leader_refs = refs[6:10]
    approx_ref = refs[10]
    peak_ref = refs[11]
    sub = iota((8, 128), 0)
    above = [
        jnp.concatenate(
            [
                above_ref[at * 16 : at * 16 + 16, :],
                jnp.where(sub == 0, above_ref[80 + at : 81 + at, :], 0.0),
            ],
            axis=0,
        )
        for at in range(5)
    ]
    near = mm3_left(table_ref, unpack_tiles(above))
    half = COL_ROOM[0]
    sixes = [
        unpack_tiles([below_ref[part * 80 + at * 16 : part * 80 + at * 16 + 16, :] for at in range(5)])
        for part in range(2)
    ]
    threes = jnp.concatenate([below_ref[160 + at * 32 : 192 + at * 32, :] for at in range(3)], axis=1)
    threes = jnp.concatenate([threes, jnp.zeros((32, half), f32)], axis=1)
    added = {0: near[0:8], 184: near[8:16], 192: near[16:24], 376: near[24:32]}
    added.update({120: sixes[0], 136: threes, 312: sixes[1]})
    cuts = sorted({0, 8, 120, 136, 168, 184, 192, 200, 312, 328, 376, 384})
    both = jnp.concatenate(
        [
            part_ref[start:stop, :] + added[start] if start in added else part_ref[start:stop, :]
            for start, stop in zip(cuts, cuts[1:])
        ],
        axis=0,
    )
    peak = None
    for level in range(4):
        room_r = ROW_ROOM[level]
        room_c = COL_ROOM[level]
        if level == 1:
            main = mm3(current, inner_ref)
            rest = mm3(jnp.concatenate([current[:, 256:384], current[:, 0:128]], axis=1), col_refs[1])
            parts = (main[:, 0:128], rest[:, 0:128], main[:, 128:256], rest[:, 128:256])
            both = mm3_left(row_refs[1], jnp.concatenate(parts, axis=1))
        elif level:
            both = mm3_left(row_refs[level], mm3(current, col_refs[level]))
        current = both[:room_r, :room_c]
        detail_a = both[:room_r, room_c:]
        detail_b = both[room_r:, :room_c]
        detail_c = both[room_r:, room_c:]
        now = jnp.maximum(jnp.maximum(jnp.abs(detail_a), jnp.abs(detail_b)), jnp.abs(detail_c))
        if peak is not None:
            now = jnp.maximum(now, peak)
        wide = jnp.maximum(now, jnp.maximum(pltpu.roll(now, 1, 1), pltpu.roll(now, room_c - 1, 1)))
        wide = jnp.maximum(wide, jnp.maximum(pltpu.roll(wide, 1, 0), pltpu.roll(wide, room_r - 1, 0)))
        n_r = R_DEV >> (level + 1)
        n_c = C_DEV >> (level + 1)
        leader_refs[level][...] = wide[:n_r, :n_c]
        if level < 3:
            pairs = jnp.maximum(now, pltpu.roll(now, room_c - 1, 1))
            pooled = []
            for across in range(room_c // 128):
                top = across * ROW_ROOM[0]
                peak_ref[top : top + room_r, :] = pairs[:, across * 128 : (across + 1) * 128]
                pooled.append(
                    jnp.maximum(
                        peak_ref[pl.ds(top, room_r // 2, stride=2), :],
                        peak_ref[pl.ds(top + 1, room_r // 2, stride=2), :],
                    )
                )
            high, low = hi_lo(jnp.concatenate(pooled, axis=1) if len(pooled) > 1 else pooled[0])
            room_n = COL_ROOM[level + 1]
            out = iota((room_c, room_n), 1)
            source = 2 * out + jnp.where(out < 3 * room_n // 4, 0, room_c - 2 * room_n)
            pick = (iota((room_c, room_n), 0) == source).astype(bf16)
            peak = mm(high, pick) + mm(low, pick)
    approx_ref[...] = current[: R_DEV >> 4, : C_DEV >> 4]


def all_levels(part, below, above, near, inner, cols, rows):
    shapes = [(R_DEV >> level, C_DEV >> level) for level in (1, 2, 3, 4, 4)]
    return pl.pallas_call(
        levels_kernel,
        out_shape=tuple(jax.ShapeDtypeStruct(shape, f32) for shape in shapes),
        scratch_shapes=[pltpu.VMEM((3 * ROW_ROOM[0], 128), f32)],
        compiler_params=pltpu.CompilerParams(vmem_limit_bytes=32 << 20),
        name="levels",
    )(part, below, above, near, inner, *cols, *rows)


def shifted(x, axis, by):
    size = lax.axis_size(axis)
    return lax.ppermute(x, axis, [(i, (i + by) % size) for i in range(size)])


def transform(arrived):
    table = jax.tree.map(jnp.asarray, tables())
    first, last, to_left, to_right, carry = place_edges(arrived)
    from_right = shifted(to_left, "cols", -1)
    from_left = shifted(to_right, "cols", 1)
    inner = place_inner(arrived, carry, first, last, table["inner"])
    own, to_up, to_down = outer_columns(
        inner, first, to_right, from_right, from_left, table["outer"], table["below"]
    )
    above = shifted(to_down, "rows", 1)
    below = shifted(to_up, "rows", -1)
    part = own_rows(own, table["own"])
    return all_levels(part, below, above, table["above"], table["inner"], table["cols"], table["rows"])


def on_device(offsets, lens_weight, counts, owners, brick_slot):
    packed = deposit_and_pack(offsets, lens_weight, counts, owners, brick_slot)
    arrived = lax.all_to_all(
        packed.reshape(N_DEST, MESSAGE // 4, 4, 128), ("rows", "cols"), split_axis=0, concat_axis=0, tiled=True
    )
    return transform(arrived.reshape(N_DEST * MESSAGE, 128))


def solution(mesh):
    placed = (
        P(("rows", "cols"), None, None),
        P(("rows", "cols"), None),
        P(("rows", "cols")),
        P(("rows", "cols")),
        P(("rows", "cols")),
    )
    return jax.shard_map(
        on_device,
        mesh=mesh,
        in_specs=placed,
        out_specs=(P("rows", "cols"),) * 5,
        check_vma=False,
    )
```

```python
import functools

import jax
import jax.numpy as jnp
import numpy as np
from jax import lax
from jax.experimental import pallas as pl
from jax.experimental.pallas import tpu as pltpu
from jax.sharding import PartitionSpec as P

R_DEV = 256
C_DEV = 512
PMAX = 256
CAP = 8
N_DEST = 128
BRICKS = 512
SLOTS = N_DEST * CAP

TILE_ROWS = 272
UP_ROWS = 80
DOWN_ROWS = 24
DOWN_FROM = 240
ROW_ROOM = (192, 96, 48, 24)
COL_ROOM = (384, 256, 128, 128)

taps_low = (
    0.33267055295008263,
    0.8068915093110925,
    0.4598775021184915,
    -0.13501102001025458,
    -0.08544127388202666,
    0.03522629188570953,
)
taps_high = tuple(((-1.0) ** index * taps_low[5 - index] for index in range(6)))

f32 = jnp.float32
bf16 = jnp.bfloat16


def spans(size):
    out = []
    for level in range(1, 5):
        n = size >> level
        before = 8 >> (level - 1)
        after = (36, 16, 6, 1)[level - 1]
        out.append((-before, n + after, -before, n + before))
    return out


def level_table(sources, room, span):
    low_from, low_to, high_from, high_to = span
    table = np.zeros((len(sources), 2 * room), np.float64)
    for position, index in enumerate(sources):
        if index is None:
            continue
        for half, (lo, hi, taps) in enumerate(
            ((low_from, low_to, taps_low), (high_from, high_to, taps_high))
        ):
            for tap in range(6):
                if (index - tap) % 2 == 0:
                    k = (index - tap) // 2
                    if lo <= k < hi:
                        table[position, half * room + (k % room)] += taps[tap]
    return table


def room_sources(room, low_from, low_to):
    out = [None] * room
    for k in range(low_from, low_to):
        out[k % room] = k
    return out


def split(table):
    table = np.asarray(table, np.float32)
    high = table.astype(jnp.bfloat16)
    low = (table - high.astype(np.float32)).astype(jnp.bfloat16)
    return np.stack([high, low])


ABOVE_ROWS = ((0, 8), (184, 192), (192, 200), (376, 384))
BELOW_ROWS = ((120, 136), (312, 328), (136, 168))
UP_MESSAGE = 5 * 16 + 5 * 16 + 3 * 32
DOWN_MESSAGE = 5 * 16 + 8
LEFT_MESSAGE = TILE_ROWS // 2 + 40


@functools.lru_cache(maxsize=1)
def tables():
    col_spans = spans(C_DEV)
    row_spans = spans(R_DEV)
    inner = level_table(list(range(384)), 128, (0, 128, 0, 128))
    right = [C_DEV + j if j < 76 else None for j in range(128)] + [None] * 128
    mixed = [None] * 128 + list(range(8)) + [None] * 104 + [j - 16 for j in range(16)]
    room = COL_ROOM[0]
    beyond = level_table(right, room, (256, 292, 256, 264)) + level_table(mixed, room, (-8, 0, -8, 0))
    partial = level_table(right, room, (254, 256, 254, 256))
    outer = np.concatenate(
        [
            beyond[:, 256:384],
            beyond[:, room + 256 : room + 384],
            partial[:, 128:256],
            partial[:, room + 128 : room + 256],
        ],
        axis=1,
    )
    row_src = [i if i < 257 else None for i in range(TILE_ROWS)]
    row_src += [R_DEV + i if i < 76 else None for i in range(UP_ROWS)]
    row_src += [i - 16 if i < 17 else None for i in range(DOWN_ROWS)]
    third = [256 + j if j < 36 else j - 128 if j >= 120 else None for j in range(128)] + [None] * 128
    room = COL_ROOM[1]
    rest = level_table(third, room, col_spans[1])
    rest += level_table([None] * 128 + list(range(8)) + [None] * 120, room, (-4, 0, -4, 0))
    rest = np.concatenate([rest[:, 128:256], rest[:, room + 128 : room + 256]], axis=1)
    cols, rows = [rest], []
    for level in range(4):
        if level > 1:
            cols.append(level_table(col_src, COL_ROOM[level], col_spans[level]))
        rows.append(level_table(row_src, ROW_ROOM[level], row_spans[level]).T)
        col_src = room_sources(COL_ROOM[level], col_spans[level][0], col_spans[level][1])
        row_src = room_sources(ROW_ROOM[level], row_spans[level][0], row_spans[level][1])
    first = rows[0]
    below = first[:, TILE_ROWS : TILE_ROWS + UP_ROWS]
    above = first[:, TILE_ROWS + UP_ROWS :]
    for part, kept in ((below, BELOW_ROWS), (above, ABOVE_ROWS)):
        far = np.ones(first.shape[0], bool)
        for start, stop in kept:
            far[start:stop] = False
        assert not part[far].any()
    below = np.concatenate([below[start:stop] for start, stop in BELOW_ROWS], axis=0)
    above = np.concatenate([above[start:stop] for start, stop in ABOVE_ROWS], axis=0)
    return {
        "inner": split(inner),
        "outer": split(outer),
        "own": split(first[:, :TILE_ROWS]),
        "below": split(below),
        "above": split(above),
        "cols": [split(t) for t in cols],
        "rows": [split(t) for t in rows[1:]],
    }


def hi_lo(x):
    high = x.astype(bf16)
    low = (x - high.astype(f32)).astype(bf16)
    return high, low


def mm(a, b):
    return jnp.dot(a, b, preferred_element_type=f32)


def mm_nt(a, b):
    return lax.dot_general(a, b, (((1,), (1,)), ((), ())), preferred_element_type=f32)


def iota(shape, dim):
    return lax.broadcasted_iota(jnp.int32, shape, dim)


STEPS = 4
STEP_BRICKS = BRICKS // STEPS
MESSAGE = 20


def deposit_kernel(
    off_hbm,
    w_hbm,
    counts_hbm,
    owners_hbm,
    slot_hbm,
    out_ref,
    off_ref,
    w_ref,
    counts_ref,
    owners_ref,
    slot_ref,
    cnt_ref,
    patch_ref,
    edge_ref,
    small_sem,
    off_sem,
    w_sem,
):
    small = [
        pltpu.make_async_copy(src, dst, small_sem.at[n])
        for n, (src, dst) in enumerate(
            ((owners_hbm, owners_ref), (slot_hbm, slot_ref), (counts_hbm, counts_ref))
        )
    ]
    for copy in small:
        copy.start()

    def fetch(index):
        off_rows = pl.ds(index * 4 * STEP_BRICKS, 4 * STEP_BRICKS)
        w_rows = pl.ds(index * STEP_BRICKS, STEP_BRICKS)
        return (
            pltpu.make_async_copy(off_hbm.at[off_rows], off_ref.at[off_rows], off_sem.at[index]),
            pltpu.make_async_copy(w_hbm.at[w_rows], w_ref.at[w_rows], w_sem.at[index]),
        )

    for index in range(STEPS):
        for copy in fetch(index):
            copy.start()
    for copy in small:
        copy.wait()

    owners = owners_ref[...]
    dest = (iota((N_DEST, BRICKS), 0) == owners).astype(f32)
    before = (iota((BRICKS, BRICKS), 0) < iota((BRICKS, BRICKS), 1)).astype(bf16)
    ranks = jnp.sum(mm(dest.astype(bf16), before) * dest, axis=0, keepdims=True)
    position = ranks.astype(jnp.int32) * N_DEST + owners

    slot = slot_ref[...]
    grid_row = slot // 32
    grid_col = slot % 32
    coarse = (grid_col % 8) * 4 + grid_col // 8
    row_id = iota((256, BRICKS), 0)
    spread = jnp.where(
        row_id < 128,
        counts_ref[...],
        jnp.where(row_id == 168, coarse, jnp.where(row_id == 169, grid_row, 0)),
    )
    eye = (iota((BRICKS, BRICKS), 0) == iota((BRICKS, BRICKS), 1)).astype(bf16)
    cnt_ref[...] = mm_nt(eye, spread.astype(f32).astype(bf16))

    lane = iota((8, 128), 1)
    sub = iota((8, 128), 0)
    particle = iota((8, PMAX), 1).astype(f32)
    cell = iota((16, PMAX), 0).astype(f32)

    zero = jnp.zeros((), bf16)
    bit = {at: (lane >> at) % 2 == 1 for at in (3, 4, 5, 6)}

    def choose(tiles, mask):
        return [jnp.where(mask, odd, even) for even, odd in zip(tiles[0::2], tiles[1::2])]

    def one_group(start):
        first = start * 4
        rows_at = jnp.concatenate([off_ref[pl.ds(first + 2 * half, 8, stride=4), :] for half in range(2)], axis=1)
        cols_at = jnp.concatenate([off_ref[pl.ds(first + 2 * half + 1, 8, stride=4), :] for half in range(2)], axis=1)
        count = cnt_ref[pl.ds(start, 8), 0:128]
        count = jnp.concatenate([count, count], axis=1)
        weight = jnp.where(particle < count, w_ref[pl.ds(start, 8), :], 0.0)
        lag = rows_at * weight
        left = []
        for i in range(17):
            left.append(weight - jnp.abs(lag))
            lag = lag - weight
        left = jnp.maximum(jnp.concatenate(left, axis=0).astype(bf16), zero)
        right = []
        for g in range(8):
            at = first + 4 * ((8 - g) % 8) + 1
            column = jnp.concatenate([off_ref[pl.ds(at + 2 * half, 8, stride=0), :] for half in range(2)], axis=1)
            right += [1.0 - jnp.abs(column - cell[0:8]), 1.0 - jnp.abs(column - cell[8:16])]
        last = cols_at - 15.0
        right = [jnp.maximum(jnp.concatenate(right, axis=0).astype(bf16), zero)]
        right += [jnp.maximum(jnp.concatenate([last, last], axis=0).astype(bf16), zero)] * 8
        full = mm_nt(left, jnp.concatenate(right, axis=0))
        halves = []
        for half in range(2):
            pairs = []
            for pair in range(4):
                at = (half * 8 + pair * 2) * 8
                even = pltpu.roll(full[at : at + 8, 0:128], 0, 1, stride=16, stride_axis=0)
                odd = pltpu.roll(full[at + 8 : at + 16, 0:128], 16, 1, stride=16, stride_axis=0)
                both = jnp.where(bit[4], odd, even)
                pairs.append(pltpu.roll(both, 32 * pair, 1) if pair else both)
            halves.append(choose(choose(pairs, bit[5]), bit[6])[0])
        bottom = pltpu.roll(full[128:136, 0:128], 0, 1, stride=16, stride_axis=0)
        corner = jnp.sum(jnp.where(lane == sub, full[128:136, 128:256], 0.0), axis=1, keepdims=True)
        third = jnp.where(lane < 16, bottom, jnp.where(lane == 32, corner, 0.0))
        edge = [full[8 * i : 8 * i + 8, 128:256] for i in range(16)]
        for at in range(3, 7):
            edge = choose(edge, bit[at])
        edge = jnp.where(lane % 8 == sub, edge[0], 0.0)
        patch_ref[pl.ds(start, 8), 0:128] = halves[0]
        patch_ref[pl.ds(start, 8), 128:256] = halves[1]
        patch_ref[pl.ds(start, 8), 256:384] = third + cnt_ref[pl.ds(start, 8), 128:256]
        edge_ref[pl.ds(start, 8), :] = edge

    for index in range(STEPS):
        for copy in fetch(index):
            copy.wait()
    for group in range(BRICKS // 8):
        one_group(group * 8)

    gather = (iota((128, 128), 1) == iota((128, 128), 0) // 8 + 16).astype(bf16)
    edge_high, edge_low = hi_lo(edge_ref[...])
    third = patch_ref[:, 256:384] + (mm(edge_high, gather) + mm(edge_low, gather))

    high, low = hi_lo(patch_ref[:, 0:256])
    ends = jnp.concatenate(hi_lo(third), axis=1)
    lane_wide = iota((N_DEST, 128), 1)
    for pair in range(4):
        edges = []
        for rank in (2 * pair, 2 * pair + 1):
            pick = (iota((N_DEST, BRICKS), 0) + rank * N_DEST == position).astype(bf16)
            inner = mm(pick, high) + mm(pick, low)
            out_ref[pl.ds(rank, N_DEST, stride=MESSAGE), :] = inner[:, 0:128]
            out_ref[pl.ds(8 + rank, N_DEST, stride=MESSAGE), :] = inner[:, 128:256]
            both = mm(pick, ends)
            edges.append(both[:, 0:128] + both[:, 128:256])
        joined = jnp.where(lane_wide < 64, edges[0], pltpu.roll(edges[1], 64, 1))
        out_ref[pl.ds(16 + pair, N_DEST, stride=MESSAGE), :] = joined


def deposit_and_pack(offsets, weights, counts, owners, slots):
    flat = offsets.reshape(BRICKS, 2, 2, 128).transpose(0, 2, 1, 3).reshape(4 * BRICKS, 128)
    return pl.pallas_call(
        deposit_kernel,
        out_shape=jax.ShapeDtypeStruct((N_DEST * MESSAGE, 128), f32),
        in_specs=[pl.BlockSpec(memory_space=pltpu.MemorySpace.HBM)] * 5,
        scratch_shapes=[
            pltpu.VMEM((4 * BRICKS, 128), f32),
            pltpu.VMEM((BRICKS, PMAX), f32),
            pltpu.VMEM((1, BRICKS), jnp.int32),
            pltpu.VMEM((1, BRICKS), jnp.int32),
            pltpu.VMEM((1, BRICKS), jnp.int32),
            pltpu.VMEM((BRICKS, 256), f32),
            pltpu.VMEM((BRICKS, 384), f32),
            pltpu.VMEM((BRICKS, 128), f32),
            pltpu.SemaphoreType.DMA((3,)),
            pltpu.SemaphoreType.DMA((STEPS,)),
            pltpu.SemaphoreType.DMA((STEPS,)),
        ],
        compiler_params=pltpu.CompilerParams(vmem_limit_bytes=40 << 20),
        name="deposit",
    )(*(pltpu.with_memory_space_constraint(x, pltpu.MemorySpace.HBM) for x in (
        flat,
        weights,
        counts.reshape(1, BRICKS),
        owners.reshape(1, BRICKS),
        slots.reshape(1, BRICKS),
    )))


def mm3(data, table):
    high, low = hi_lo(data)
    return mm(high, table[0]) + (mm(low, table[0]) + mm(high, table[1]))


def mm3_left(table, data):
    high, low = hi_lo(data)
    return mm(table[0], high) + (mm(table[0], low) + mm(table[1], high))


def place(x_ref, grid_ref, blocks):
    lane8 = iota((8, 128), 1)
    upper = jnp.concatenate([x_ref[pl.ds(rank, N_DEST, stride=MESSAGE), :] for rank in range(8)], axis=0)
    lower = jnp.concatenate([x_ref[pl.ds(8 + rank, N_DEST, stride=MESSAGE), :] for rank in range(8)], axis=0)
    ends = []
    for pair in range(4):
        joined = x_ref[pl.ds(16 + pair, N_DEST, stride=MESSAGE), :]
        ends += [joined, pltpu.roll(joined, 64, 1)]
    ends_high, ends_low = hi_lo(jnp.concatenate(ends, axis=0))
    weigh = jnp.where(lane8 == 40, 16.0, jnp.where(lane8 == 41, 1.0, 0.0)).astype(bf16)
    slot = mm_nt(weigh, ends_high)[0:1, :].astype(jnp.int32)
    high, low = hi_lo(jnp.concatenate([upper, lower], axis=1))
    ends = jnp.concatenate([ends_high, ends_low], axis=1)
    row = iota((128, SLOTS), 0)
    for at, block in enumerate(blocks):
        rows = slice(at * 128, (at + 1) * 128)
        pick = ((row // 16) * 64 + row % 16 + block * 16 == slot).astype(bf16)
        grid_ref[rows, 0:256] = mm(pick, high) + mm(pick, low)
        both = mm(pick, ends)
        grid_ref[rows, 256:384] = both[:, 0:128] + both[:, 128:256]


def swap_groups(tiles):
    group = iota((8, 128), 1) // 16
    for d in (1, 2, 4):
        mask = (group // d) % 2 == 0
        new = list(tiles)
        for a in range(8):
            if (a // d) % 2 == 0:
                one, two = tiles[a], tiles[a + d]
                new[a] = jnp.where(mask, one, pltpu.roll(two, 16 * d, 1))
                new[a + d] = jnp.where(mask, pltpu.roll(one, 128 - 16 * d, 1), two)
        tiles = new
    return tiles


def turn(side, corner):
    turned = [[pltpu.roll(side[half], 16 - i, 1) for half in range(2)] for i in range(16)]
    return turned + [[pltpu.roll(corner[half], 16, 1) for half in range(2)]]


def unpack_block(grid_ref, at):
    rows = [[None, None] for _ in range(17)]
    side, corner = [None, None], [None, None]
    for half in range(2):
        parts = []
        for third in range(3):
            parts.append(
                swap_groups(
                    [
                        grid_ref[at * 128 + col * 16 + half * 8 : at * 128 + col * 16 + half * 8 + 8, third * 128 : (third + 1) * 128]
                        for col in range(8)
                    ]
                )
            )
        for i in range(8):
            rows[i][half] = parts[0][i]
            rows[8 + i][half] = parts[1][i]
        rows[16][half] = parts[2][0]
        side[half] = parts[2][1]
        corner[half] = parts[2][2]
    return rows, side, corner


def add_spills(rows, turned, previous):
    lane8 = iota((8, 128), 1)
    out = []
    for i in range(17):
        pair = []
        for half in range(2):
            spill = jnp.where(lane8 % 16 == 0, turned[i][half], 0.0)
            first = 0.0 if previous is None else previous[i][half]
            pair.append(rows[i][half] + jnp.where(lane8 == 0, first, spill))
        out.append(pair)
    return out


def store_block(rows, ref):
    sub = iota((8, 128), 0)
    down = [pltpu.roll(rows[16][half], 1, 0) for half in range(2)]
    for i in range(16):
        low, high = rows[i]
        if i == 0:
            low = low + jnp.where(sub == 0, 0.0, down[0])
            high = high + jnp.where(sub == 0, down[0], down[1])
        ref[pl.ds(i, 8, stride=16), :] = low
        ref[pl.ds(128 + i, 8, stride=16), :] = high
    ref[256:264, :] = jnp.where(sub == 0, down[1], 0.0)
    ref[264:TILE_ROWS, :] = jnp.zeros((8, 128), f32)


def place_edges_kernel(x_ref, first_ref, last_ref, left_ref, right_ref, carry_ref, grid_ref, side_ref):
    place(x_ref, grid_ref, (0, 3))
    lane8 = iota((8, 128), 1)
    rows, side, corner = unpack_block(grid_ref, 0)
    store_block(add_spills(rows, turn(side, corner), None), first_ref)
    for half in range(2):
        carry_ref[half * 8 : half * 8 + 8, :] = side[half]
        carry_ref[16 + half * 8 : 24 + half * 8, :] = corner[half]
    rows, side, corner = unpack_block(grid_ref, 1)
    turned = turn(side, corner)
    rows = add_spills(rows, turned, None)
    store_block(rows, last_ref)
    store_block(
        [[jnp.where(lane8 == 0, turned[i][half], rows[i][half]) for half in range(2)] for i in range(17)], side_ref
    )
    right = [jnp.zeros((8, 128), f32)] * 5
    left = [jnp.zeros((8, 128), f32)] * 5
    for tile in range(33):
        group, at = divmod(tile, 5)
        rows8 = slice(tile * 8, tile * 8 + 8)
        both = side_ref[rows8, :]
        moved = jnp.where(lane8 == 112 + group, pltpu.roll(both, 112 + group, 1), right[at])
        right[at] = jnp.where(lane8 // 16 == group, pltpu.roll(both, 16 * group + 16, 1), moved)
        turned64 = pltpu.roll(first_ref[rows8, :], (64 + 16 * group) % 128, 1) if group != 4 else first_ref[rows8, :]
        left[at] = jnp.where(lane8 // 16 == group, turned64, left[at])
    for at in range(5):
        right_ref[at * 8 : at * 8 + 8, :] = right[at]
        left_ref[136 + at * 8 : 144 + at * 8, :] = left[at]
    lane = iota((136, 128), 1)
    left_ref[0:136, :] = jnp.where(lane < 64, first_ref[0:136, :], pltpu.roll(first_ref[136:272, :], 64, 1))


def place_edges(arrived):
    tile = jax.ShapeDtypeStruct((TILE_ROWS, 128), f32)
    return pl.pallas_call(
        place_edges_kernel,
        out_shape=(
            tile,
            tile,
            jax.ShapeDtypeStruct((LEFT_MESSAGE, 128), f32),
            jax.ShapeDtypeStruct((40, 128), f32),
            jax.ShapeDtypeStruct((32, 128), f32),
        ),
        scratch_shapes=[pltpu.VMEM((256, 384), f32), pltpu.VMEM((TILE_ROWS, 128), f32)],
        compiler_params=pltpu.CompilerParams(vmem_limit_bytes=32 << 20),
        cost_estimate=pl.CostEstimate(flops=600_000_000, bytes_accessed=2_000_000, transcendentals=0),
        name="place_edges",
    )(arrived)


def place_inner_kernel(x_ref, carry_ref, first_ref, last_ref, inner_ref, own_ref, grid_ref, second_ref, third_ref, fix_ref):
    place(x_ref, grid_ref, (1, 2))
    lane8 = iota((8, 128), 1)
    previous = turn(
        [carry_ref[half * 8 : half * 8 + 8, :] for half in range(2)],
        [carry_ref[16 + half * 8 : 24 + half * 8, :] for half in range(2)],
    )
    for at, ref in enumerate((second_ref, third_ref)):
        rows, side, corner = unpack_block(grid_ref, at)
        turned = turn(side, corner)
        store_block(add_spills(rows, turned, previous), ref)
        previous = turned
    store_block([[jnp.where(lane8 == 0, previous[i][half], 0.0) for half in range(2)] for i in range(17)], fix_ref)
    left = jnp.concatenate([first_ref[...], second_ref[...], third_ref[...]], axis=1)
    right = jnp.concatenate([third_ref[...], last_ref[...] + fix_ref[...]], axis=1)
    own_ref[:, 0:256] = mm3(left, inner_ref)
    own_ref[:, 256:512] = mm3(right, inner_ref[:, 0:256, :])


def place_inner(arrived, carry, first, last, inner):
    tile = pltpu.VMEM((TILE_ROWS, 128), f32)
    return pl.pallas_call(
        place_inner_kernel,
        out_shape=jax.ShapeDtypeStruct((TILE_ROWS, 512), f32),
        scratch_shapes=[pltpu.VMEM((256, 384), f32), tile, tile, tile],
        compiler_params=pltpu.CompilerParams(vmem_limit_bytes=32 << 20),
        cost_estimate=pl.CostEstimate(flops=800_000_000, bytes_accessed=3_000_000, transcendentals=0),
        name="place_inner",
    )(arrived, carry, first, last, inner)


def pack_tiles(tiles):
    lane = iota(tiles[0].shape, 1)
    shared = jnp.where((lane >= 56) & (lane < 72), pltpu.roll(tiles[5], 64, 1), tiles[2])
    return [tiles[0], tiles[1], shared, tiles[3], tiles[4]]


def unpack_tiles(tiles):
    return jnp.concatenate([*tiles, pltpu.roll(tiles[2], 64, 1)], axis=1)


def columns_kernel(
    own_ref, first_ref, to_right_ref, from_right_ref, from_left_ref, outer_ref, out_ref, down_ref
):
    lane8 = iota((8, 128), 1)
    none = jnp.zeros((8, 128), f32)
    spills, rows = [], []
    for tile in range(TILE_ROWS // 8):
        group, at = divmod(tile, 5)
        own = first_ref[tile * 8 : tile * 8 + 8, :]
        if tile == 33:
            spills.append(none)
            rows.append(jnp.concatenate([none, jnp.where(lane8 < 8, own, 0.0)], axis=1))
            continue
        packed = from_left_ref[at * 8 : at * 8 + 8, :]
        spill = jnp.where(lane8 == 0, pltpu.roll(packed, 16 - group, 1), 0.0)
        near = pltpu.roll(packed, 112 - 16 * group, 1)
        spills.append(spill)
        mixed = jnp.where(lane8 < 8, own + spill, jnp.where(lane8 >= 112, near, 0.0))
        wide = from_right_ref[(tile % 17) * 8 : (tile % 17) * 8 + 8, :]
        if tile >= 17:
            wide = pltpu.roll(wide, 64, 1)
        rest = from_right_ref[136 + at * 8 : 144 + at * 8, :]
        if group != 4:
            rest = pltpu.roll(rest, (64 - 16 * group) % 128, 1)
        over = jnp.where(lane8 == 0, pltpu.roll(to_right_ref[at * 8 : at * 8 + 8, :], 16 - group, 1), 0.0)
        right = jnp.where(lane8 < 64, wide, jnp.where(lane8 < 80, rest, 0.0)) + over
        rows.append(jnp.concatenate([right, mixed], axis=1))
    spill = jnp.concatenate(spills, axis=0)
    outer = mm3(jnp.concatenate(rows, axis=0), outer_ref)
    pieces = [
        own_ref[:, 0:128] + taps_low[0] * spill,
        own_ref[:, 256:384] + outer[:, 256:384],
        outer[:, 0:128],
        own_ref[:, 128:256] + taps_high[0] * spill,
        own_ref[:, 384:512] + outer[:, 384:512],
        outer[:, 128:256],
    ]
    for at, tile in enumerate(pack_tiles([piece[DOWN_FROM : DOWN_FROM + 24] for piece in pieces])):
        down_ref[at * 16 : at * 16 + 16, :] = tile[0:16]
        down_ref[80 + at : 81 + at, :] = tile[16:17]
    down_ref[85:88, :] = jnp.zeros((3, 128), f32)
    for at, piece in enumerate(pieces):
        out_ref[:, at * 128 : (at + 1) * 128] = piece


def outer_columns(own, first, to_right, from_right, from_left, outer):
    width = 2 * COL_ROOM[0]
    return pl.pallas_call(
        columns_kernel,
        out_shape=(
            jax.ShapeDtypeStruct((TILE_ROWS, width), f32),
            jax.ShapeDtypeStruct((DOWN_MESSAGE, 128), f32),
        ),
        compiler_params=pltpu.CompilerParams(vmem_limit_bytes=32 << 20),
        cost_estimate=pl.CostEstimate(flops=220_000_000, bytes_accessed=2_000_000, transcendentals=0),
        name="columns",
    )(own, first, to_right, from_right, from_left, outer)


def upward_kernel(own_ref, below_ref, up_ref):
    half = COL_ROOM[0]
    low = mm3_left(below_ref, own_ref[0:UP_ROWS, 0:half])
    high = mm3_left(below_ref[:, 0:32, :], own_ref[0:UP_ROWS, half : 2 * half])
    for part in range(2):
        rows16 = slice(part * 16, part * 16 + 16)
        fives = pack_tiles([side[rows16, at * 128 : (at + 1) * 128] for side in (low, high) for at in range(3)])
        for at, tile in enumerate(fives):
            up_ref[part * 80 + at * 16 : part * 80 + at * 16 + 16, :] = tile
    for at in range(3):
        up_ref[160 + at * 32 : 192 + at * 32, :] = low[32:64, at * 128 : (at + 1) * 128]


def upward(own, below):
    return pl.pallas_call(
        upward_kernel,
        out_shape=jax.ShapeDtypeStruct((UP_MESSAGE, 128), f32),
        compiler_params=pltpu.CompilerParams(vmem_limit_bytes=32 << 20),
        cost_estimate=pl.CostEstimate(flops=2_000_000_000, bytes_accessed=6_000_000, transcendentals=0),
        name="upward",
    )(own, below)


def own_rows_kernel(own_ref, table_ref, out_ref):
    for at in range(3):
        cols = slice(at * 256, (at + 1) * 256)
        out_ref[:, cols] = mm3_left(table_ref, own_ref[:, cols])


def own_rows(own, table):
    return pl.pallas_call(
        own_rows_kernel,
        out_shape=jax.ShapeDtypeStruct((2 * ROW_ROOM[0], 2 * COL_ROOM[0]), f32),
        compiler_params=pltpu.CompilerParams(vmem_limit_bytes=32 << 20),
        cost_estimate=pl.CostEstimate(flops=4_800_000_000, bytes_accessed=20_000_000, transcendentals=0),
        name="own_rows",
    )(own, table)


def levels_kernel(part_ref, below_ref, above_ref, table_ref, inner_ref, *refs):
    col_refs = (None,) + refs[0:3]
    row_refs = (None,) + refs[3:6]
    leader_refs = refs[6:10]
    approx_ref = refs[10]
    peak_ref = refs[11]
    sub = iota((8, 128), 0)
    above = [
        jnp.concatenate(
            [
                above_ref[at * 16 : at * 16 + 16, :],
                jnp.where(sub == 0, above_ref[80 + at : 81 + at, :], 0.0),
            ],
            axis=0,
        )
        for at in range(5)
    ]
    near = mm3_left(table_ref, unpack_tiles(above))
    half = COL_ROOM[0]
    sixes = [
        unpack_tiles([below_ref[part * 80 + at * 16 : part * 80 + at * 16 + 16, :] for at in range(5)])
        for part in range(2)
    ]
    threes = jnp.concatenate([below_ref[160 + at * 32 : 192 + at * 32, :] for at in range(3)], axis=1)
    threes = jnp.concatenate([threes, jnp.zeros((32, half), f32)], axis=1)
    added = {0: near[0:8], 184: near[8:16], 192: near[16:24], 376: near[24:32]}
    added.update({120: sixes[0], 136: threes, 312: sixes[1]})
    cuts = sorted({0, 8, 120, 136, 168, 184, 192, 200, 312, 328, 376, 384})
    both = jnp.concatenate(
        [
            part_ref[start:stop, :] + added[start] if start in added else part_ref[start:stop, :]
            for start, stop in zip(cuts, cuts[1:])
        ],
        axis=0,
    )
    peak = None
    for level in range(4):
        room_r = ROW_ROOM[level]
        room_c = COL_ROOM[level]
        if level == 1:
            main = mm3(current, inner_ref)
            rest = mm3(jnp.concatenate([current[:, 256:384], current[:, 0:128]], axis=1), col_refs[1])
            parts = (main[:, 0:128], rest[:, 0:128], main[:, 128:256], rest[:, 128:256])
            both = mm3_left(row_refs[1], jnp.concatenate(parts, axis=1))
        elif level:
            both = mm3_left(row_refs[level], mm3(current, col_refs[level]))
        current = both[:room_r, :room_c]
        detail_a = both[:room_r, room_c:]
        detail_b = both[room_r:, :room_c]
        detail_c = both[room_r:, room_c:]
        now = jnp.maximum(jnp.maximum(jnp.abs(detail_a), jnp.abs(detail_b)), jnp.abs(detail_c))
        if peak is not None:
            now = jnp.maximum(now, peak)
        wide = jnp.maximum(now, jnp.maximum(pltpu.roll(now, 1, 1), pltpu.roll(now, room_c - 1, 1)))
        wide = jnp.maximum(wide, jnp.maximum(pltpu.roll(wide, 1, 0), pltpu.roll(wide, room_r - 1, 0)))
        n_r = R_DEV >> (level + 1)
        n_c = C_DEV >> (level + 1)
        leader_refs[level][...] = wide[:n_r, :n_c]
        if level < 3:
            pairs = jnp.maximum(now, pltpu.roll(now, room_c - 1, 1))
            pooled = []
            for across in range(room_c // 128):
                top = across * ROW_ROOM[0]
                peak_ref[top : top + room_r, :] = pairs[:, across * 128 : (across + 1) * 128]
                pooled.append(
                    jnp.maximum(
                        peak_ref[pl.ds(top, room_r // 2, stride=2), :],
                        peak_ref[pl.ds(top + 1, room_r // 2, stride=2), :],
                    )
                )
            high, low = hi_lo(jnp.concatenate(pooled, axis=1) if len(pooled) > 1 else pooled[0])
            room_n = COL_ROOM[level + 1]
            out = iota((room_c, room_n), 1)
            source = 2 * out + jnp.where(out < 3 * room_n // 4, 0, room_c - 2 * room_n)
            pick = (iota((room_c, room_n), 0) == source).astype(bf16)
            peak = mm(high, pick) + mm(low, pick)
    approx_ref[...] = current[: R_DEV >> 4, : C_DEV >> 4]


def all_levels(part, below, above, near, inner, cols, rows):
    shapes = [(R_DEV >> level, C_DEV >> level) for level in (1, 2, 3, 4, 4)]
    return pl.pallas_call(
        levels_kernel,
        out_shape=tuple(jax.ShapeDtypeStruct(shape, f32) for shape in shapes),
        scratch_shapes=[pltpu.VMEM((3 * ROW_ROOM[0], 128), f32)],
        compiler_params=pltpu.CompilerParams(vmem_limit_bytes=32 << 20),
        name="levels",
    )(part, below, above, near, inner, *cols, *rows)


def shifted(x, axis, by):
    size = lax.axis_size(axis)
    return lax.ppermute(x, axis, [(i, (i + by) % size) for i in range(size)])


def transform(arrived):
    table = jax.tree.map(jnp.asarray, tables())
    first, last, to_left, to_right, carry = place_edges(arrived)
    from_right = shifted(to_left, "cols", -1)
    from_left = shifted(to_right, "cols", 1)
    inner = place_inner(arrived, carry, first, last, table["inner"])
    own, to_down = outer_columns(inner, first, to_right, from_right, from_left, table["outer"])
    above = shifted(to_down, "rows", 1)
    below = shifted(upward(own, table["below"]), "rows", -1)
    part = own_rows(own, table["own"])
    return all_levels(part, below, above, table["above"], table["inner"], table["cols"], table["rows"])


def on_device(offsets, lens_weight, counts, owners, brick_slot):
    packed = deposit_and_pack(offsets, lens_weight, counts, owners, brick_slot)
    arrived = lax.all_to_all(
        packed.reshape(N_DEST, MESSAGE // 4, 4, 128), ("rows", "cols"), split_axis=0, concat_axis=0, tiled=True
    )
    return transform(arrived.reshape(N_DEST * MESSAGE, 128))


def solution(mesh):
    placed = (
        P(("rows", "cols"), None, None),
        P(("rows", "cols"), None),
        P(("rows", "cols")),
        P(("rows", "cols")),
        P(("rows", "cols")),
    )
    return jax.shard_map(
        on_device,
        mesh=mesh,
        in_specs=placed,
        out_specs=(P("rows", "cols"),) * 5,
        check_vma=False,
    )
```

```python
import functools

import jax
import jax.numpy as jnp
import numpy as np
from jax import lax
from jax.experimental import pallas as pl
from jax.experimental.pallas import tpu as pltpu
from jax.sharding import PartitionSpec as P

R_DEV = 256
C_DEV = 512
PMAX = 256
CAP = 8
N_DEST = 128
BRICKS = 512
SLOTS = N_DEST * CAP

TILE_ROWS = 272
UP_ROWS = 80
DOWN_ROWS = 24
DOWN_FROM = 240
ROW_ROOM = (192, 96, 48, 24)
COL_ROOM = (384, 256, 128, 128)

taps_low = (
    0.33267055295008263,
    0.8068915093110925,
    0.4598775021184915,
    -0.13501102001025458,
    -0.08544127388202666,
    0.03522629188570953,
)
taps_high = tuple(((-1.0) ** index * taps_low[5 - index] for index in range(6)))

f32 = jnp.float32
bf16 = jnp.bfloat16


def spans(size):
    out = []
    for level in range(1, 5):
        n = size >> level
        before = 8 >> (level - 1)
        after = (36, 16, 6, 1)[level - 1]
        out.append((-before, n + after, -before, n + before))
    return out


def level_table(sources, room, span):
    low_from, low_to, high_from, high_to = span
    table = np.zeros((len(sources), 2 * room), np.float64)
    for position, index in enumerate(sources):
        if index is None:
            continue
        for half, (lo, hi, taps) in enumerate(
            ((low_from, low_to, taps_low), (high_from, high_to, taps_high))
        ):
            for tap in range(6):
                if (index - tap) % 2 == 0:
                    k = (index - tap) // 2
                    if lo <= k < hi:
                        table[position, half * room + (k % room)] += taps[tap]
    return table


def room_sources(room, low_from, low_to):
    out = [None] * room
    for k in range(low_from, low_to):
        out[k % room] = k
    return out


def split(table):
    table = np.asarray(table, np.float32)
    high = table.astype(jnp.bfloat16)
    low = (table - high.astype(np.float32)).astype(jnp.bfloat16)
    return np.stack([high, low])


ABOVE_ROWS = ((0, 8), (184, 192), (192, 200), (376, 384))
BELOW_ROWS = ((120, 136), (312, 328), (136, 168))
SECOND_ROWS = ((0, 8), (120, 136), (136, 168), (184, 192))
UP_MESSAGE = 5 * 16 + 5 * 16 + 3 * 32
DOWN_MESSAGE = 5 * 16 + 8
LEFT_MESSAGE = TILE_ROWS // 2 + 40


@functools.lru_cache(maxsize=1)
def tables():
    col_spans = spans(C_DEV)
    row_spans = spans(R_DEV)
    inner = level_table(list(range(384)), 128, (0, 128, 0, 128))
    right = [C_DEV + j if j < 76 else None for j in range(128)] + [None] * 128
    mixed = [None] * 128 + list(range(8)) + [None] * 104 + [j - 16 for j in range(16)]
    room = COL_ROOM[0]
    beyond = level_table(right, room, (256, 292, 256, 264)) + level_table(mixed, room, (-8, 0, -8, 0))
    partial = level_table(right, room, (254, 256, 254, 256))
    outer = np.concatenate(
        [
            beyond[:, 256:384],
            beyond[:, room + 256 : room + 384],
            partial[:, 128:256],
            partial[:, room + 128 : room + 256],
        ],
        axis=1,
    )
    row_src = [i if i < 257 else None for i in range(TILE_ROWS)]
    row_src += [R_DEV + i if i < 76 else None for i in range(UP_ROWS)]
    row_src += [i - 16 if i < 17 else None for i in range(DOWN_ROWS)]
    third = [256 + j if j < 36 else j - 128 if j >= 120 else None for j in range(128)] + [None] * 128
    room = COL_ROOM[1]
    rest = level_table(third, room, col_spans[1])
    rest += level_table([None] * 128 + list(range(8)) + [None] * 120, room, (-4, 0, -4, 0))
    rest = np.concatenate([rest[:, 128:256], rest[:, room + 128 : room + 256]], axis=1)
    cols, rows = [rest], []
    for level in range(4):
        if level > 1:
            cols.append(level_table(col_src, COL_ROOM[level], col_spans[level]))
        rows.append(level_table(row_src, ROW_ROOM[level], row_spans[level]).T)
        col_src = room_sources(COL_ROOM[level], col_spans[level][0], col_spans[level][1])
        row_src = room_sources(ROW_ROOM[level], row_spans[level][0], row_spans[level][1])
    first = rows[0]
    below = first[:, TILE_ROWS : TILE_ROWS + UP_ROWS]
    above = first[:, TILE_ROWS + UP_ROWS :]
    for part, kept in ((below, BELOW_ROWS), (above, ABOVE_ROWS)):
        far = np.ones(first.shape[0], bool)
        for start, stop in kept:
            far[start:stop] = False
        assert not part[far].any()
    below = np.concatenate([below[start:stop] for start, stop in BELOW_ROWS], axis=0)
    above = np.concatenate([above[start:stop] for start, stop in ABOVE_ROWS], axis=0)
    second = np.concatenate([rows[1][:, start:stop] for start, stop in SECOND_ROWS], axis=1)
    return {
        "second": split(second),
        "inner": split(inner),
        "outer": split(outer),
        "own": split(first[:, :TILE_ROWS]),
        "below": split(below),
        "above": split(above),
        "cols": [split(t) for t in cols],
        "rows": [split(t) for t in rows[1:]],
    }


def hi_lo(x):
    high = x.astype(bf16)
    low = (x - high.astype(f32)).astype(bf16)
    return high, low


def mm(a, b):
    return jnp.dot(a, b, preferred_element_type=f32)


def mm_nt(a, b):
    return lax.dot_general(a, b, (((1,), (1,)), ((), ())), preferred_element_type=f32)


def iota(shape, dim):
    return lax.broadcasted_iota(jnp.int32, shape, dim)


STEPS = 4
STEP_BRICKS = BRICKS // STEPS
MESSAGE = 20


def deposit_kernel(
    off_hbm,
    w_hbm,
    counts_hbm,
    owners_hbm,
    slot_hbm,
    out_ref,
    off_ref,
    w_ref,
    counts_ref,
    owners_ref,
    slot_ref,
    cnt_ref,
    patch_ref,
    edge_ref,
    small_sem,
    off_sem,
    w_sem,
):
    small = [
        pltpu.make_async_copy(src, dst, small_sem.at[n])
        for n, (src, dst) in enumerate(
            ((owners_hbm, owners_ref), (slot_hbm, slot_ref), (counts_hbm, counts_ref))
        )
    ]
    for copy in small:
        copy.start()

    def fetch(index):
        off_rows = pl.ds(index * 4 * STEP_BRICKS, 4 * STEP_BRICKS)
        w_rows = pl.ds(index * STEP_BRICKS, STEP_BRICKS)
        return (
            pltpu.make_async_copy(off_hbm.at[off_rows], off_ref.at[off_rows], off_sem.at[index]),
            pltpu.make_async_copy(w_hbm.at[w_rows], w_ref.at[w_rows], w_sem.at[index]),
        )

    for index in range(STEPS):
        for copy in fetch(index):
            copy.start()
    for copy in small:
        copy.wait()

    owners = owners_ref[...]
    dest = (iota((N_DEST, BRICKS), 0) == owners).astype(f32)
    before = (iota((BRICKS, BRICKS), 0) < iota((BRICKS, BRICKS), 1)).astype(bf16)
    ranks = jnp.sum(mm(dest.astype(bf16), before) * dest, axis=0, keepdims=True)
    position = ranks.astype(jnp.int32) * N_DEST + owners

    slot = slot_ref[...]
    grid_row = slot // 32
    grid_col = slot % 32
    coarse = (grid_col % 8) * 4 + grid_col // 8
    row_id = iota((256, BRICKS), 0)
    spread = jnp.where(
        row_id < 128,
        counts_ref[...],
        jnp.where(row_id == 168, coarse, jnp.where(row_id == 169, grid_row, 0)),
    )
    eye = (iota((BRICKS, BRICKS), 0) == iota((BRICKS, BRICKS), 1)).astype(bf16)
    cnt_ref[...] = mm_nt(eye, spread.astype(f32).astype(bf16))

    lane = iota((8, 128), 1)
    sub = iota((8, 128), 0)
    particle = iota((8, PMAX), 1).astype(f32)
    cell = iota((16, PMAX), 0).astype(f32)

    zero = jnp.zeros((), bf16)
    bit = {at: (lane >> at) % 2 == 1 for at in (3, 4, 5, 6)}

    def choose(tiles, mask):
        return [jnp.where(mask, odd, even) for even, odd in zip(tiles[0::2], tiles[1::2])]

    def one_group(start):
        first = start * 4
        rows_at = jnp.concatenate([off_ref[pl.ds(first + 2 * half, 8, stride=4), :] for half in range(2)], axis=1)
        cols_at = jnp.concatenate([off_ref[pl.ds(first + 2 * half + 1, 8, stride=4), :] for half in range(2)], axis=1)
        count = cnt_ref[pl.ds(start, 8), 0:128]
        count = jnp.concatenate([count, count], axis=1)
        weight = jnp.where(particle < count, w_ref[pl.ds(start, 8), :], 0.0)
        lag = rows_at * weight
        left = []
        for i in range(17):
            left.append(weight - jnp.abs(lag))
            lag = lag - weight
        left = jnp.maximum(jnp.concatenate(left, axis=0).astype(bf16), zero)
        right = []
        for g in range(8):
            at = first + 4 * ((8 - g) % 8) + 1
            column = jnp.concatenate([off_ref[pl.ds(at + 2 * half, 8, stride=0), :] for half in range(2)], axis=1)
            right += [1.0 - jnp.abs(column - cell[0:8]), 1.0 - jnp.abs(column - cell[8:16])]
        last = cols_at - 15.0
        right = [jnp.maximum(jnp.concatenate(right, axis=0).astype(bf16), zero)]
        right += [jnp.maximum(jnp.concatenate([last, last], axis=0).astype(bf16), zero)] * 8
        full = mm_nt(left, jnp.concatenate(right, axis=0))
        halves = []
        for half in range(2):
            pairs = []
            for pair in range(4):
                at = (half * 8 + pair * 2) * 8
                even = pltpu.roll(full[at : at + 8, 0:128], 0, 1, stride=16, stride_axis=0)
                odd = pltpu.roll(full[at + 8 : at + 16, 0:128], 16, 1, stride=16, stride_axis=0)
                both = jnp.where(bit[4], odd, even)
                pairs.append(pltpu.roll(both, 32 * pair, 1) if pair else both)
            halves.append(choose(choose(pairs, bit[5]), bit[6])[0])
        bottom = pltpu.roll(full[128:136, 0:128], 0, 1, stride=16, stride_axis=0)
        corner = jnp.sum(jnp.where(lane == sub, full[128:136, 128:256], 0.0), axis=1, keepdims=True)
        third = jnp.where(lane < 16, bottom, jnp.where(lane == 32, corner, 0.0))
        edge = [full[8 * i : 8 * i + 8, 128:256] for i in range(16)]
        for at in range(3, 7):
            edge = choose(edge, bit[at])
        edge = jnp.where(lane % 8 == sub, edge[0], 0.0)
        patch_ref[pl.ds(start, 8), 0:128] = halves[0]
        patch_ref[pl.ds(start, 8), 128:256] = halves[1]
        patch_ref[pl.ds(start, 8), 256:384] = third + cnt_ref[pl.ds(start, 8), 128:256]
        edge_ref[pl.ds(start, 8), :] = edge

    for index in range(STEPS):
        for copy in fetch(index):
            copy.wait()
    for group in range(BRICKS // 8):
        one_group(group * 8)

    gather = (iota((128, 128), 1) == iota((128, 128), 0) // 8 + 16).astype(bf16)
    edge_high, edge_low = hi_lo(edge_ref[...])
    third = patch_ref[:, 256:384] + (mm(edge_high, gather) + mm(edge_low, gather))

    high, low = hi_lo(patch_ref[:, 0:256])
    ends = jnp.concatenate(hi_lo(third), axis=1)
    lane_wide = iota((N_DEST, 128), 1)
    for pair in range(4):
        edges = []
        for rank in (2 * pair, 2 * pair + 1):
            pick = (iota((N_DEST, BRICKS), 0) + rank * N_DEST == position).astype(bf16)
            inner = mm(pick, high) + mm(pick, low)
            out_ref[pl.ds(rank, N_DEST, stride=MESSAGE), :] = inner[:, 0:128]
            out_ref[pl.ds(8 + rank, N_DEST, stride=MESSAGE), :] = inner[:, 128:256]
            both = mm(pick, ends)
            edges.append(both[:, 0:128] + both[:, 128:256])
        joined = jnp.where(lane_wide < 64, edges[0], pltpu.roll(edges[1], 64, 1))
        out_ref[pl.ds(16 + pair, N_DEST, stride=MESSAGE), :] = joined


def deposit_and_pack(offsets, weights, counts, owners, slots):
    flat = offsets.reshape(BRICKS, 2, 2, 128).transpose(0, 2, 1, 3).reshape(4 * BRICKS, 128)
    return pl.pallas_call(
        deposit_kernel,
        out_shape=jax.ShapeDtypeStruct((N_DEST * MESSAGE, 128), f32),
        in_specs=[pl.BlockSpec(memory_space=pltpu.MemorySpace.HBM)] * 5,
        scratch_shapes=[
            pltpu.VMEM((4 * BRICKS, 128), f32),
            pltpu.VMEM((BRICKS, PMAX), f32),
            pltpu.VMEM((1, BRICKS), jnp.int32),
            pltpu.VMEM((1, BRICKS), jnp.int32),
            pltpu.VMEM((1, BRICKS), jnp.int32),
            pltpu.VMEM((BRICKS, 256), f32),
            pltpu.VMEM((BRICKS, 384), f32),
            pltpu.VMEM((BRICKS, 128), f32),
            pltpu.SemaphoreType.DMA((3,)),
            pltpu.SemaphoreType.DMA((STEPS,)),
            pltpu.SemaphoreType.DMA((STEPS,)),
        ],
        compiler_params=pltpu.CompilerParams(vmem_limit_bytes=40 << 20),
        name="deposit",
    )(*(pltpu.with_memory_space_constraint(x, pltpu.MemorySpace.HBM) for x in (
        flat,
        weights,
        counts.reshape(1, BRICKS),
        owners.reshape(1, BRICKS),
        slots.reshape(1, BRICKS),
    )))


def mm3(data, table):
    high, low = hi_lo(data)
    return mm(high, table[0]) + (mm(low, table[0]) + mm(high, table[1]))


def mm3_left(table, data):
    high, low = hi_lo(data)
    return mm(table[0], high) + (mm(table[0], low) + mm(table[1], high))


def place(x_ref, grid_ref, blocks):
    lane8 = iota((8, 128), 1)
    upper = jnp.concatenate([x_ref[pl.ds(rank, N_DEST, stride=MESSAGE), :] for rank in range(8)], axis=0)
    lower = jnp.concatenate([x_ref[pl.ds(8 + rank, N_DEST, stride=MESSAGE), :] for rank in range(8)], axis=0)
    ends = []
    for pair in range(4):
        joined = x_ref[pl.ds(16 + pair, N_DEST, stride=MESSAGE), :]
        ends += [joined, pltpu.roll(joined, 64, 1)]
    ends_high, ends_low = hi_lo(jnp.concatenate(ends, axis=0))
    weigh = jnp.where(lane8 == 40, 16.0, jnp.where(lane8 == 41, 1.0, 0.0)).astype(bf16)
    slot = mm_nt(weigh, ends_high)[0:1, :].astype(jnp.int32)
    high, low = hi_lo(jnp.concatenate([upper, lower], axis=1))
    ends = jnp.concatenate([ends_high, ends_low], axis=1)
    row = iota((128, SLOTS), 0)
    for at, block in enumerate(blocks):
        rows = slice(at * 128, (at + 1) * 128)
        pick = ((row // 16) * 64 + row % 16 + block * 16 == slot).astype(bf16)
        grid_ref[rows, 0:256] = mm(pick, high) + mm(pick, low)
        both = mm(pick, ends)
        grid_ref[rows, 256:384] = both[:, 0:128] + both[:, 128:256]


def swap_groups(tiles):
    group = iota((8, 128), 1) // 16
    for d in (1, 2, 4):
        mask = (group // d) % 2 == 0
        new = list(tiles)
        for a in range(8):
            if (a // d) % 2 == 0:
                one, two = tiles[a], tiles[a + d]
                new[a] = jnp.where(mask, one, pltpu.roll(two, 16 * d, 1))
                new[a + d] = jnp.where(mask, pltpu.roll(one, 128 - 16 * d, 1), two)
        tiles = new
    return tiles


def turn(side, corner):
    turned = [[pltpu.roll(side[half], 16 - i, 1) for half in range(2)] for i in range(16)]
    return turned + [[pltpu.roll(corner[half], 16, 1) for half in range(2)]]


def unpack_block(grid_ref, at):
    rows = [[None, None] for _ in range(17)]
    side, corner = [None, None], [None, None]
    for half in range(2):
        parts = []
        for third in range(3):
            parts.append(
                swap_groups(
                    [
                        grid_ref[at * 128 + col * 16 + half * 8 : at * 128 + col * 16 + half * 8 + 8, third * 128 : (third + 1) * 128]
                        for col in range(8)
                    ]
                )
            )
        for i in range(8):
            rows[i][half] = parts[0][i]
            rows[8 + i][half] = parts[1][i]
        rows[16][half] = parts[2][0]
        side[half] = parts[2][1]
        corner[half] = parts[2][2]
    return rows, side, corner


def add_spills(rows, turned, previous):
    lane8 = iota((8, 128), 1)
    out = []
    for i in range(17):
        pair = []
        for half in range(2):
            spill = jnp.where(lane8 % 16 == 0, turned[i][half], 0.0)
            first = 0.0 if previous is None else previous[i][half]
            pair.append(rows[i][half] + jnp.where(lane8 == 0, first, spill))
        out.append(pair)
    return out


def store_block(rows, ref):
    sub = iota((8, 128), 0)
    down = [pltpu.roll(rows[16][half], 1, 0) for half in range(2)]
    for i in range(16):
        low, high = rows[i]
        if i == 0:
            low = low + jnp.where(sub == 0, 0.0, down[0])
            high = high + jnp.where(sub == 0, down[0], down[1])
        ref[pl.ds(i, 8, stride=16), :] = low
        ref[pl.ds(128 + i, 8, stride=16), :] = high
    ref[256:264, :] = jnp.where(sub == 0, down[1], 0.0)
    ref[264:TILE_ROWS, :] = jnp.zeros((8, 128), f32)


def place_edges_kernel(x_ref, first_ref, last_ref, left_ref, right_ref, carry_ref, grid_ref, side_ref):
    place(x_ref, grid_ref, (0, 3))
    lane8 = iota((8, 128), 1)
    rows, side, corner = unpack_block(grid_ref, 0)
    store_block(add_spills(rows, turn(side, corner), None), first_ref)
    for half in range(2):
        carry_ref[half * 8 : half * 8 + 8, :] = side[half]
        carry_ref[16 + half * 8 : 24 + half * 8, :] = corner[half]
    rows, side, corner = unpack_block(grid_ref, 1)
    turned = turn(side, corner)
    rows = add_spills(rows, turned, None)
    store_block(rows, last_ref)
    store_block(
        [[jnp.where(lane8 == 0, turned[i][half], rows[i][half]) for half in range(2)] for i in range(17)], side_ref
    )
    right = [jnp.zeros((8, 128), f32)] * 5
    left = [jnp.zeros((8, 128), f32)] * 5
    for tile in range(33):
        group, at = divmod(tile, 5)
        rows8 = slice(tile * 8, tile * 8 + 8)
        both = side_ref[rows8, :]
        moved = jnp.where(lane8 == 112 + group, pltpu.roll(both, 112 + group, 1), right[at])
        right[at] = jnp.where(lane8 // 16 == group, pltpu.roll(both, 16 * group + 16, 1), moved)
        turned64 = pltpu.roll(first_ref[rows8, :], (64 + 16 * group) % 128, 1) if group != 4 else first_ref[rows8, :]
        left[at] = jnp.where(lane8 // 16 == group, turned64, left[at])
    for at in range(5):
        right_ref[at * 8 : at * 8 + 8, :] = right[at]
        left_ref[136 + at * 8 : 144 + at * 8, :] = left[at]
    lane = iota((136, 128), 1)
    left_ref[0:136, :] = jnp.where(lane < 64, first_ref[0:136, :], pltpu.roll(first_ref[136:272, :], 64, 1))


def place_edges(arrived):
    tile = jax.ShapeDtypeStruct((TILE_ROWS, 128), f32)
    return pl.pallas_call(
        place_edges_kernel,
        out_shape=(
            tile,
            tile,
            jax.ShapeDtypeStruct((LEFT_MESSAGE, 128), f32),
            jax.ShapeDtypeStruct((40, 128), f32),
            jax.ShapeDtypeStruct((32, 128), f32),
        ),
        scratch_shapes=[pltpu.VMEM((256, 384), f32), pltpu.VMEM((TILE_ROWS, 128), f32)],
        compiler_params=pltpu.CompilerParams(vmem_limit_bytes=32 << 20),
        cost_estimate=pl.CostEstimate(flops=600_000_000, bytes_accessed=2_000_000, transcendentals=0),
        name="place_edges",
    )(arrived)


def place_inner_kernel(x_ref, carry_ref, first_ref, last_ref, inner_ref, own_ref, grid_ref, second_ref, third_ref, fix_ref):
    place(x_ref, grid_ref, (1, 2))
    lane8 = iota((8, 128), 1)
    previous = turn(
        [carry_ref[half * 8 : half * 8 + 8, :] for half in range(2)],
        [carry_ref[16 + half * 8 : 24 + half * 8, :] for half in range(2)],
    )
    for at, ref in enumerate((second_ref, third_ref)):
        rows, side, corner = unpack_block(grid_ref, at)
        turned = turn(side, corner)
        store_block(add_spills(rows, turned, previous), ref)
        previous = turned
    store_block([[jnp.where(lane8 == 0, previous[i][half], 0.0) for half in range(2)] for i in range(17)], fix_ref)
    left = jnp.concatenate([first_ref[...], second_ref[...], third_ref[...]], axis=1)
    right = jnp.concatenate([third_ref[...], last_ref[...] + fix_ref[...]], axis=1)
    own_ref[:, 0:256] = mm3(left, inner_ref)
    own_ref[:, 256:512] = mm3(right, inner_ref[:, 0:256, :])


def place_inner(arrived, carry, first, last, inner):
    tile = pltpu.VMEM((TILE_ROWS, 128), f32)
    return pl.pallas_call(
        place_inner_kernel,
        out_shape=jax.ShapeDtypeStruct((TILE_ROWS, 512), f32),
        scratch_shapes=[pltpu.VMEM((256, 384), f32), tile, tile, tile],
        compiler_params=pltpu.CompilerParams(vmem_limit_bytes=32 << 20),
        cost_estimate=pl.CostEstimate(flops=800_000_000, bytes_accessed=3_000_000, transcendentals=0),
        name="place_inner",
    )(arrived, carry, first, last, inner)


def pack_tiles(tiles):
    lane = iota(tiles[0].shape, 1)
    shared = jnp.where((lane >= 56) & (lane < 72), pltpu.roll(tiles[5], 64, 1), tiles[2])
    return [tiles[0], tiles[1], shared, tiles[3], tiles[4]]


def unpack_tiles(tiles):
    return jnp.concatenate([*tiles, pltpu.roll(tiles[2], 64, 1)], axis=1)


def columns_kernel(
    own_ref, first_ref, to_right_ref, from_right_ref, from_left_ref, outer_ref, below_ref, out_ref, up_ref, down_ref
):
    lane8 = iota((8, 128), 1)
    none = jnp.zeros((8, 128), f32)
    spills, rows = [], []
    for tile in range(TILE_ROWS // 8):
        group, at = divmod(tile, 5)
        own = first_ref[tile * 8 : tile * 8 + 8, :]
        if tile == 33:
            spills.append(none)
            rows.append(jnp.concatenate([none, jnp.where(lane8 < 8, own, 0.0)], axis=1))
            continue
        packed = from_left_ref[at * 8 : at * 8 + 8, :]
        spill = jnp.where(lane8 == 0, pltpu.roll(packed, 16 - group, 1), 0.0)
        near = pltpu.roll(packed, 112 - 16 * group, 1)
        spills.append(spill)
        mixed = jnp.where(lane8 < 8, own + spill, jnp.where(lane8 >= 112, near, 0.0))
        wide = from_right_ref[(tile % 17) * 8 : (tile % 17) * 8 + 8, :]
        if tile >= 17:
            wide = pltpu.roll(wide, 64, 1)
        rest = from_right_ref[136 + at * 8 : 144 + at * 8, :]
        if group != 4:
            rest = pltpu.roll(rest, (64 - 16 * group) % 128, 1)
        over = jnp.where(lane8 == 0, pltpu.roll(to_right_ref[at * 8 : at * 8 + 8, :], 16 - group, 1), 0.0)
        right = jnp.where(lane8 < 64, wide, jnp.where(lane8 < 80, rest, 0.0)) + over
        rows.append(jnp.concatenate([right, mixed], axis=1))
    spill = jnp.concatenate(spills, axis=0)
    outer = mm3(jnp.concatenate(rows, axis=0), outer_ref)
    pieces = [
        own_ref[:, 0:128] + taps_low[0] * spill,
        own_ref[:, 256:384] + outer[:, 256:384],
        outer[:, 0:128],
        own_ref[:, 128:256] + taps_high[0] * spill,
        own_ref[:, 384:512] + outer[:, 384:512],
        outer[:, 128:256],
    ]
    low = mm3_left(below_ref, jnp.concatenate([piece[0:UP_ROWS] for piece in pieces[0:3]], axis=1))
    high = mm3_left(below_ref[:, 0:32, :], jnp.concatenate([piece[0:UP_ROWS] for piece in pieces[3:6]], axis=1))
    for part in range(2):
        rows16 = slice(part * 16, part * 16 + 16)
        fives = pack_tiles([half[rows16, at * 128 : (at + 1) * 128] for half in (low, high) for at in range(3)])
        for at, tile in enumerate(fives):
            up_ref[part * 80 + at * 16 : part * 80 + at * 16 + 16, :] = tile
    for at in range(3):
        up_ref[160 + at * 32 : 192 + at * 32, :] = low[32:64, at * 128 : (at + 1) * 128]
    for at, tile in enumerate(pack_tiles([piece[DOWN_FROM : DOWN_FROM + 24] for piece in pieces])):
        down_ref[at * 16 : at * 16 + 16, :] = tile[0:16]
        down_ref[80 + at : 81 + at, :] = tile[16:17]
    down_ref[85:88, :] = jnp.zeros((3, 128), f32)
    for at, piece in enumerate(pieces):
        out_ref[:, at * 128 : (at + 1) * 128] = piece


def outer_columns(own, first, to_right, from_right, from_left, outer, below):
    width = 2 * COL_ROOM[0]
    return pl.pallas_call(
        columns_kernel,
        out_shape=(
            jax.ShapeDtypeStruct((TILE_ROWS, width), f32),
            jax.ShapeDtypeStruct((UP_MESSAGE, 128), f32),
            jax.ShapeDtypeStruct((DOWN_MESSAGE, 128), f32),
        ),
        compiler_params=pltpu.CompilerParams(vmem_limit_bytes=32 << 20),
        cost_estimate=pl.CostEstimate(flops=220_000_000, bytes_accessed=2_000_000, transcendentals=0),
        name="columns",
    )(own, first, to_right, from_right, from_left, outer, below)


def second_columns(current, inner, rest):
    main = mm3(current, inner)
    rest = mm3(jnp.concatenate([current[:, 256:384], current[:, 0:128]], axis=1), rest)
    return jnp.concatenate([main[:, 0:128], rest[:, 0:128], main[:, 128:256], rest[:, 128:256]], axis=1)


def own_rows_kernel(own_ref, table_ref, inner_ref, rest_ref, rows_ref, out_ref, second_ref):
    for at in range(3):
        cols = slice(at * 256, (at + 1) * 256)
        out_ref[:, cols] = mm3_left(table_ref, own_ref[:, cols])
    current = out_ref[0 : ROW_ROOM[0], 0 : COL_ROOM[0]]
    second_ref[...] = mm3_left(rows_ref, second_columns(current, inner_ref, rest_ref))


def own_rows(own, table, inner, rest, rows):
    return pl.pallas_call(
        own_rows_kernel,
        out_shape=(
            jax.ShapeDtypeStruct((2 * ROW_ROOM[0], 2 * COL_ROOM[0]), f32),
            jax.ShapeDtypeStruct((2 * ROW_ROOM[1], 2 * COL_ROOM[1]), f32),
        ),
        compiler_params=pltpu.CompilerParams(vmem_limit_bytes=32 << 20),
        cost_estimate=pl.CostEstimate(flops=4_800_000_000, bytes_accessed=20_000_000, transcendentals=0),
        name="own_rows",
    )(own, table, inner, rest, rows)


def levels_kernel(part_ref, second_ref, below_ref, above_ref, table_ref, inner_ref, added_ref, *refs):
    col_refs = (None,) + refs[0:3]
    row_refs = (None, None) + refs[3:5]
    leader_refs = refs[5:9]
    approx_ref = refs[9]
    peak_ref = refs[10]
    sub = iota((8, 128), 0)
    above = [
        jnp.concatenate(
            [
                above_ref[at * 16 : at * 16 + 16, :],
                jnp.where(sub == 0, above_ref[80 + at : 81 + at, :], 0.0),
            ],
            axis=0,
        )
        for at in range(5)
    ]
    near = mm3_left(table_ref, unpack_tiles(above))
    half = COL_ROOM[0]
    sixes = [
        unpack_tiles([below_ref[part * 80 + at * 16 : part * 80 + at * 16 + 16, :] for at in range(5)])
        for part in range(2)
    ]
    threes = jnp.concatenate([below_ref[160 + at * 32 : 192 + at * 32, :] for at in range(3)], axis=1)
    threes = jnp.concatenate([threes, jnp.zeros((32, half), f32)], axis=1)
    added = {0: near[0:8], 184: near[8:16], 192: near[16:24], 376: near[24:32]}
    added.update({120: sixes[0], 136: threes, 312: sixes[1]})
    cuts = sorted({0, 8, 120, 136, 168, 184, 192, 200, 312, 328, 376, 384})
    both = jnp.concatenate(
        [
            part_ref[start:stop, :] + added[start] if start in added else part_ref[start:stop, :]
            for start, stop in zip(cuts, cuts[1:])
        ],
        axis=0,
    )
    peak = None
    for level in range(4):
        room_r = ROW_ROOM[level]
        room_c = COL_ROOM[level]
        if level == 1:
            halo = jnp.concatenate([added[start][:, :half] for start, _ in SECOND_ROWS], axis=0)
            both = second_ref[...] + mm3_left(added_ref, second_columns(halo, inner_ref, col_refs[1]))
        elif level:
            both = mm3_left(row_refs[level], mm3(current, col_refs[level]))
        current = both[:room_r, :room_c]
        detail_a = both[:room_r, room_c:]
        detail_b = both[room_r:, :room_c]
        detail_c = both[room_r:, room_c:]
        now = jnp.maximum(jnp.maximum(jnp.abs(detail_a), jnp.abs(detail_b)), jnp.abs(detail_c))
        if peak is not None:
            now = jnp.maximum(now, peak)
        wide = jnp.maximum(now, jnp.maximum(pltpu.roll(now, 1, 1), pltpu.roll(now, room_c - 1, 1)))
        wide = jnp.maximum(wide, jnp.maximum(pltpu.roll(wide, 1, 0), pltpu.roll(wide, room_r - 1, 0)))
        n_r = R_DEV >> (level + 1)
        n_c = C_DEV >> (level + 1)
        leader_refs[level][...] = wide[:n_r, :n_c]
        if level < 3:
            pairs = jnp.maximum(now, pltpu.roll(now, room_c - 1, 1))
            pooled = []
            for across in range(room_c // 128):
                top = across * ROW_ROOM[0]
                peak_ref[top : top + room_r, :] = pairs[:, across * 128 : (across + 1) * 128]
                pooled.append(
                    jnp.maximum(
                        peak_ref[pl.ds(top, room_r // 2, stride=2), :],
                        peak_ref[pl.ds(top + 1, room_r // 2, stride=2), :],
                    )
                )
            high, low = hi_lo(jnp.concatenate(pooled, axis=1) if len(pooled) > 1 else pooled[0])
            room_n = COL_ROOM[level + 1]
            out = iota((room_c, room_n), 1)
            source = 2 * out + jnp.where(out < 3 * room_n // 4, 0, room_c - 2 * room_n)
            pick = (iota((room_c, room_n), 0) == source).astype(bf16)
            peak = mm(high, pick) + mm(low, pick)
    approx_ref[...] = current[: R_DEV >> 4, : C_DEV >> 4]


def all_levels(part, second, below, above, near, inner, added, cols, rows):
    shapes = [(R_DEV >> level, C_DEV >> level) for level in (1, 2, 3, 4, 4)]
    return pl.pallas_call(
        levels_kernel,
        out_shape=tuple(jax.ShapeDtypeStruct(shape, f32) for shape in shapes),
        scratch_shapes=[pltpu.VMEM((3 * ROW_ROOM[0], 128), f32)],
        compiler_params=pltpu.CompilerParams(vmem_limit_bytes=32 << 20),
        name="levels",
    )(part, second, below, above, near, inner, added, *cols, *rows)


def shifted(x, axis, by):
    size = lax.axis_size(axis)
    return lax.ppermute(x, axis, [(i, (i + by) % size) for i in range(size)])


def transform(arrived):
    table = jax.tree.map(jnp.asarray, tables())
    first, last, to_left, to_right, carry = place_edges(arrived)
    from_right = shifted(to_left, "cols", -1)
    from_left = shifted(to_right, "cols", 1)
    inner = place_inner(arrived, carry, first, last, table["inner"])
    own, to_up, to_down = outer_columns(
        inner, first, to_right, from_right, from_left, table["outer"], table["below"]
    )
    above = shifted(to_down, "rows", 1)
    below = shifted(to_up, "rows", -1)
    part, second = own_rows(own, table["own"], table["inner"], table["cols"][0], table["rows"][0])
    return all_levels(
        part, second, below, above, table["above"], table["inner"], table["second"], table["cols"], table["rows"][1:]
    )


def on_device(offsets, lens_weight, counts, owners, brick_slot):
    packed = deposit_and_pack(offsets, lens_weight, counts, owners, brick_slot)
    arrived = lax.all_to_all(
        packed.reshape(N_DEST, MESSAGE // 4, 4, 128), ("rows", "cols"), split_axis=0, concat_axis=0, tiled=True
    )
    return transform(arrived.reshape(N_DEST * MESSAGE, 128))


def solution(mesh):
    placed = (
        P(("rows", "cols"), None, None),
        P(("rows", "cols"), None),
        P(("rows", "cols")),
        P(("rows", "cols")),
        P(("rows", "cols")),
    )
    return jax.shard_map(
        on_device,
        mesh=mesh,
        in_specs=placed,
        out_specs=(P("rows", "cols"),) * 5,
        check_vma=False,
    )
```

```python
import functools

import jax
import jax.numpy as jnp
import numpy as np
from jax import lax
from jax.experimental import pallas as pl
from jax.experimental.pallas import tpu as pltpu
from jax.sharding import PartitionSpec as P

R_DEV = 256
C_DEV = 512
PMAX = 256
CAP = 8
N_DEST = 128
BRICKS = 512
SLOTS = N_DEST * CAP

TILE_ROWS = 272
UP_ROWS = 80
DOWN_ROWS = 24
DOWN_FROM = 240
ROW_ROOM = (192, 96, 48, 24)
COL_ROOM = (384, 256, 128, 128)

taps_low = (
    0.33267055295008263,
    0.8068915093110925,
    0.4598775021184915,
    -0.13501102001025458,
    -0.08544127388202666,
    0.03522629188570953,
)
taps_high = tuple(((-1.0) ** index * taps_low[5 - index] for index in range(6)))

f32 = jnp.float32
bf16 = jnp.bfloat16


def spans(size):
    out = []
    for level in range(1, 5):
        n = size >> level
        before = 8 >> (level - 1)
        after = (36, 16, 6, 1)[level - 1]
        out.append((-before, n + after, -before, n + before))
    return out


def level_table(sources, room, span):
    low_from, low_to, high_from, high_to = span
    table = np.zeros((len(sources), 2 * room), np.float64)
    for position, index in enumerate(sources):
        if index is None:
            continue
        for half, (lo, hi, taps) in enumerate(
            ((low_from, low_to, taps_low), (high_from, high_to, taps_high))
        ):
            for tap in range(6):
                if (index - tap) % 2 == 0:
                    k = (index - tap) // 2
                    if lo <= k < hi:
                        table[position, half * room + (k % room)] += taps[tap]
    return table


def room_sources(room, low_from, low_to):
    out = [None] * room
    for k in range(low_from, low_to):
        out[k % room] = k
    return out


def split(table):
    table = np.asarray(table, np.float32)
    high = table.astype(jnp.bfloat16)
    low = (table - high.astype(np.float32)).astype(jnp.bfloat16)
    return np.stack([high, low])


ABOVE_ROWS = ((0, 8), (184, 192), (192, 200), (376, 384))
BELOW_ROWS = ((120, 136), (312, 328), (136, 168))
SECOND_ROWS = ((0, 8), (120, 136), (136, 168), (184, 192))
UP_MESSAGE = 5 * 16 + 5 * 16 + 3 * 32
DOWN_MESSAGE = 5 * 16 + 8
LEFT_MESSAGE = TILE_ROWS // 2 + 40


@functools.lru_cache(maxsize=1)
def tables():
    col_spans = spans(C_DEV)
    row_spans = spans(R_DEV)
    inner = level_table(list(range(384)), 128, (0, 128, 0, 128))
    right = [C_DEV + j if j < 76 else None for j in range(128)] + [None] * 128
    mixed = [None] * 128 + list(range(8)) + [None] * 104 + [j - 16 for j in range(16)]
    room = COL_ROOM[0]
    beyond = level_table(right, room, (256, 292, 256, 264)) + level_table(mixed, room, (-8, 0, -8, 0))
    partial = level_table(right, room, (254, 256, 254, 256))
    outer = np.concatenate(
        [
            beyond[:, 256:384],
            beyond[:, room + 256 : room + 384],
            partial[:, 128:256],
            partial[:, room + 128 : room + 256],
        ],
        axis=1,
    )
    row_src = [i if i < 257 else None for i in range(TILE_ROWS)]
    row_src += [R_DEV + i if i < 76 else None for i in range(UP_ROWS)]
    row_src += [i - 16 if i < 17 else None for i in range(DOWN_ROWS)]
    third = [256 + j if j < 36 else j - 128 if j >= 120 else None for j in range(128)] + [None] * 128
    room = COL_ROOM[1]
    rest = level_table(third, room, col_spans[1])
    rest += level_table([None] * 128 + list(range(8)) + [None] * 120, room, (-4, 0, -4, 0))
    rest = np.concatenate([rest[:, 128:256], rest[:, room + 128 : room + 256]], axis=1)
    cols, rows = [rest], []
    for level in range(4):
        if level > 1:
            cols.append(level_table(col_src, COL_ROOM[level], col_spans[level]))
        rows.append(level_table(row_src, ROW_ROOM[level], row_spans[level]).T)
        col_src = room_sources(COL_ROOM[level], col_spans[level][0], col_spans[level][1])
        row_src = room_sources(ROW_ROOM[level], row_spans[level][0], row_spans[level][1])
    first = rows[0]
    below = first[:, TILE_ROWS : TILE_ROWS + UP_ROWS]
    above = first[:, TILE_ROWS + UP_ROWS :]
    for part, kept in ((below, BELOW_ROWS), (above, ABOVE_ROWS)):
        far = np.ones(first.shape[0], bool)
        for start, stop in kept:
            far[start:stop] = False
        assert not part[far].any()
    below = np.concatenate([below[start:stop] for start, stop in BELOW_ROWS], axis=0)
    above = np.concatenate([above[start:stop] for start, stop in ABOVE_ROWS], axis=0)
    second = np.concatenate([rows[1][:, start:stop] for start, stop in SECOND_ROWS], axis=1)
    return {
        "second": split(second),
        "inner": split(inner),
        "outer": split(outer),
        "own": split(first[:, :TILE_ROWS]),
        "below": split(below),
        "above": split(above),
        "cols": [split(t) for t in cols],
        "rows": [split(t) for t in rows[1:]],
    }


def hi_lo(x):
    high = x.astype(bf16)
    low = (x - high.astype(f32)).astype(bf16)
    return high, low


def mm(a, b):
    return jnp.dot(a, b, preferred_element_type=f32)


def mm_nt(a, b):
    return lax.dot_general(a, b, (((1,), (1,)), ((), ())), preferred_element_type=f32)


def iota(shape, dim):
    return lax.broadcasted_iota(jnp.int32, shape, dim)


STEPS = 4
STEP_BRICKS = BRICKS // STEPS
MESSAGE = 20


def deposit_kernel(
    off_hbm,
    w_hbm,
    counts_hbm,
    owners_hbm,
    slot_hbm,
    out_ref,
    off_ref,
    w_ref,
    counts_ref,
    owners_ref,
    slot_ref,
    cnt_ref,
    patch_ref,
    edge_ref,
    small_sem,
    off_sem,
    w_sem,
):
    small = [
        pltpu.make_async_copy(src, dst, small_sem.at[n])
        for n, (src, dst) in enumerate(
            ((owners_hbm, owners_ref), (slot_hbm, slot_ref), (counts_hbm, counts_ref))
        )
    ]
    for copy in small:
        copy.start()

    def fetch(index):
        off_rows = pl.ds(index * 4 * STEP_BRICKS, 4 * STEP_BRICKS)
        w_rows = pl.ds(index * STEP_BRICKS, STEP_BRICKS)
        return (
            pltpu.make_async_copy(off_hbm.at[off_rows], off_ref.at[off_rows], off_sem.at[index]),
            pltpu.make_async_copy(w_hbm.at[w_rows], w_ref.at[w_rows], w_sem.at[index]),
        )

    for index in range(STEPS):
        for copy in fetch(index):
            copy.start()
    for copy in small:
        copy.wait()

    owners = owners_ref[...]
    dest = (iota((N_DEST, BRICKS), 0) == owners).astype(f32)
    before = (iota((BRICKS, BRICKS), 0) < iota((BRICKS, BRICKS), 1)).astype(bf16)
    ranks = jnp.sum(mm(dest.astype(bf16), before) * dest, axis=0, keepdims=True)
    position = ranks.astype(jnp.int32) * N_DEST + owners

    slot = slot_ref[...]
    grid_row = slot // 32
    grid_col = slot % 32
    coarse = (grid_col % 8) * 4 + grid_col // 8
    row_id = iota((256, BRICKS), 0)
    spread = jnp.where(
        row_id < 128,
        counts_ref[...],
        jnp.where(row_id == 168, coarse, jnp.where(row_id == 169, grid_row, 0)),
    )
    eye = (iota((BRICKS, BRICKS), 0) == iota((BRICKS, BRICKS), 1)).astype(bf16)
    cnt_ref[...] = mm_nt(eye, spread.astype(f32).astype(bf16))

    lane = iota((8, 128), 1)
    sub = iota((8, 128), 0)
    particle = iota((8, PMAX), 1).astype(f32)
    cell = iota((16, PMAX), 0).astype(f32)

    zero = jnp.zeros((), bf16)
    bit = {at: (lane >> at) % 2 == 1 for at in (3, 4, 5, 6)}

    def choose(tiles, mask):
        return [jnp.where(mask, odd, even) for even, odd in zip(tiles[0::2], tiles[1::2])]

    def one_group(start):
        first = start * 4
        rows_at = jnp.concatenate([off_ref[pl.ds(first + 2 * half, 8, stride=4), :] for half in range(2)], axis=1)
        cols_at = jnp.concatenate([off_ref[pl.ds(first + 2 * half + 1, 8, stride=4), :] for half in range(2)], axis=1)
        count = cnt_ref[pl.ds(start, 8), 0:128]
        count = jnp.concatenate([count, count], axis=1)
        weight = jnp.where(particle < count, w_ref[pl.ds(start, 8), :], 0.0)
        lag = rows_at * weight
        left = []
        for i in range(17):
            left.append(weight - jnp.abs(lag))
            lag = lag - weight
        left = jnp.maximum(jnp.concatenate(left, axis=0).astype(bf16), zero)
        right = []
        for g in range(8):
            at = first + 4 * ((8 - g) % 8) + 1
            column = jnp.concatenate([off_ref[pl.ds(at + 2 * half, 8, stride=0), :] for half in range(2)], axis=1)
            right += [1.0 - jnp.abs(column - cell[0:8]), 1.0 - jnp.abs(column - cell[8:16])]
        last = cols_at - 15.0
        right = [jnp.maximum(jnp.concatenate(right, axis=0).astype(bf16), zero)]
        right += [jnp.maximum(jnp.concatenate([last, last], axis=0).astype(bf16), zero)] * 8
        full = mm_nt(left, jnp.concatenate(right, axis=0))
        halves = []
        for half in range(2):
            pairs = []
            for pair in range(4):
                at = (half * 8 + pair * 2) * 8
                even = pltpu.roll(full[at : at + 8, 0:128], 0, 1, stride=16, stride_axis=0)
                odd = pltpu.roll(full[at + 8 : at + 16, 0:128], 16, 1, stride=16, stride_axis=0)
                both = jnp.where(bit[4], odd, even)
                pairs.append(pltpu.roll(both, 32 * pair, 1) if pair else both)
            halves.append(choose(choose(pairs, bit[5]), bit[6])[0])
        bottom = pltpu.roll(full[128:136, 0:128], 0, 1, stride=16, stride_axis=0)
        corner = jnp.sum(jnp.where(lane == sub, full[128:136, 128:256], 0.0), axis=1, keepdims=True)
        third = jnp.where(lane < 16, bottom, jnp.where(lane == 32, corner, 0.0))
        edge = [full[8 * i : 8 * i + 8, 128:256] for i in range(16)]
        for at in range(3, 7):
            edge = choose(edge, bit[at])
        edge = jnp.where(lane % 8 == sub, edge[0], 0.0)
        patch_ref[pl.ds(start, 8), 0:128] = halves[0]
        patch_ref[pl.ds(start, 8), 128:256] = halves[1]
        patch_ref[pl.ds(start, 8), 256:384] = third + cnt_ref[pl.ds(start, 8), 128:256]
        edge_ref[pl.ds(start, 8), :] = edge

    for index in range(STEPS):
        for copy in fetch(index):
            copy.wait()
    for group in range(BRICKS // 8):
        one_group(group * 8)

    gather = (iota((128, 128), 1) == iota((128, 128), 0) // 8 + 16).astype(bf16)
    edge_high, edge_low = hi_lo(edge_ref[...])
    third = patch_ref[:, 256:384] + (mm(edge_high, gather) + mm(edge_low, gather))

    high, low = hi_lo(patch_ref[:, 0:256])
    ends = jnp.concatenate(hi_lo(third), axis=1)
    lane_wide = iota((N_DEST, 128), 1)
    for pair in range(4):
        edges = []
        for rank in (2 * pair, 2 * pair + 1):
            pick = (iota((N_DEST, BRICKS), 0) + rank * N_DEST == position).astype(bf16)
            inner = mm(pick, high) + mm(pick, low)
            out_ref[pl.ds(rank, N_DEST, stride=MESSAGE), :] = inner[:, 0:128]
            out_ref[pl.ds(8 + rank, N_DEST, stride=MESSAGE), :] = inner[:, 128:256]
            both = mm(pick, ends)
            edges.append(both[:, 0:128] + both[:, 128:256])
        joined = jnp.where(lane_wide < 64, edges[0], pltpu.roll(edges[1], 64, 1))
        out_ref[pl.ds(16 + pair, N_DEST, stride=MESSAGE), :] = joined


def deposit_and_pack(offsets, weights, counts, owners, slots):
    flat = offsets.reshape(BRICKS, 2, 2, 128).transpose(0, 2, 1, 3).reshape(4 * BRICKS, 128)
    return pl.pallas_call(
        deposit_kernel,
        out_shape=jax.ShapeDtypeStruct((N_DEST * MESSAGE, 128), f32),
        in_specs=[pl.BlockSpec(memory_space=pltpu.MemorySpace.HBM)] * 5,
        scratch_shapes=[
            pltpu.VMEM((4 * BRICKS, 128), f32),
            pltpu.VMEM((BRICKS, PMAX), f32),
            pltpu.VMEM((1, BRICKS), jnp.int32),
            pltpu.VMEM((1, BRICKS), jnp.int32),
            pltpu.VMEM((1, BRICKS), jnp.int32),
            pltpu.VMEM((BRICKS, 256), f32),
            pltpu.VMEM((BRICKS, 384), f32),
            pltpu.VMEM((BRICKS, 128), f32),
            pltpu.SemaphoreType.DMA((3,)),
            pltpu.SemaphoreType.DMA((STEPS,)),
            pltpu.SemaphoreType.DMA((STEPS,)),
        ],
        compiler_params=pltpu.CompilerParams(vmem_limit_bytes=40 << 20),
        name="deposit",
    )(*(pltpu.with_memory_space_constraint(x, pltpu.MemorySpace.HBM) for x in (
        flat,
        weights,
        counts.reshape(1, BRICKS),
        owners.reshape(1, BRICKS),
        slots.reshape(1, BRICKS),
    )))


def mm3(data, table):
    high, low = hi_lo(data)
    return mm(high, table[0]) + (mm(low, table[0]) + mm(high, table[1]))


def mm3_left(table, data):
    high, low = hi_lo(data)
    return mm(table[0], high) + (mm(table[0], low) + mm(table[1], high))


def block_slots(block):
    row = iota((128, SLOTS), 0)
    return (row // 16) * 64 + row % 16 + block * 16


def edge_slots():
    row = iota((128, SLOTS), 0)
    return (row // 16) * 64 + row % 16 + jnp.where(row < 80, 0, 64 + 48)


def place(x_ref, grid_ref, picks):
    lane8 = iota((8, 128), 1)
    upper = jnp.concatenate([x_ref[pl.ds(rank, N_DEST, stride=MESSAGE), :] for rank in range(8)], axis=0)
    lower = jnp.concatenate([x_ref[pl.ds(8 + rank, N_DEST, stride=MESSAGE), :] for rank in range(8)], axis=0)
    ends = []
    for pair in range(4):
        joined = x_ref[pl.ds(16 + pair, N_DEST, stride=MESSAGE), :]
        ends += [joined, pltpu.roll(joined, 64, 1)]
    ends_high, ends_low = hi_lo(jnp.concatenate(ends, axis=0))
    weigh = jnp.where(lane8 == 40, 16.0, jnp.where(lane8 == 41, 1.0, 0.0)).astype(bf16)
    slot = mm_nt(weigh, ends_high)[0:1, :].astype(jnp.int32)
    high, low = hi_lo(jnp.concatenate([upper, lower], axis=1))
    ends = jnp.concatenate([ends_high, ends_low], axis=1)
    for at, slots in enumerate(picks):
        rows = slice(at * 128, (at + 1) * 128)
        pick = (slots == slot).astype(bf16)
        grid_ref[rows, 0:256] = mm(pick, high) + mm(pick, low)
        both = mm(pick, ends)
        grid_ref[rows, 256:384] = both[:, 0:128] + both[:, 128:256]


def swap_groups(tiles):
    group = iota((8, 128), 1) // 16
    for d in (1, 2, 4):
        mask = (group // d) % 2 == 0
        new = list(tiles)
        for a in range(8):
            if (a // d) % 2 == 0:
                one, two = tiles[a], tiles[a + d]
                new[a] = jnp.where(mask, one, pltpu.roll(two, 16 * d, 1))
                new[a + d] = jnp.where(mask, pltpu.roll(one, 128 - 16 * d, 1), two)
        tiles = new
    return tiles


def turn(side, corner):
    turned = [[pltpu.roll(side[half], 16 - i, 1) for half in range(2)] for i in range(16)]
    return turned + [[pltpu.roll(corner[half], 16, 1) for half in range(2)]]


def unpack_block(grid_ref, starts):
    rows = [[None, None] for _ in range(17)]
    side, corner = [None, None], [None, None]
    none = jnp.zeros((8, 128), f32)
    for half in range(2):
        parts = []
        for third in range(3):
            lanes = slice(third * 128, (third + 1) * 128)
            parts.append(
                swap_groups(
                    [none if at is None else grid_ref[at + half * 8 : at + half * 8 + 8, lanes] for at in starts]
                )
            )
        for i in range(8):
            rows[i][half] = parts[0][i]
            rows[8 + i][half] = parts[1][i]
        rows[16][half] = parts[2][0]
        side[half] = parts[2][1]
        corner[half] = parts[2][2]
    return rows, side, corner


def add_spills(rows, turned, previous):
    lane8 = iota((8, 128), 1)
    out = []
    for i in range(17):
        pair = []
        for half in range(2):
            spill = jnp.where(lane8 % 16 == 0, turned[i][half], 0.0)
            first = 0.0 if previous is None else previous[i][half]
            pair.append(rows[i][half] + jnp.where(lane8 == 0, first, spill))
        out.append(pair)
    return out


def store_block(rows, ref):
    sub = iota((8, 128), 0)
    down = [pltpu.roll(rows[16][half], 1, 0) for half in range(2)]
    for i in range(16):
        low, high = rows[i]
        if i == 0:
            low = low + jnp.where(sub == 0, 0.0, down[0])
            high = high + jnp.where(sub == 0, down[0], down[1])
        ref[pl.ds(i, 8, stride=16), :] = low
        ref[pl.ds(128 + i, 8, stride=16), :] = high
    ref[256:264, :] = jnp.where(sub == 0, down[1], 0.0)
    ref[264:TILE_ROWS, :] = jnp.zeros((8, 128), f32)


def place_edges_kernel(x_ref, first_ref, left_ref, right_ref, grid_ref, side_ref):
    place(x_ref, grid_ref, [edge_slots()])
    lane8 = iota((8, 128), 1)
    rows, side, corner = unpack_block(grid_ref, [0, 16, 32, 48, 64, None, None, None])
    store_block(add_spills(rows, turn(side, corner), None), first_ref)
    rows, side, corner = unpack_block(grid_ref, [None] * 6 + [80, 96])
    turned = turn(side, corner)
    rows = add_spills(rows, turned, None)
    store_block(
        [[jnp.where(lane8 == 0, turned[i][half], rows[i][half]) for half in range(2)] for i in range(17)], side_ref
    )
    right = [jnp.zeros((8, 128), f32)] * 5
    left = [jnp.zeros((8, 128), f32)] * 5
    for tile in range(33):
        group, at = divmod(tile, 5)
        rows8 = slice(tile * 8, tile * 8 + 8)
        both = side_ref[rows8, :]
        moved = jnp.where(lane8 == 112 + group, pltpu.roll(both, 112 + group, 1), right[at])
        right[at] = jnp.where(lane8 // 16 == group, pltpu.roll(both, 16 * group + 16, 1), moved)
        turned64 = pltpu.roll(first_ref[rows8, :], (64 + 16 * group) % 128, 1) if group != 4 else first_ref[rows8, :]
        left[at] = jnp.where(lane8 // 16 == group, turned64, left[at])
    for at in range(5):
        right_ref[at * 8 : at * 8 + 8, :] = right[at]
        left_ref[136 + at * 8 : 144 + at * 8, :] = left[at]
    lane = iota((136, 128), 1)
    left_ref[0:136, :] = jnp.where(lane < 64, first_ref[0:136, :], pltpu.roll(first_ref[136:272, :], 64, 1))


def place_edges(arrived):
    tile = jax.ShapeDtypeStruct((TILE_ROWS, 128), f32)
    return pl.pallas_call(
        place_edges_kernel,
        out_shape=(
            tile,
            jax.ShapeDtypeStruct((LEFT_MESSAGE, 128), f32),
            jax.ShapeDtypeStruct((40, 128), f32),
        ),
        scratch_shapes=[pltpu.VMEM((128, 384), f32), pltpu.VMEM((TILE_ROWS, 128), f32)],
        compiler_params=pltpu.CompilerParams(vmem_limit_bytes=32 << 20),
        cost_estimate=pl.CostEstimate(flops=600_000_000, bytes_accessed=2_000_000, transcendentals=0),
        name="place_edges",
    )(arrived)


def place_inner_kernel(x_ref, inner_ref, own_ref, grid_ref, *tile_refs):
    place(x_ref, grid_ref, [block_slots(block) for block in range(4)])
    previous = None
    for block, ref in enumerate(tile_refs):
        rows, side, corner = unpack_block(grid_ref, [block * 128 + col * 16 for col in range(8)])
        turned = turn(side, corner)
        store_block(add_spills(rows, turned, previous), ref)
        previous = turned
    own_ref[:, 0:256] = mm3(jnp.concatenate([ref[...] for ref in tile_refs[0:3]], axis=1), inner_ref)
    own_ref[:, 256:512] = mm3(jnp.concatenate([ref[...] for ref in tile_refs[2:4]], axis=1), inner_ref[:, 0:256, :])


def place_inner(arrived, inner):
    return pl.pallas_call(
        place_inner_kernel,
        out_shape=jax.ShapeDtypeStruct((TILE_ROWS, 512), f32),
        scratch_shapes=[pltpu.VMEM((BRICKS, 384), f32)] + [pltpu.VMEM((TILE_ROWS, 128), f32)] * 4,
        compiler_params=pltpu.CompilerParams(vmem_limit_bytes=32 << 20),
        cost_estimate=pl.CostEstimate(flops=1_600_000_000, bytes_accessed=3_000_000, transcendentals=0),
        name="place_inner",
    )(arrived, inner)


def pack_tiles(tiles):
    lane = iota(tiles[0].shape, 1)
    shared = jnp.where((lane >= 56) & (lane < 72), pltpu.roll(tiles[5], 64, 1), tiles[2])
    return [tiles[0], tiles[1], shared, tiles[3], tiles[4]]


def unpack_tiles(tiles):
    return jnp.concatenate([*tiles, pltpu.roll(tiles[2], 64, 1)], axis=1)


def columns_kernel(
    own_ref, first_ref, to_right_ref, from_right_ref, from_left_ref, outer_ref, below_ref, out_ref, up_ref, down_ref
):
    lane8 = iota((8, 128), 1)
    none = jnp.zeros((8, 128), f32)
    spills, rows = [], []
    for tile in range(TILE_ROWS // 8):
        group, at = divmod(tile, 5)
        own = first_ref[tile * 8 : tile * 8 + 8, :]
        if tile == 33:
            spills.append(none)
            rows.append(jnp.concatenate([none, jnp.where(lane8 < 8, own, 0.0)], axis=1))
            continue
        packed = from_left_ref[at * 8 : at * 8 + 8, :]
        spill = jnp.where(lane8 == 0, pltpu.roll(packed, 16 - group, 1), 0.0)
        near = pltpu.roll(packed, 112 - 16 * group, 1)
        spills.append(spill)
        mixed = jnp.where(lane8 < 8, own + spill, jnp.where(lane8 >= 112, near, 0.0))
        wide = from_right_ref[(tile % 17) * 8 : (tile % 17) * 8 + 8, :]
        if tile >= 17:
            wide = pltpu.roll(wide, 64, 1)
        rest = from_right_ref[136 + at * 8 : 144 + at * 8, :]
        if group != 4:
            rest = pltpu.roll(rest, (64 - 16 * group) % 128, 1)
        over = jnp.where(lane8 == 0, pltpu.roll(to_right_ref[at * 8 : at * 8 + 8, :], 16 - group, 1), 0.0)
        right = jnp.where(lane8 < 64, wide, jnp.where(lane8 < 80, rest, 0.0)) + over
        rows.append(jnp.concatenate([right, mixed], axis=1))
    spill = jnp.concatenate(spills, axis=0)
    outer = mm3(jnp.concatenate(rows, axis=0), outer_ref)
    pieces = [
        own_ref[:, 0:128] + taps_low[0] * spill,
        own_ref[:, 256:384] + outer[:, 256:384],
        outer[:, 0:128],
        own_ref[:, 128:256] + taps_high[0] * spill,
        own_ref[:, 384:512] + outer[:, 384:512],
        outer[:, 128:256],
    ]
    low = mm3_left(below_ref, jnp.concatenate([piece[0:UP_ROWS] for piece in pieces[0:3]], axis=1))
    high = mm3_left(below_ref[:, 0:32, :], jnp.concatenate([piece[0:UP_ROWS] for piece in pieces[3:6]], axis=1))
    for part in range(2):
        rows16 = slice(part * 16, part * 16 + 16)
        fives = pack_tiles([half[rows16, at * 128 : (at + 1) * 128] for half in (low, high) for at in range(3)])
        for at, tile in enumerate(fives):
            up_ref[part * 80 + at * 16 : part * 80 + at * 16 + 16, :] = tile
    for at in range(3):
        up_ref[160 + at * 32 : 192 + at * 32, :] = low[32:64, at * 128 : (at + 1) * 128]
    for at, tile in enumerate(pack_tiles([piece[DOWN_FROM : DOWN_FROM + 24] for piece in pieces])):
        down_ref[at * 16 : at * 16 + 16, :] = tile[0:16]
        down_ref[80 + at : 81 + at, :] = tile[16:17]
    down_ref[85:88, :] = jnp.zeros((3, 128), f32)
    for at, piece in enumerate(pieces):
        out_ref[:, at * 128 : (at + 1) * 128] = piece


def outer_columns(own, first, to_right, from_right, from_left, outer, below):
    width = 2 * COL_ROOM[0]
    return pl.pallas_call(
        columns_kernel,
        out_shape=(
            jax.ShapeDtypeStruct((TILE_ROWS, width), f32),
            jax.ShapeDtypeStruct((UP_MESSAGE, 128), f32),
            jax.ShapeDtypeStruct((DOWN_MESSAGE, 128), f32),
        ),
        compiler_params=pltpu.CompilerParams(vmem_limit_bytes=32 << 20),
        cost_estimate=pl.CostEstimate(flops=220_000_000, bytes_accessed=2_000_000, transcendentals=0),
        name="columns",
    )(own, first, to_right, from_right, from_left, outer, below)


def second_columns(current, inner, rest):
    main = mm3(current, inner)
    rest = mm3(jnp.concatenate([current[:, 256:384], current[:, 0:128]], axis=1), rest)
    return jnp.concatenate([main[:, 0:128], rest[:, 0:128], main[:, 128:256], rest[:, 128:256]], axis=1)


def own_rows_kernel(own_ref, table_ref, inner_ref, rest_ref, rows_ref, out_ref, second_ref):
    for at in range(3):
        cols = slice(at * 256, (at + 1) * 256)
        out_ref[:, cols] = mm3_left(table_ref, own_ref[:, cols])
    current = out_ref[0 : ROW_ROOM[0], 0 : COL_ROOM[0]]
    second_ref[...] = mm3_left(rows_ref, second_columns(current, inner_ref, rest_ref))


def own_rows(own, table, inner, rest, rows):
    return pl.pallas_call(
        own_rows_kernel,
        out_shape=(
            jax.ShapeDtypeStruct((2 * ROW_ROOM[0], 2 * COL_ROOM[0]), f32),
            jax.ShapeDtypeStruct((2 * ROW_ROOM[1], 2 * COL_ROOM[1]), f32),
        ),
        compiler_params=pltpu.CompilerParams(vmem_limit_bytes=32 << 20),
        cost_estimate=pl.CostEstimate(flops=4_800_000_000, bytes_accessed=20_000_000, transcendentals=0),
        name="own_rows",
    )(own, table, inner, rest, rows)


def levels_kernel(part_ref, second_ref, below_ref, above_ref, table_ref, inner_ref, added_ref, *refs):
    col_refs = (None,) + refs[0:3]
    row_refs = (None, None) + refs[3:5]
    leader_refs = refs[5:9]
    approx_ref = refs[9]
    peak_ref = refs[10]
    sub = iota((8, 128), 0)
    above = [
        jnp.concatenate(
            [
                above_ref[at * 16 : at * 16 + 16, :],
                jnp.where(sub == 0, above_ref[80 + at : 81 + at, :], 0.0),
            ],
            axis=0,
        )
        for at in range(5)
    ]
    near = mm3_left(table_ref, unpack_tiles(above))
    half = COL_ROOM[0]
    sixes = [
        unpack_tiles([below_ref[part * 80 + at * 16 : part * 80 + at * 16 + 16, :] for at in range(5)])
        for part in range(2)
    ]
    threes = jnp.concatenate([below_ref[160 + at * 32 : 192 + at * 32, :] for at in range(3)], axis=1)
    threes = jnp.concatenate([threes, jnp.zeros((32, half), f32)], axis=1)
    added = {0: near[0:8], 184: near[8:16], 192: near[16:24], 376: near[24:32]}
    added.update({120: sixes[0], 136: threes, 312: sixes[1]})
    cuts = sorted({0, 8, 120, 136, 168, 184, 192, 200, 312, 328, 376, 384})
    both = jnp.concatenate(
        [
            part_ref[start:stop, :] + added[start] if start in added else part_ref[start:stop, :]
            for start, stop in zip(cuts, cuts[1:])
        ],
        axis=0,
    )
    peak = None
    for level in range(4):
        room_r = ROW_ROOM[level]
        room_c = COL_ROOM[level]
        if level == 1:
            halo = jnp.concatenate([added[start][:, :half] for start, _ in SECOND_ROWS], axis=0)
            both = second_ref[...] + mm3_left(added_ref, second_columns(halo, inner_ref, col_refs[1]))
        elif level:
            both = mm3_left(row_refs[level], mm3(current, col_refs[level]))
        current = both[:room_r, :room_c]
        detail_a = both[:room_r, room_c:]
        detail_b = both[room_r:, :room_c]
        detail_c = both[room_r:, room_c:]
        now = jnp.maximum(jnp.maximum(jnp.abs(detail_a), jnp.abs(detail_b)), jnp.abs(detail_c))
        if peak is not None:
            now = jnp.maximum(now, peak)
        wide = jnp.maximum(now, jnp.maximum(pltpu.roll(now, 1, 1), pltpu.roll(now, room_c - 1, 1)))
        wide = jnp.maximum(wide, jnp.maximum(pltpu.roll(wide, 1, 0), pltpu.roll(wide, room_r - 1, 0)))
        n_r = R_DEV >> (level + 1)
        n_c = C_DEV >> (level + 1)
        leader_refs[level][...] = wide[:n_r, :n_c]
        if level < 3:
            pairs = jnp.maximum(now, pltpu.roll(now, room_c - 1, 1))
            pooled = []
            for across in range(room_c // 128):
                top = across * ROW_ROOM[0]
                peak_ref[top : top + room_r, :] = pairs[:, across * 128 : (across + 1) * 128]
                pooled.append(
                    jnp.maximum(
                        peak_ref[pl.ds(top, room_r // 2, stride=2), :],
                        peak_ref[pl.ds(top + 1, room_r // 2, stride=2), :],
                    )
                )
            high, low = hi_lo(jnp.concatenate(pooled, axis=1) if len(pooled) > 1 else pooled[0])
            room_n = COL_ROOM[level + 1]
            out = iota((room_c, room_n), 1)
            source = 2 * out + jnp.where(out < 3 * room_n // 4, 0, room_c - 2 * room_n)
            pick = (iota((room_c, room_n), 0) == source).astype(bf16)
            peak = mm(high, pick) + mm(low, pick)
    approx_ref[...] = current[: R_DEV >> 4, : C_DEV >> 4]


def all_levels(part, second, below, above, near, inner, added, cols, rows):
    shapes = [(R_DEV >> level, C_DEV >> level) for level in (1, 2, 3, 4, 4)]
    return pl.pallas_call(
        levels_kernel,
        out_shape=tuple(jax.ShapeDtypeStruct(shape, f32) for shape in shapes),
        scratch_shapes=[pltpu.VMEM((3 * ROW_ROOM[0], 128), f32)],
        compiler_params=pltpu.CompilerParams(vmem_limit_bytes=32 << 20),
        name="levels",
    )(part, second, below, above, near, inner, added, *cols, *rows)


def shifted(x, axis, by):
    size = lax.axis_size(axis)
    return lax.ppermute(x, axis, [(i, (i + by) % size) for i in range(size)])


def transform(arrived):
    table = jax.tree.map(jnp.asarray, tables())
    first, to_left, to_right = place_edges(arrived)
    from_right = shifted(to_left, "cols", -1)
    from_left = shifted(to_right, "cols", 1)
    inner = place_inner(arrived, table["inner"])
    own, to_up, to_down = outer_columns(
        inner, first, to_right, from_right, from_left, table["outer"], table["below"]
    )
    above = shifted(to_down, "rows", 1)
    below = shifted(to_up, "rows", -1)
    part, second = own_rows(own, table["own"], table["inner"], table["cols"][0], table["rows"][0])
    return all_levels(
        part, second, below, above, table["above"], table["inner"], table["second"], table["cols"], table["rows"][1:]
    )


def on_device(offsets, lens_weight, counts, owners, brick_slot):
    packed = deposit_and_pack(offsets, lens_weight, counts, owners, brick_slot)
    arrived = lax.all_to_all(
        packed.reshape(N_DEST, MESSAGE // 4, 4, 128), ("rows", "cols"), split_axis=0, concat_axis=0, tiled=True
    )
    return transform(arrived.reshape(N_DEST * MESSAGE, 128))


def solution(mesh):
    placed = (
        P(("rows", "cols"), None, None),
        P(("rows", "cols"), None),
        P(("rows", "cols")),
        P(("rows", "cols")),
        P(("rows", "cols")),
    )
    return jax.shard_map(
        on_device,
        mesh=mesh,
        in_specs=placed,
        out_specs=(P("rows", "cols"),) * 5,
        check_vma=False,
    )
```

```python
import functools

import jax
import jax.numpy as jnp
import numpy as np
from jax import lax
from jax.experimental import pallas as pl
from jax.experimental.pallas import tpu as pltpu
from jax.sharding import PartitionSpec as P

R_DEV = 256
C_DEV = 512
PMAX = 256
CAP = 8
N_DEST = 128
BRICKS = 512
SLOTS = N_DEST * CAP

TILE_ROWS = 272
UP_ROWS = 80
DOWN_ROWS = 24
DOWN_FROM = 240
ROW_ROOM = (192, 96, 48, 24)
COL_ROOM = (384, 256, 128, 128)

taps_low = (
    0.33267055295008263,
    0.8068915093110925,
    0.4598775021184915,
    -0.13501102001025458,
    -0.08544127388202666,
    0.03522629188570953,
)
taps_high = tuple(((-1.0) ** index * taps_low[5 - index] for index in range(6)))

f32 = jnp.float32
bf16 = jnp.bfloat16


def spans(size):
    out = []
    for level in range(1, 5):
        n = size >> level
        before = 8 >> (level - 1)
        after = (36, 16, 6, 1)[level - 1]
        out.append((-before, n + after, -before, n + before))
    return out


def level_table(sources, room, span):
    low_from, low_to, high_from, high_to = span
    table = np.zeros((len(sources), 2 * room), np.float64)
    for position, index in enumerate(sources):
        if index is None:
            continue
        for half, (lo, hi, taps) in enumerate(
            ((low_from, low_to, taps_low), (high_from, high_to, taps_high))
        ):
            for tap in range(6):
                if (index - tap) % 2 == 0:
                    k = (index - tap) // 2
                    if lo <= k < hi:
                        table[position, half * room + (k % room)] += taps[tap]
    return table


def room_sources(room, low_from, low_to):
    out = [None] * room
    for k in range(low_from, low_to):
        out[k % room] = k
    return out


def split(table):
    table = np.asarray(table, np.float32)
    high = table.astype(jnp.bfloat16)
    low = (table - high.astype(np.float32)).astype(jnp.bfloat16)
    return np.stack([high, low])


ABOVE_ROWS = ((0, 8), (184, 192), (192, 200), (376, 384))
BELOW_ROWS = ((120, 136), (312, 328), (136, 168))
SECOND_ROWS = ((0, 8), (120, 136), (136, 168), (184, 192))
UP_MESSAGE = 5 * 16 + 5 * 16 + 3 * 32
DOWN_MESSAGE = 5 * 16 + 8
LEFT_MESSAGE = TILE_ROWS // 2 + 40


@functools.lru_cache(maxsize=1)
def tables():
    col_spans = spans(C_DEV)
    row_spans = spans(R_DEV)
    inner = level_table(list(range(384)), 128, (0, 128, 0, 128))
    right = [C_DEV + j if j < 76 else None for j in range(128)] + [None] * 128
    mixed = [None] * 128 + list(range(8)) + [None] * 104 + [j - 16 for j in range(16)]
    room = COL_ROOM[0]
    beyond = level_table(right, room, (256, 292, 256, 264)) + level_table(mixed, room, (-8, 0, -8, 0))
    partial = level_table(right, room, (254, 256, 254, 256))
    outer = np.concatenate(
        [
            beyond[:, 256:384],
            beyond[:, room + 256 : room + 384],
            partial[:, 128:256],
            partial[:, room + 128 : room + 256],
        ],
        axis=1,
    )
    row_src = [i if i < 257 else None for i in range(TILE_ROWS)]
    row_src += [R_DEV + i if i < 76 else None for i in range(UP_ROWS)]
    row_src += [i - 16 if i < 17 else None for i in range(DOWN_ROWS)]
    third = [256 + j if j < 36 else j - 128 if j >= 120 else None for j in range(128)] + [None] * 128
    room = COL_ROOM[1]
    rest = level_table(third, room, col_spans[1])
    rest += level_table([None] * 128 + list(range(8)) + [None] * 120, room, (-4, 0, -4, 0))
    rest = np.concatenate([rest[:, 128:256], rest[:, room + 128 : room + 256]], axis=1)
    cols, rows = [rest], []
    for level in range(4):
        if level > 1:
            cols.append(level_table(col_src, COL_ROOM[level], col_spans[level]))
        rows.append(level_table(row_src, ROW_ROOM[level], row_spans[level]).T)
        col_src = room_sources(COL_ROOM[level], col_spans[level][0], col_spans[level][1])
        row_src = room_sources(ROW_ROOM[level], row_spans[level][0], row_spans[level][1])
    first = rows[0]
    below = first[:, TILE_ROWS : TILE_ROWS + UP_ROWS]
    above = first[:, TILE_ROWS + UP_ROWS :]
    for part, kept in ((below, BELOW_ROWS), (above, ABOVE_ROWS)):
        far = np.ones(first.shape[0], bool)
        for start, stop in kept:
            far[start:stop] = False
        assert not part[far].any()
    below = np.concatenate([below[start:stop] for start, stop in BELOW_ROWS], axis=0)
    above = np.concatenate([above[start:stop] for start, stop in ABOVE_ROWS], axis=0)
    second = np.concatenate([rows[1][:, start:stop] for start, stop in SECOND_ROWS], axis=1)
    return {
        "second": split(second),
        "inner": split(inner),
        "outer": split(outer),
        "own": split(first[:, :TILE_ROWS]),
        "below": split(below),
        "above": split(above),
        "cols": [split(t) for t in cols],
        "rows": [split(t) for t in rows[1:]],
    }


def hi_lo(x):
    high = x.astype(bf16)
    low = (x - high.astype(f32)).astype(bf16)
    return high, low


def mm(a, b):
    return jnp.dot(a, b, preferred_element_type=f32)


def mm_nt(a, b):
    return lax.dot_general(a, b, (((1,), (1,)), ((), ())), preferred_element_type=f32)


def iota(shape, dim):
    return lax.broadcasted_iota(jnp.int32, shape, dim)


STEPS = 4
STEP_BRICKS = BRICKS // STEPS
MESSAGE = 20


def deposit_kernel(
    off_hbm,
    w_hbm,
    counts_hbm,
    owners_hbm,
    slot_hbm,
    out_ref,
    off_ref,
    w_ref,
    counts_ref,
    owners_ref,
    slot_ref,
    cnt_ref,
    patch_ref,
    edge_ref,
    small_sem,
    off_sem,
    w_sem,
):
    small = [
        pltpu.make_async_copy(src, dst, small_sem.at[n])
        for n, (src, dst) in enumerate(
            ((owners_hbm, owners_ref), (slot_hbm, slot_ref), (counts_hbm, counts_ref))
        )
    ]
    for copy in small:
        copy.start()

    def fetch(index):
        off_rows = pl.ds(index * 4 * STEP_BRICKS, 4 * STEP_BRICKS)
        w_rows = pl.ds(index * STEP_BRICKS, STEP_BRICKS)
        return (
            pltpu.make_async_copy(off_hbm.at[off_rows], off_ref.at[off_rows], off_sem.at[index]),
            pltpu.make_async_copy(w_hbm.at[w_rows], w_ref.at[w_rows], w_sem.at[index]),
        )

    for index in range(STEPS):
        for copy in fetch(index):
            copy.start()
    for copy in small:
        copy.wait()

    owners = owners_ref[...]
    dest = (iota((N_DEST, BRICKS), 0) == owners).astype(f32)
    before = (iota((BRICKS, BRICKS), 0) < iota((BRICKS, BRICKS), 1)).astype(bf16)
    ranks = jnp.sum(mm(dest.astype(bf16), before) * dest, axis=0, keepdims=True)
    position = ranks.astype(jnp.int32) * N_DEST + owners

    slot = slot_ref[...]
    grid_row = slot // 32
    grid_col = slot % 32
    coarse = (grid_col % 8) * 4 + grid_col // 8
    row_id = iota((256, BRICKS), 0)
    spread = jnp.where(
        row_id < 128,
        counts_ref[...],
        jnp.where(row_id == 168, coarse, jnp.where(row_id == 169, grid_row, 0)),
    )
    eye = (iota((BRICKS, BRICKS), 0) == iota((BRICKS, BRICKS), 1)).astype(bf16)
    cnt_ref[...] = mm_nt(eye, spread.astype(f32).astype(bf16))

    lane = iota((8, 128), 1)
    sub = iota((8, 128), 0)
    particle = iota((8, PMAX), 1).astype(f32)
    cell = iota((16, PMAX), 0).astype(f32)

    zero = jnp.zeros((), bf16)
    bit = {at: (lane >> at) % 2 == 1 for at in (3, 4, 5, 6)}

    def choose(tiles, mask):
        return [jnp.where(mask, odd, even) for even, odd in zip(tiles[0::2], tiles[1::2])]

    def one_group(start):
        first = start * 4
        rows_at = jnp.concatenate([off_ref[pl.ds(first + 2 * half, 8, stride=4), :] for half in range(2)], axis=1)
        cols_at = jnp.concatenate([off_ref[pl.ds(first + 2 * half + 1, 8, stride=4), :] for half in range(2)], axis=1)
        count = cnt_ref[pl.ds(start, 8), 0:128]
        count = jnp.concatenate([count, count], axis=1)
        weight = jnp.where(particle < count, w_ref[pl.ds(start, 8), :], 0.0)
        lag = rows_at * weight
        left = []
        for i in range(17):
            left.append(weight - jnp.abs(lag))
            lag = lag - weight
        left = jnp.maximum(jnp.concatenate(left, axis=0).astype(bf16), zero)
        right = []
        for g in range(8):
            at = first + 4 * ((8 - g) % 8) + 1
            column = jnp.concatenate([off_ref[pl.ds(at + 2 * half, 8, stride=0), :] for half in range(2)], axis=1)
            right += [1.0 - jnp.abs(column - cell[0:8]), 1.0 - jnp.abs(column - cell[8:16])]
        last = cols_at - 15.0
        right = [jnp.maximum(jnp.concatenate(right, axis=0).astype(bf16), zero)]
        right += [jnp.maximum(jnp.concatenate([last, last], axis=0).astype(bf16), zero)] * 8
        full = mm_nt(left, jnp.concatenate(right, axis=0))
        halves = []
        for half in range(2):
            pairs = []
            for pair in range(4):
                at = (half * 8 + pair * 2) * 8
                even = pltpu.roll(full[at : at + 8, 0:128], 0, 1, stride=16, stride_axis=0)
                odd = pltpu.roll(full[at + 8 : at + 16, 0:128], 16, 1, stride=16, stride_axis=0)
                both = jnp.where(bit[4], odd, even)
                pairs.append(pltpu.roll(both, 32 * pair, 1) if pair else both)
            halves.append(choose(choose(pairs, bit[5]), bit[6])[0])
        bottom = pltpu.roll(full[128:136, 0:128], 0, 1, stride=16, stride_axis=0)
        corner = jnp.sum(jnp.where(lane == sub, full[128:136, 128:256], 0.0), axis=1, keepdims=True)
        third = jnp.where(lane < 16, bottom, jnp.where(lane == 32, corner, 0.0))
        edge = [full[8 * i : 8 * i + 8, 128:256] for i in range(16)]
        for at in range(3, 7):
            edge = choose(edge, bit[at])
        edge = jnp.where(lane % 8 == sub, edge[0], 0.0)
        patch_ref[pl.ds(start, 8), 0:128] = halves[0]
        patch_ref[pl.ds(start, 8), 128:256] = halves[1]
        patch_ref[pl.ds(start, 8), 256:384] = third + cnt_ref[pl.ds(start, 8), 128:256]
        edge_ref[pl.ds(start, 8), :] = edge

    for index in range(STEPS):
        for copy in fetch(index):
            copy.wait()
    for group in range(BRICKS // 8):
        one_group(group * 8)

    gather = (iota((128, 128), 1) == iota((128, 128), 0) // 8 + 16).astype(bf16)
    edge_high, edge_low = hi_lo(edge_ref[...])
    third = patch_ref[:, 256:384] + (mm(edge_high, gather) + mm(edge_low, gather))

    high, low = hi_lo(patch_ref[:, 0:256])
    ends = jnp.concatenate(hi_lo(third), axis=1)
    lane_wide = iota((N_DEST, 128), 1)
    for pair in range(4):
        edges = []
        for rank in (2 * pair, 2 * pair + 1):
            pick = (iota((N_DEST, BRICKS), 0) + rank * N_DEST == position).astype(bf16)
            inner = mm(pick, high) + mm(pick, low)
            out_ref[pl.ds(rank, N_DEST, stride=MESSAGE), :] = inner[:, 0:128]
            out_ref[pl.ds(8 + rank, N_DEST, stride=MESSAGE), :] = inner[:, 128:256]
            both = mm(pick, ends)
            edges.append(both[:, 0:128] + both[:, 128:256])
        joined = jnp.where(lane_wide < 64, edges[0], pltpu.roll(edges[1], 64, 1))
        out_ref[pl.ds(16 + pair, N_DEST, stride=MESSAGE), :] = joined


def deposit_and_pack(offsets, weights, counts, owners, slots):
    flat = offsets.reshape(BRICKS, 2, 2, 128).transpose(0, 2, 1, 3).reshape(4 * BRICKS, 128)
    return pl.pallas_call(
        deposit_kernel,
        out_shape=jax.ShapeDtypeStruct((N_DEST * MESSAGE, 128), f32),
        in_specs=[pl.BlockSpec(memory_space=pltpu.MemorySpace.HBM)] * 5,
        scratch_shapes=[
            pltpu.VMEM((4 * BRICKS, 128), f32),
            pltpu.VMEM((BRICKS, PMAX), f32),
            pltpu.VMEM((1, BRICKS), jnp.int32),
            pltpu.VMEM((1, BRICKS), jnp.int32),
            pltpu.VMEM((1, BRICKS), jnp.int32),
            pltpu.VMEM((BRICKS, 256), f32),
            pltpu.VMEM((BRICKS, 384), f32),
            pltpu.VMEM((BRICKS, 128), f32),
            pltpu.SemaphoreType.DMA((3,)),
            pltpu.SemaphoreType.DMA((STEPS,)),
            pltpu.SemaphoreType.DMA((STEPS,)),
        ],
        compiler_params=pltpu.CompilerParams(vmem_limit_bytes=40 << 20),
        name="deposit",
    )(*(pltpu.with_memory_space_constraint(x, pltpu.MemorySpace.HBM) for x in (
        flat,
        weights,
        counts.reshape(1, BRICKS),
        owners.reshape(1, BRICKS),
        slots.reshape(1, BRICKS),
    )))


def mm3(data, table):
    high, low = hi_lo(data)
    return mm(high, table[0]) + (mm(low, table[0]) + mm(high, table[1]))


def mm3_left(table, data):
    high, low = hi_lo(data)
    return mm(table[0], high) + (mm(table[0], low) + mm(table[1], high))


def block_slots(block):
    row = iota((128, SLOTS), 0)
    return (row // 16) * 64 + row % 16 + block * 16


def edge_slots():
    row = iota((128, SLOTS), 0)
    return (row // 16) * 64 + row % 16 + jnp.where(row < 80, 0, 64 + 48)


def place(x_ref, grid_ref, picks):
    lane8 = iota((8, 128), 1)
    upper = jnp.concatenate([x_ref[pl.ds(rank, N_DEST, stride=MESSAGE), :] for rank in range(8)], axis=0)
    lower = jnp.concatenate([x_ref[pl.ds(8 + rank, N_DEST, stride=MESSAGE), :] for rank in range(8)], axis=0)
    ends = []
    for pair in range(4):
        joined = x_ref[pl.ds(16 + pair, N_DEST, stride=MESSAGE), :]
        ends += [joined, pltpu.roll(joined, 64, 1)]
    ends_high, ends_low = hi_lo(jnp.concatenate(ends, axis=0))
    weigh = jnp.where(lane8 == 40, 16.0, jnp.where(lane8 == 41, 1.0, 0.0)).astype(bf16)
    slot = mm_nt(weigh, ends_high)[0:1, :].astype(jnp.int32)
    high, low = hi_lo(jnp.concatenate([upper, lower], axis=1))
    ends = jnp.concatenate([ends_high, ends_low], axis=1)
    for at, slots in enumerate(picks):
        rows = slice(at * 128, (at + 1) * 128)
        pick = (slots == slot).astype(bf16)
        grid_ref[rows, 0:256] = mm(pick, high) + mm(pick, low)
        both = mm(pick, ends)
        grid_ref[rows, 256:384] = both[:, 0:128] + both[:, 128:256]


def swap_groups(tiles):
    group = iota((8, 128), 1) // 16
    for d in (1, 2, 4):
        mask = (group // d) % 2 == 0
        new = list(tiles)
        for a in range(8):
            if (a // d) % 2 == 0:
                one, two = tiles[a], tiles[a + d]
                new[a] = jnp.where(mask, one, pltpu.roll(two, 16 * d, 1))
                new[a + d] = jnp.where(mask, pltpu.roll(one, 128 - 16 * d, 1), two)
        tiles = new
    return tiles


def turn(side, corner):
    turned = [[pltpu.roll(side[half], 16 - i, 1) for half in range(2)] for i in range(16)]
    return turned + [[pltpu.roll(corner[half], 16, 1) for half in range(2)]]


def unpack_block(grid_ref, starts):
    rows = [[None, None] for _ in range(17)]
    side, corner = [None, None], [None, None]
    none = jnp.zeros((8, 128), f32)
    for half in range(2):
        parts = []
        for third in range(3):
            lanes = slice(third * 128, (third + 1) * 128)
            parts.append(
                swap_groups(
                    [none if at is None else grid_ref[at + half * 8 : at + half * 8 + 8, lanes] for at in starts]
                )
            )
        for i in range(8):
            rows[i][half] = parts[0][i]
            rows[8 + i][half] = parts[1][i]
        rows[16][half] = parts[2][0]
        side[half] = parts[2][1]
        corner[half] = parts[2][2]
    return rows, side, corner


def add_spills(rows, turned, previous):
    lane8 = iota((8, 128), 1)
    out = []
    for i in range(17):
        pair = []
        for half in range(2):
            spill = jnp.where(lane8 % 16 == 0, turned[i][half], 0.0)
            first = 0.0 if previous is None else previous[i][half]
            pair.append(rows[i][half] + jnp.where(lane8 == 0, first, spill))
        out.append(pair)
    return out


def store_block(rows, ref):
    sub = iota((8, 128), 0)
    down = [pltpu.roll(rows[16][half], 1, 0) for half in range(2)]
    for i in range(16):
        low, high = rows[i]
        if i == 0:
            low = low + jnp.where(sub == 0, 0.0, down[0])
            high = high + jnp.where(sub == 0, down[0], down[1])
        ref[pl.ds(i, 8, stride=16), :] = low
        ref[pl.ds(128 + i, 8, stride=16), :] = high
    ref[256:264, :] = jnp.where(sub == 0, down[1], 0.0)
    ref[264:TILE_ROWS, :] = jnp.zeros((8, 128), f32)


def place_edges_kernel(x_ref, first_ref, left_ref, right_ref, grid_ref, side_ref):
    place(x_ref, grid_ref, [edge_slots()])
    lane8 = iota((8, 128), 1)
    rows, side, corner = unpack_block(grid_ref, [0, 16, 32, 48, 64, None, None, None])
    store_block(add_spills(rows, turn(side, corner), None), first_ref)
    rows, side, corner = unpack_block(grid_ref, [None] * 6 + [80, 96])
    turned = turn(side, corner)
    rows = add_spills(rows, turned, None)
    store_block(
        [[jnp.where(lane8 == 0, turned[i][half], rows[i][half]) for half in range(2)] for i in range(17)], side_ref
    )
    right = [jnp.zeros((8, 128), f32)] * 5
    left = [jnp.zeros((8, 128), f32)] * 5
    for tile in range(33):
        group, at = divmod(tile, 5)
        rows8 = slice(tile * 8, tile * 8 + 8)
        both = side_ref[rows8, :]
        moved = jnp.where(lane8 == 112 + group, pltpu.roll(both, 112 + group, 1), right[at])
        right[at] = jnp.where(lane8 // 16 == group, pltpu.roll(both, 16 * group + 16, 1), moved)
        turned64 = pltpu.roll(first_ref[rows8, :], (64 + 16 * group) % 128, 1) if group != 4 else first_ref[rows8, :]
        left[at] = jnp.where(lane8 // 16 == group, turned64, left[at])
    for at in range(5):
        right_ref[at * 8 : at * 8 + 8, :] = right[at]
        left_ref[136 + at * 8 : 144 + at * 8, :] = left[at]
    lane = iota((136, 128), 1)
    left_ref[0:136, :] = jnp.where(lane < 64, first_ref[0:136, :], pltpu.roll(first_ref[136:272, :], 64, 1))


def place_edges(arrived):
    tile = jax.ShapeDtypeStruct((TILE_ROWS, 128), f32)
    return pl.pallas_call(
        place_edges_kernel,
        out_shape=(
            tile,
            jax.ShapeDtypeStruct((LEFT_MESSAGE, 128), f32),
            jax.ShapeDtypeStruct((40, 128), f32),
        ),
        scratch_shapes=[pltpu.VMEM((128, 384), f32), pltpu.VMEM((TILE_ROWS, 128), f32)],
        compiler_params=pltpu.CompilerParams(vmem_limit_bytes=32 << 20),
        cost_estimate=pl.CostEstimate(flops=600_000_000, bytes_accessed=2_000_000, transcendentals=0),
        name="place_edges",
    )(arrived)


def place_inner_kernel(x_ref, inner_ref, own_ref, grid_ref, *tile_refs):
    place(x_ref, grid_ref, [block_slots(block) for block in range(4)])
    previous = None
    for block, ref in enumerate(tile_refs):
        rows, side, corner = unpack_block(grid_ref, [block * 128 + col * 16 for col in range(8)])
        turned = turn(side, corner)
        store_block(add_spills(rows, turned, previous), ref)
        previous = turned
    own_ref[:, 0:256] = mm3(jnp.concatenate([ref[...] for ref in tile_refs[0:3]], axis=1), inner_ref)
    own_ref[:, 256:512] = mm3(jnp.concatenate([ref[...] for ref in tile_refs[2:4]], axis=1), inner_ref[:, 0:256, :])


def place_inner(arrived, inner):
    return pl.pallas_call(
        place_inner_kernel,
        out_shape=jax.ShapeDtypeStruct((TILE_ROWS, 512), f32),
        scratch_shapes=[pltpu.VMEM((BRICKS, 384), f32)] + [pltpu.VMEM((TILE_ROWS, 128), f32)] * 4,
        compiler_params=pltpu.CompilerParams(vmem_limit_bytes=32 << 20),
        cost_estimate=pl.CostEstimate(flops=800_000_000, bytes_accessed=3_000_000, transcendentals=0),
        name="place_inner",
    )(arrived, inner)


def pack_tiles(tiles):
    lane = iota(tiles[0].shape, 1)
    shared = jnp.where((lane >= 56) & (lane < 72), pltpu.roll(tiles[5], 64, 1), tiles[2])
    return [tiles[0], tiles[1], shared, tiles[3], tiles[4]]


def unpack_tiles(tiles):
    return jnp.concatenate([*tiles, pltpu.roll(tiles[2], 64, 1)], axis=1)


def columns_kernel(
    own_ref, first_ref, to_right_ref, from_right_ref, from_left_ref, outer_ref, below_ref, out_ref, up_ref, down_ref
):
    lane8 = iota((8, 128), 1)
    none = jnp.zeros((8, 128), f32)
    spills, rows = [], []
    for tile in range(TILE_ROWS // 8):
        group, at = divmod(tile, 5)
        own = first_ref[tile * 8 : tile * 8 + 8, :]
        if tile == 33:
            spills.append(none)
            rows.append(jnp.concatenate([none, jnp.where(lane8 < 8, own, 0.0)], axis=1))
            continue
        packed = from_left_ref[at * 8 : at * 8 + 8, :]
        spill = jnp.where(lane8 == 0, pltpu.roll(packed, 16 - group, 1), 0.0)
        near = pltpu.roll(packed, 112 - 16 * group, 1)
        spills.append(spill)
        mixed = jnp.where(lane8 < 8, own + spill, jnp.where(lane8 >= 112, near, 0.0))
        wide = from_right_ref[(tile % 17) * 8 : (tile % 17) * 8 + 8, :]
        if tile >= 17:
            wide = pltpu.roll(wide, 64, 1)
        rest = from_right_ref[136 + at * 8 : 144 + at * 8, :]
        if group != 4:
            rest = pltpu.roll(rest, (64 - 16 * group) % 128, 1)
        over = jnp.where(lane8 == 0, pltpu.roll(to_right_ref[at * 8 : at * 8 + 8, :], 16 - group, 1), 0.0)
        right = jnp.where(lane8 < 64, wide, jnp.where(lane8 < 80, rest, 0.0)) + over
        rows.append(jnp.concatenate([right, mixed], axis=1))
    spill = jnp.concatenate(spills, axis=0)
    outer = mm3(jnp.concatenate(rows, axis=0), outer_ref)
    pieces = [
        own_ref[:, 0:128] + taps_low[0] * spill,
        own_ref[:, 256:384] + outer[:, 256:384],
        outer[:, 0:128],
        own_ref[:, 128:256] + taps_high[0] * spill,
        own_ref[:, 384:512] + outer[:, 384:512],
        outer[:, 128:256],
    ]
    low = mm3_left(below_ref, jnp.concatenate([piece[0:UP_ROWS] for piece in pieces[0:3]], axis=1))
    high = mm3_left(below_ref[:, 0:32, :], jnp.concatenate([piece[0:UP_ROWS] for piece in pieces[3:6]], axis=1))
    for part in range(2):
        rows16 = slice(part * 16, part * 16 + 16)
        fives = pack_tiles([half[rows16, at * 128 : (at + 1) * 128] for half in (low, high) for at in range(3)])
        for at, tile in enumerate(fives):
            up_ref[part * 80 + at * 16 : part * 80 + at * 16 + 16, :] = tile
    for at in range(3):
        up_ref[160 + at * 32 : 192 + at * 32, :] = low[32:64, at * 128 : (at + 1) * 128]
    for at, tile in enumerate(pack_tiles([piece[DOWN_FROM : DOWN_FROM + 24] for piece in pieces])):
        down_ref[at * 16 : at * 16 + 16, :] = tile[0:16]
        down_ref[80 + at : 81 + at, :] = tile[16:17]
    down_ref[85:88, :] = jnp.zeros((3, 128), f32)
    for at, piece in enumerate(pieces):
        out_ref[:, at * 128 : (at + 1) * 128] = piece


def outer_columns(own, first, to_right, from_right, from_left, outer, below):
    width = 2 * COL_ROOM[0]
    return pl.pallas_call(
        columns_kernel,
        out_shape=(
            jax.ShapeDtypeStruct((TILE_ROWS, width), f32),
            jax.ShapeDtypeStruct((UP_MESSAGE, 128), f32),
            jax.ShapeDtypeStruct((DOWN_MESSAGE, 128), f32),
        ),
        compiler_params=pltpu.CompilerParams(vmem_limit_bytes=32 << 20),
        cost_estimate=pl.CostEstimate(flops=220_000_000, bytes_accessed=2_000_000, transcendentals=0),
        name="columns",
    )(own, first, to_right, from_right, from_left, outer, below)


def second_columns(current, inner, rest):
    main = mm3(current, inner)
    rest = mm3(jnp.concatenate([current[:, 256:384], current[:, 0:128]], axis=1), rest)
    return jnp.concatenate([main[:, 0:128], rest[:, 0:128], main[:, 128:256], rest[:, 128:256]], axis=1)


def own_rows_kernel(own_ref, table_ref, inner_ref, rest_ref, rows_ref, out_ref, second_ref):
    for at in range(3):
        cols = slice(at * 256, (at + 1) * 256)
        out_ref[:, cols] = mm3_left(table_ref, own_ref[:, cols])
    current = out_ref[0 : ROW_ROOM[0], 0 : COL_ROOM[0]]
    second_ref[...] = mm3_left(rows_ref, second_columns(current, inner_ref, rest_ref))


def own_rows(own, table, inner, rest, rows):
    return pl.pallas_call(
        own_rows_kernel,
        out_shape=(
            jax.ShapeDtypeStruct((2 * ROW_ROOM[0], 2 * COL_ROOM[0]), f32),
            jax.ShapeDtypeStruct((2 * ROW_ROOM[1], 2 * COL_ROOM[1]), f32),
        ),
        compiler_params=pltpu.CompilerParams(vmem_limit_bytes=32 << 20),
        cost_estimate=pl.CostEstimate(flops=4_800_000_000, bytes_accessed=20_000_000, transcendentals=0),
        name="own_rows",
    )(own, table, inner, rest, rows)


def levels_kernel(part_ref, second_ref, below_ref, above_ref, table_ref, inner_ref, added_ref, *refs):
    col_refs = (None,) + refs[0:3]
    row_refs = (None, None) + refs[3:5]
    leader_refs = refs[5:9]
    approx_ref = refs[9]
    peak_ref = refs[10]
    sub = iota((8, 128), 0)
    above = [
        jnp.concatenate(
            [
                above_ref[at * 16 : at * 16 + 16, :],
                jnp.where(sub == 0, above_ref[80 + at : 81 + at, :], 0.0),
            ],
            axis=0,
        )
        for at in range(5)
    ]
    near = mm3_left(table_ref, unpack_tiles(above))
    half = COL_ROOM[0]
    sixes = [
        unpack_tiles([below_ref[part * 80 + at * 16 : part * 80 + at * 16 + 16, :] for at in range(5)])
        for part in range(2)
    ]
    threes = jnp.concatenate([below_ref[160 + at * 32 : 192 + at * 32, :] for at in range(3)], axis=1)
    threes = jnp.concatenate([threes, jnp.zeros((32, half), f32)], axis=1)
    added = {0: near[0:8], 184: near[8:16], 192: near[16:24], 376: near[24:32]}
    added.update({120: sixes[0], 136: threes, 312: sixes[1]})
    cuts = sorted({0, 8, 120, 136, 168, 184, 192, 200, 312, 328, 376, 384})
    both = jnp.concatenate(
        [
            part_ref[start:stop, :] + added[start] if start in added else part_ref[start:stop, :]
            for start, stop in zip(cuts, cuts[1:])
        ],
        axis=0,
    )
    peak = None
    for level in range(4):
        room_r = ROW_ROOM[level]
        room_c = COL_ROOM[level]
        if level == 1:
            halo = jnp.concatenate([added[start][:, :half] for start, _ in SECOND_ROWS], axis=0)
            both = second_ref[...] + mm3_left(added_ref, second_columns(halo, inner_ref, col_refs[1]))
        elif level:
            both = mm3_left(row_refs[level], mm3(current, col_refs[level]))
        current = both[:room_r, :room_c]
        detail_a = both[:room_r, room_c:]
        detail_b = both[room_r:, :room_c]
        detail_c = both[room_r:, room_c:]
        now = jnp.maximum(jnp.maximum(jnp.abs(detail_a), jnp.abs(detail_b)), jnp.abs(detail_c))
        if peak is not None:
            now = jnp.maximum(now, peak)
        wide = jnp.maximum(now, jnp.maximum(pltpu.roll(now, 1, 1), pltpu.roll(now, room_c - 1, 1)))
        wide = jnp.maximum(wide, jnp.maximum(pltpu.roll(wide, 1, 0), pltpu.roll(wide, room_r - 1, 0)))
        n_r = R_DEV >> (level + 1)
        n_c = C_DEV >> (level + 1)
        leader_refs[level][...] = wide[:n_r, :n_c]
        if level < 3:
            pairs = jnp.maximum(now, pltpu.roll(now, room_c - 1, 1))
            pooled = []
            for across in range(room_c // 128):
                top = across * ROW_ROOM[0]
                peak_ref[top : top + room_r, :] = pairs[:, across * 128 : (across + 1) * 128]
                pooled.append(
                    jnp.maximum(
                        peak_ref[pl.ds(top, room_r // 2, stride=2), :],
                        peak_ref[pl.ds(top + 1, room_r // 2, stride=2), :],
                    )
                )
            high, low = hi_lo(jnp.concatenate(pooled, axis=1) if len(pooled) > 1 else pooled[0])
            room_n = COL_ROOM[level + 1]
            out = iota((room_c, room_n), 1)
            source = 2 * out + jnp.where(out < 3 * room_n // 4, 0, room_c - 2 * room_n)
            pick = (iota((room_c, room_n), 0) == source).astype(bf16)
            peak = mm(high, pick) + mm(low, pick)
    approx_ref[...] = current[: R_DEV >> 4, : C_DEV >> 4]


def all_levels(part, second, below, above, near, inner, added, cols, rows):
    shapes = [(R_DEV >> level, C_DEV >> level) for level in (1, 2, 3, 4, 4)]
    return pl.pallas_call(
        levels_kernel,
        out_shape=tuple(jax.ShapeDtypeStruct(shape, f32) for shape in shapes),
        scratch_shapes=[pltpu.VMEM((3 * ROW_ROOM[0], 128), f32)],
        compiler_params=pltpu.CompilerParams(vmem_limit_bytes=32 << 20),
        name="levels",
    )(part, second, below, above, near, inner, added, *cols, *rows)


def shifted(x, axis, by):
    size = lax.axis_size(axis)
    return lax.ppermute(x, axis, [(i, (i + by) % size) for i in range(size)])


def transform(arrived):
    table = jax.tree.map(jnp.asarray, tables())
    first, to_left, to_right = place_edges(arrived)
    from_right = shifted(to_left, "cols", -1)
    from_left = shifted(to_right, "cols", 1)
    inner = place_inner(arrived, table["inner"])
    own, to_up, to_down = outer_columns(
        inner, first, to_right, from_right, from_left, table["outer"], table["below"]
    )
    above = shifted(to_down, "rows", 1)
    below = shifted(to_up, "rows", -1)
    part, second = own_rows(own, table["own"], table["inner"], table["cols"][0], table["rows"][0])
    return all_levels(
        part, second, below, above, table["above"], table["inner"], table["second"], table["cols"], table["rows"][1:]
    )


def on_device(offsets, lens_weight, counts, owners, brick_slot):
    packed = deposit_and_pack(offsets, lens_weight, counts, owners, brick_slot)
    arrived = lax.all_to_all(
        packed.reshape(N_DEST, MESSAGE // 4, 4, 128), ("rows", "cols"), split_axis=0, concat_axis=0, tiled=True
    )
    return transform(arrived.reshape(N_DEST * MESSAGE, 128))


def solution(mesh):
    placed = (
        P(("rows", "cols"), None, None),
        P(("rows", "cols"), None),
        P(("rows", "cols")),
        P(("rows", "cols")),
        P(("rows", "cols")),
    )
    return jax.shard_map(
        on_device,
        mesh=mesh,
        in_specs=placed,
        out_specs=(P("rows", "cols"),) * 5,
        check_vma=False,
    )
```

```python
import functools

import jax
import jax.numpy as jnp
import numpy as np
from jax import lax
from jax.experimental import pallas as pl
from jax.experimental.pallas import tpu as pltpu
from jax.sharding import PartitionSpec as P

R_DEV = 256
C_DEV = 512
PMAX = 256
CAP = 8
N_DEST = 128
BRICKS = 512
SLOTS = N_DEST * CAP

TILE_ROWS = 272
UP_ROWS = 80
DOWN_ROWS = 24
DOWN_FROM = 240
ROW_ROOM = (192, 96, 48, 24)
COL_ROOM = (384, 256, 128, 128)

taps_low = (
    0.33267055295008263,
    0.8068915093110925,
    0.4598775021184915,
    -0.13501102001025458,
    -0.08544127388202666,
    0.03522629188570953,
)
taps_high = tuple(((-1.0) ** index * taps_low[5 - index] for index in range(6)))

f32 = jnp.float32
bf16 = jnp.bfloat16


def spans(size):
    out = []
    for level in range(1, 5):
        n = size >> level
        before = 8 >> (level - 1)
        after = (36, 16, 6, 1)[level - 1]
        out.append((-before, n + after, -before, n + before))
    return out


def level_table(sources, room, span):
    low_from, low_to, high_from, high_to = span
    table = np.zeros((len(sources), 2 * room), np.float64)
    for position, index in enumerate(sources):
        if index is None:
            continue
        for half, (lo, hi, taps) in enumerate(
            ((low_from, low_to, taps_low), (high_from, high_to, taps_high))
        ):
            for tap in range(6):
                if (index - tap) % 2 == 0:
                    k = (index - tap) // 2
                    if lo <= k < hi:
                        table[position, half * room + (k % room)] += taps[tap]
    return table


def room_sources(room, low_from, low_to):
    out = [None] * room
    for k in range(low_from, low_to):
        out[k % room] = k
    return out


def split(table):
    table = np.asarray(table, np.float32)
    high = table.astype(jnp.bfloat16)
    low = (table - high.astype(np.float32)).astype(jnp.bfloat16)
    return np.stack([high, low])


ABOVE_ROWS = ((0, 8), (184, 192), (192, 200), (376, 384))
BELOW_ROWS = ((120, 136), (312, 328), (136, 168))
SECOND_ROWS = ((0, 8), (120, 136), (136, 168), (184, 192))
UP_MESSAGE = 5 * 16 + 5 * 16 + 3 * 32
DOWN_MESSAGE = 5 * 16 + 8
LEFT_MESSAGE = TILE_ROWS // 2 + 40


@functools.lru_cache(maxsize=1)
def tables():
    col_spans = spans(C_DEV)
    row_spans = spans(R_DEV)
    inner = level_table(list(range(384)), 128, (0, 128, 0, 128))
    right = [C_DEV + j if j < 76 else None for j in range(128)] + [None] * 128
    mixed = [None] * 128 + list(range(8)) + [None] * 104 + [j - 16 for j in range(16)]
    room = COL_ROOM[0]
    beyond = level_table(right, room, (256, 292, 256, 264)) + level_table(mixed, room, (-8, 0, -8, 0))
    partial = level_table(right, room, (254, 256, 254, 256))
    outer = np.concatenate(
        [
            beyond[:, 256:384],
            beyond[:, room + 256 : room + 384],
            partial[:, 128:256],
            partial[:, room + 128 : room + 256],
        ],
        axis=1,
    )
    row_src = [i if i < 257 else None for i in range(TILE_ROWS)]
    row_src += [R_DEV + i if i < 76 else None for i in range(UP_ROWS)]
    row_src += [i - 16 if i < 17 else None for i in range(DOWN_ROWS)]
    third = [256 + j if j < 36 else j - 128 if j >= 120 else None for j in range(128)] + [None] * 128
    room = COL_ROOM[1]
    rest = level_table(third, room, col_spans[1])
    rest += level_table([None] * 128 + list(range(8)) + [None] * 120, room, (-4, 0, -4, 0))
    rest = np.concatenate([rest[:, 128:256], rest[:, room + 128 : room + 256]], axis=1)
    cols, rows = [rest], []
    for level in range(4):
        if level > 1:
            cols.append(level_table(col_src, COL_ROOM[level], col_spans[level]))
        rows.append(level_table(row_src, ROW_ROOM[level], row_spans[level]).T)
        col_src = room_sources(COL_ROOM[level], col_spans[level][0], col_spans[level][1])
        row_src = room_sources(ROW_ROOM[level], row_spans[level][0], row_spans[level][1])
    first = rows[0]
    below = first[:, TILE_ROWS : TILE_ROWS + UP_ROWS]
    above = first[:, TILE_ROWS + UP_ROWS :]
    for part, kept in ((below, BELOW_ROWS), (above, ABOVE_ROWS)):
        far = np.ones(first.shape[0], bool)
        for start, stop in kept:
            far[start:stop] = False
        assert not part[far].any()
    below = np.concatenate([below[start:stop] for start, stop in BELOW_ROWS], axis=0)
    above = np.concatenate([above[start:stop] for start, stop in ABOVE_ROWS], axis=0)
    second = np.concatenate([rows[1][:, start:stop] for start, stop in SECOND_ROWS], axis=1)
    return {
        "second": split(second),
        "inner": split(inner),
        "outer": split(outer),
        "own": split(first[:, :TILE_ROWS]),
        "below": split(below),
        "above": split(above),
        "cols": [split(t) for t in cols],
        "rows": [split(t) for t in rows[1:]],
    }


def hi_lo(x):
    high = x.astype(bf16)
    low = (x - high.astype(f32)).astype(bf16)
    return high, low


def mm(a, b):
    return jnp.dot(a, b, preferred_element_type=f32)


def mm_nt(a, b):
    return lax.dot_general(a, b, (((1,), (1,)), ((), ())), preferred_element_type=f32)


def iota(shape, dim):
    return lax.broadcasted_iota(jnp.int32, shape, dim)


STEPS = 4
STEP_BRICKS = BRICKS // STEPS
MESSAGE = 20


def deposit_kernel(
    off_hbm,
    w_hbm,
    counts_hbm,
    owners_hbm,
    slot_hbm,
    out_ref,
    off_ref,
    w_ref,
    counts_ref,
    owners_ref,
    slot_ref,
    cnt_ref,
    patch_ref,
    edge_ref,
    small_sem,
    off_sem,
    w_sem,
):
    small = [
        pltpu.make_async_copy(src, dst, small_sem.at[n])
        for n, (src, dst) in enumerate(
            ((owners_hbm, owners_ref), (slot_hbm, slot_ref), (counts_hbm, counts_ref))
        )
    ]
    for copy in small:
        copy.start()

    def fetch(index):
        off_rows = pl.ds(index * 4 * STEP_BRICKS, 4 * STEP_BRICKS)
        w_rows = pl.ds(index * STEP_BRICKS, STEP_BRICKS)
        return (
            pltpu.make_async_copy(off_hbm.at[off_rows], off_ref.at[off_rows], off_sem.at[index]),
            pltpu.make_async_copy(w_hbm.at[w_rows], w_ref.at[w_rows], w_sem.at[index]),
        )

    for index in range(STEPS):
        for copy in fetch(index):
            copy.start()
    for copy in small:
        copy.wait()

    owners = owners_ref[...]
    dest = (iota((N_DEST, BRICKS), 0) == owners).astype(f32)
    before = (iota((BRICKS, BRICKS), 0) < iota((BRICKS, BRICKS), 1)).astype(bf16)
    ranks = jnp.sum(mm(dest.astype(bf16), before) * dest, axis=0, keepdims=True)
    position = ranks.astype(jnp.int32) * N_DEST + owners

    slot = slot_ref[...]
    grid_row = slot // 32
    grid_col = slot % 32
    coarse = (grid_col % 8) * 4 + grid_col // 8
    row_id = iota((256, BRICKS), 0)
    spread = jnp.where(
        row_id < 128,
        counts_ref[...],
        jnp.where(row_id == 168, coarse, jnp.where(row_id == 169, grid_row, 0)),
    )
    eye = (iota((BRICKS, BRICKS), 0) == iota((BRICKS, BRICKS), 1)).astype(bf16)
    cnt_ref[...] = mm_nt(eye, spread.astype(f32).astype(bf16))

    lane = iota((8, 128), 1)
    sub = iota((8, 128), 0)
    particle = iota((8, PMAX), 1).astype(f32)
    cell = iota((16, PMAX), 0).astype(f32)

    zero = jnp.zeros((), bf16)
    bit = {at: (lane >> at) % 2 == 1 for at in (3, 4, 5, 6)}

    def choose(tiles, mask):
        return [jnp.where(mask, odd, even) for even, odd in zip(tiles[0::2], tiles[1::2])]

    def one_group(start):
        first = start * 4
        rows_at = jnp.concatenate([off_ref[pl.ds(first + 2 * half, 8, stride=4), :] for half in range(2)], axis=1)
        cols_at = jnp.concatenate([off_ref[pl.ds(first + 2 * half + 1, 8, stride=4), :] for half in range(2)], axis=1)
        count = cnt_ref[pl.ds(start, 8), 0:128]
        count = jnp.concatenate([count, count], axis=1)
        weight = jnp.where(particle < count, w_ref[pl.ds(start, 8), :], 0.0)
        lag = rows_at * weight
        left = []
        for i in range(17):
            left.append(weight - jnp.abs(lag))
            lag = lag - weight
        left = jnp.maximum(jnp.concatenate(left, axis=0).astype(bf16), zero)
        right = []
        for g in range(8):
            at = first + 4 * ((8 - g) % 8) + 1
            column = jnp.concatenate([off_ref[pl.ds(at + 2 * half, 8, stride=0), :] for half in range(2)], axis=1)
            right += [1.0 - jnp.abs(column - cell[0:8]), 1.0 - jnp.abs(column - cell[8:16])]
        last = cols_at - 15.0
        right = [jnp.maximum(jnp.concatenate(right, axis=0).astype(bf16), zero)]
        right += [jnp.maximum(jnp.concatenate([last, last], axis=0).astype(bf16), zero)] * 8
        full = mm_nt(left, jnp.concatenate(right, axis=0))
        halves = []
        for half in range(2):
            pairs = []
            for pair in range(4):
                at = (half * 8 + pair * 2) * 8
                even = pltpu.roll(full[at : at + 8, 0:128], 0, 1, stride=16, stride_axis=0)
                odd = pltpu.roll(full[at + 8 : at + 16, 0:128], 16, 1, stride=16, stride_axis=0)
                both = jnp.where(bit[4], odd, even)
                pairs.append(pltpu.roll(both, 32 * pair, 1) if pair else both)
            halves.append(choose(choose(pairs, bit[5]), bit[6])[0])
        bottom = pltpu.roll(full[128:136, 0:128], 0, 1, stride=16, stride_axis=0)
        corner = jnp.sum(jnp.where(lane == sub, full[128:136, 128:256], 0.0), axis=1, keepdims=True)
        third = jnp.where(lane < 16, bottom, jnp.where(lane == 32, corner, 0.0))
        edge = [full[8 * i : 8 * i + 8, 128:256] for i in range(16)]
        for at in range(3, 7):
            edge = choose(edge, bit[at])
        edge = jnp.where(lane % 8 == sub, edge[0], 0.0)
        patch_ref[pl.ds(start, 8), 0:128] = halves[0]
        patch_ref[pl.ds(start, 8), 128:256] = halves[1]
        patch_ref[pl.ds(start, 8), 256:384] = third + cnt_ref[pl.ds(start, 8), 128:256]
        edge_ref[pl.ds(start, 8), :] = edge

    for index in range(STEPS):
        for copy in fetch(index):
            copy.wait()
    for group in range(BRICKS // 8):
        one_group(group * 8)

    gather = (iota((128, 128), 1) == iota((128, 128), 0) // 8 + 16).astype(bf16)
    edge_high, edge_low = hi_lo(edge_ref[...])
    third = patch_ref[:, 256:384] + (mm(edge_high, gather) + mm(edge_low, gather))

    high, low = hi_lo(patch_ref[:, 0:256])
    ends = jnp.concatenate(hi_lo(third), axis=1)
    lane_wide = iota((N_DEST, 128), 1)
    for pair in range(4):
        edges = []
        for rank in (2 * pair, 2 * pair + 1):
            pick = (iota((N_DEST, BRICKS), 0) + rank * N_DEST == position).astype(bf16)
            inner = mm(pick, high) + mm(pick, low)
            out_ref[pl.ds(rank, N_DEST, stride=MESSAGE), :] = inner[:, 0:128]
            out_ref[pl.ds(8 + rank, N_DEST, stride=MESSAGE), :] = inner[:, 128:256]
            both = mm(pick, ends)
            edges.append(both[:, 0:128] + both[:, 128:256])
        joined = jnp.where(lane_wide < 64, edges[0], pltpu.roll(edges[1], 64, 1))
        out_ref[pl.ds(16 + pair, N_DEST, stride=MESSAGE), :] = joined


def deposit_and_pack(offsets, weights, counts, owners, slots):
    flat = offsets.reshape(BRICKS, 2, 2, 128).transpose(0, 2, 1, 3).reshape(4 * BRICKS, 128)
    return pl.pallas_call(
        deposit_kernel,
        out_shape=jax.ShapeDtypeStruct((N_DEST * MESSAGE, 128), f32),
        in_specs=[pl.BlockSpec(memory_space=pltpu.MemorySpace.HBM)] * 5,
        scratch_shapes=[
            pltpu.VMEM((4 * BRICKS, 128), f32),
            pltpu.VMEM((BRICKS, PMAX), f32),
            pltpu.VMEM((1, BRICKS), jnp.int32),
            pltpu.VMEM((1, BRICKS), jnp.int32),
            pltpu.VMEM((1, BRICKS), jnp.int32),
            pltpu.VMEM((BRICKS, 256), f32),
            pltpu.VMEM((BRICKS, 384), f32),
            pltpu.VMEM((BRICKS, 128), f32),
            pltpu.SemaphoreType.DMA((3,)),
            pltpu.SemaphoreType.DMA((STEPS,)),
            pltpu.SemaphoreType.DMA((STEPS,)),
        ],
        compiler_params=pltpu.CompilerParams(vmem_limit_bytes=40 << 20),
        name="deposit",
    )(*(pltpu.with_memory_space_constraint(x, pltpu.MemorySpace.HBM) for x in (
        flat,
        weights,
        counts.reshape(1, BRICKS),
        owners.reshape(1, BRICKS),
        slots.reshape(1, BRICKS),
    )))


def mm3(data, table):
    high, low = hi_lo(data)
    return mm(high, table[0]) + (mm(low, table[0]) + mm(high, table[1]))


def mm3_left(table, data):
    high, low = hi_lo(data)
    return mm(table[0], high) + (mm(table[0], low) + mm(table[1], high))


def block_slots(block):
    row = iota((128, SLOTS), 0)
    return (row // 16) * 64 + row % 16 + block * 16


def edge_slots():
    row = iota((128, SLOTS), 0)
    return (row // 16) * 64 + row % 16 + jnp.where(row < 80, 0, 64 + 48)


def place(x_ref, grid_ref, picks):
    lane8 = iota((8, 128), 1)
    upper = jnp.concatenate([x_ref[pl.ds(rank, N_DEST, stride=MESSAGE), :] for rank in range(8)], axis=0)
    lower = jnp.concatenate([x_ref[pl.ds(8 + rank, N_DEST, stride=MESSAGE), :] for rank in range(8)], axis=0)
    ends = []
    for pair in range(4):
        joined = x_ref[pl.ds(16 + pair, N_DEST, stride=MESSAGE), :]
        ends += [joined, pltpu.roll(joined, 64, 1)]
    ends_high, ends_low = hi_lo(jnp.concatenate(ends, axis=0))
    weigh = jnp.where(lane8 == 40, 16.0, jnp.where(lane8 == 41, 1.0, 0.0)).astype(bf16)
    slot = mm_nt(weigh, ends_high)[0:1, :].astype(jnp.int32)
    high, low = hi_lo(jnp.concatenate([upper, lower], axis=1))
    ends = jnp.concatenate([ends_high, ends_low], axis=1)
    for at, slots in enumerate(picks):
        rows = slice(at * 128, (at + 1) * 128)
        pick = (slots == slot).astype(bf16)
        grid_ref[rows, 0:256] = mm(pick, high) + mm(pick, low)
        both = mm(pick, ends)
        grid_ref[rows, 256:384] = both[:, 0:128] + both[:, 128:256]


def swap_groups(tiles):
    group = iota((8, 128), 1) // 16
    for d in (1, 2, 4):
        mask = (group // d) % 2 == 0
        new = list(tiles)
        for a in range(8):
            if (a // d) % 2 == 0:
                one, two = tiles[a], tiles[a + d]
                new[a] = jnp.where(mask, one, pltpu.roll(two, 16 * d, 1))
                new[a + d] = jnp.where(mask, pltpu.roll(one, 128 - 16 * d, 1), two)
        tiles = new
    return tiles


def turn(side, corner):
    turned = [[pltpu.roll(side[half], 16 - i, 1) for half in range(2)] for i in range(16)]
    return turned + [[pltpu.roll(corner[half], 16, 1) for half in range(2)]]


def unpack_block(grid_ref, starts):
    rows = [[None, None] for _ in range(17)]
    side, corner = [None, None], [None, None]
    none = jnp.zeros((8, 128), f32)
    for half in range(2):
        parts = []
        for third in range(3):
            lanes = slice(third * 128, (third + 1) * 128)
            parts.append(
                swap_groups(
                    [none if at is None else grid_ref[at + half * 8 : at + half * 8 + 8, lanes] for at in starts]
                )
            )
        for i in range(8):
            rows[i][half] = parts[0][i]
            rows[8 + i][half] = parts[1][i]
        rows[16][half] = parts[2][0]
        side[half] = parts[2][1]
        corner[half] = parts[2][2]
    return rows, side, corner


def add_spills(rows, turned, previous):
    lane8 = iota((8, 128), 1)
    out = []
    for i in range(17):
        pair = []
        for half in range(2):
            spill = jnp.where(lane8 % 16 == 0, turned[i][half], 0.0)
            first = 0.0 if previous is None else previous[i][half]
            pair.append(rows[i][half] + jnp.where(lane8 == 0, first, spill))
        out.append(pair)
    return out


def store_block(rows, ref):
    sub = iota((8, 128), 0)
    down = [pltpu.roll(rows[16][half], 1, 0) for half in range(2)]
    for i in range(16):
        low, high = rows[i]
        if i == 0:
            low = low + jnp.where(sub == 0, 0.0, down[0])
            high = high + jnp.where(sub == 0, down[0], down[1])
        ref[pl.ds(i, 8, stride=16), :] = low
        ref[pl.ds(128 + i, 8, stride=16), :] = high
    ref[256:264, :] = jnp.where(sub == 0, down[1], 0.0)
    ref[264:TILE_ROWS, :] = jnp.zeros((8, 128), f32)


def place_edges_kernel(x_ref, first_ref, left_ref, right_ref, grid_ref, side_ref):
    place(x_ref, grid_ref, [edge_slots()])
    lane8 = iota((8, 128), 1)
    rows, side, corner = unpack_block(grid_ref, [0, 16, 32, 48, 64, None, None, None])
    store_block(add_spills(rows, turn(side, corner), None), first_ref)
    rows, side, corner = unpack_block(grid_ref, [None] * 6 + [80, 96])
    turned = turn(side, corner)
    rows = add_spills(rows, turned, None)
    store_block(
        [[jnp.where(lane8 == 0, turned[i][half], rows[i][half]) for half in range(2)] for i in range(17)], side_ref
    )
    right = [jnp.zeros((8, 128), f32)] * 5
    left = [jnp.zeros((8, 128), f32)] * 5
    for tile in range(33):
        group, at = divmod(tile, 5)
        rows8 = slice(tile * 8, tile * 8 + 8)
        both = side_ref[rows8, :]
        moved = jnp.where(lane8 == 112 + group, pltpu.roll(both, 112 + group, 1), right[at])
        right[at] = jnp.where(lane8 // 16 == group, pltpu.roll(both, 16 * group + 16, 1), moved)
        turned64 = pltpu.roll(first_ref[rows8, :], (64 + 16 * group) % 128, 1) if group != 4 else first_ref[rows8, :]
        left[at] = jnp.where(lane8 // 16 == group, turned64, left[at])
    for at in range(5):
        right_ref[at * 8 : at * 8 + 8, :] = right[at]
        left_ref[136 + at * 8 : 144 + at * 8, :] = left[at]
    lane = iota((136, 128), 1)
    left_ref[0:136, :] = jnp.where(lane < 64, first_ref[0:136, :], pltpu.roll(first_ref[136:272, :], 64, 1))


def place_edges(arrived):
    tile = jax.ShapeDtypeStruct((TILE_ROWS, 128), f32)
    return pl.pallas_call(
        place_edges_kernel,
        out_shape=(
            tile,
            jax.ShapeDtypeStruct((LEFT_MESSAGE, 128), f32),
            jax.ShapeDtypeStruct((40, 128), f32),
        ),
        scratch_shapes=[pltpu.VMEM((128, 384), f32), pltpu.VMEM((TILE_ROWS, 128), f32)],
        compiler_params=pltpu.CompilerParams(vmem_limit_bytes=32 << 20),
        cost_estimate=pl.CostEstimate(flops=600_000_000, bytes_accessed=2_000_000, transcendentals=0),
        name="place_edges",
    )(arrived)


def place_inner_kernel(x_ref, inner_ref, own_ref, grid_ref, *tile_refs):
    place(x_ref, grid_ref, [block_slots(block) for block in range(4)])
    previous = None
    for block, ref in enumerate(tile_refs):
        rows, side, corner = unpack_block(grid_ref, [block * 128 + col * 16 for col in range(8)])
        turned = turn(side, corner)
        store_block(add_spills(rows, turned, previous), ref)
        previous = turned
    own_ref[:, 0:256] = mm3(jnp.concatenate([ref[...] for ref in tile_refs[0:3]], axis=1), inner_ref)
    own_ref[:, 256:512] = mm3(jnp.concatenate([ref[...] for ref in tile_refs[2:4]], axis=1), inner_ref[:, 0:256, :])


def place_inner(arrived, inner):
    return pl.pallas_call(
        place_inner_kernel,
        out_shape=jax.ShapeDtypeStruct((TILE_ROWS, 512), f32),
        scratch_shapes=[pltpu.VMEM((BRICKS, 384), f32)] + [pltpu.VMEM((TILE_ROWS, 128), f32)] * 4,
        compiler_params=pltpu.CompilerParams(vmem_limit_bytes=32 << 20),
        cost_estimate=pl.CostEstimate(flops=800_000_000, bytes_accessed=3_000_000, transcendentals=0),
        name="place_inner",
    )(arrived, inner)


def pack_tiles(tiles):
    lane = iota(tiles[0].shape, 1)
    shared = jnp.where((lane >= 56) & (lane < 72), pltpu.roll(tiles[5], 64, 1), tiles[2])
    return [tiles[0], tiles[1], shared, tiles[3], tiles[4]]


def unpack_tiles(tiles):
    return jnp.concatenate([*tiles, pltpu.roll(tiles[2], 64, 1)], axis=1)


def columns_kernel(
    own_ref, first_ref, to_right_ref, from_right_ref, from_left_ref, outer_ref, out_ref, down_ref
):
    lane8 = iota((8, 128), 1)
    none = jnp.zeros((8, 128), f32)
    spills, rows = [], []
    for tile in range(TILE_ROWS // 8):
        group, at = divmod(tile, 5)
        own = first_ref[tile * 8 : tile * 8 + 8, :]
        if tile == 33:
            spills.append(none)
            rows.append(jnp.concatenate([none, jnp.where(lane8 < 8, own, 0.0)], axis=1))
            continue
        packed = from_left_ref[at * 8 : at * 8 + 8, :]
        spill = jnp.where(lane8 == 0, pltpu.roll(packed, 16 - group, 1), 0.0)
        near = pltpu.roll(packed, 112 - 16 * group, 1)
        spills.append(spill)
        mixed = jnp.where(lane8 < 8, own + spill, jnp.where(lane8 >= 112, near, 0.0))
        wide = from_right_ref[(tile % 17) * 8 : (tile % 17) * 8 + 8, :]
        if tile >= 17:
            wide = pltpu.roll(wide, 64, 1)
        rest = from_right_ref[136 + at * 8 : 144 + at * 8, :]
        if group != 4:
            rest = pltpu.roll(rest, (64 - 16 * group) % 128, 1)
        over = jnp.where(lane8 == 0, pltpu.roll(to_right_ref[at * 8 : at * 8 + 8, :], 16 - group, 1), 0.0)
        right = jnp.where(lane8 < 64, wide, jnp.where(lane8 < 80, rest, 0.0)) + over
        rows.append(jnp.concatenate([right, mixed], axis=1))
    spill = jnp.concatenate(spills, axis=0)
    outer = mm3(jnp.concatenate(rows, axis=0), outer_ref)
    pieces = [
        own_ref[:, 0:128] + taps_low[0] * spill,
        own_ref[:, 256:384] + outer[:, 256:384],
        outer[:, 0:128],
        own_ref[:, 128:256] + taps_high[0] * spill,
        own_ref[:, 384:512] + outer[:, 384:512],
        outer[:, 128:256],
    ]
    for at, tile in enumerate(pack_tiles([piece[DOWN_FROM : DOWN_FROM + 24] for piece in pieces])):
        down_ref[at * 16 : at * 16 + 16, :] = tile[0:16]
        down_ref[80 + at : 81 + at, :] = tile[16:17]
    down_ref[85:88, :] = jnp.zeros((3, 128), f32)
    for at, piece in enumerate(pieces):
        out_ref[:, at * 128 : (at + 1) * 128] = piece


def outer_columns(own, first, to_right, from_right, from_left, outer):
    width = 2 * COL_ROOM[0]
    return pl.pallas_call(
        columns_kernel,
        out_shape=(
            jax.ShapeDtypeStruct((TILE_ROWS, width), f32),
            jax.ShapeDtypeStruct((DOWN_MESSAGE, 128), f32),
        ),
        compiler_params=pltpu.CompilerParams(vmem_limit_bytes=32 << 20),
        cost_estimate=pl.CostEstimate(flops=220_000_000, bytes_accessed=2_000_000, transcendentals=0),
        name="columns",
    )(own, first, to_right, from_right, from_left, outer)


def upward_kernel(own_ref, below_ref, up_ref):
    half = COL_ROOM[0]
    low = mm3_left(below_ref, own_ref[0:UP_ROWS, 0:half])
    high = mm3_left(below_ref[:, 0:32, :], own_ref[0:UP_ROWS, half : 2 * half])
    for part in range(2):
        rows16 = slice(part * 16, part * 16 + 16)
        fives = pack_tiles([side[rows16, at * 128 : (at + 1) * 128] for side in (low, high) for at in range(3)])
        for at, tile in enumerate(fives):
            up_ref[part * 80 + at * 16 : part * 80 + at * 16 + 16, :] = tile
    for at in range(3):
        up_ref[160 + at * 32 : 192 + at * 32, :] = low[32:64, at * 128 : (at + 1) * 128]


def upward(own, below):
    return pl.pallas_call(
        upward_kernel,
        out_shape=jax.ShapeDtypeStruct((UP_MESSAGE, 128), f32),
        compiler_params=pltpu.CompilerParams(vmem_limit_bytes=32 << 20),
        cost_estimate=pl.CostEstimate(flops=2_000_000_000, bytes_accessed=6_000_000, transcendentals=0),
        name="upward",
    )(own, below)


def second_columns(current, inner, rest):
    main = mm3(current, inner)
    rest = mm3(jnp.concatenate([current[:, 256:384], current[:, 0:128]], axis=1), rest)
    return jnp.concatenate([main[:, 0:128], rest[:, 0:128], main[:, 128:256], rest[:, 128:256]], axis=1)


def own_rows_kernel(own_ref, table_ref, inner_ref, rest_ref, rows_ref, out_ref, second_ref):
    for at in range(3):
        cols = slice(at * 256, (at + 1) * 256)
        out_ref[:, cols] = mm3_left(table_ref, own_ref[:, cols])
    current = out_ref[0 : ROW_ROOM[0], 0 : COL_ROOM[0]]
    second_ref[...] = mm3_left(rows_ref, second_columns(current, inner_ref, rest_ref))


def own_rows(own, table, inner, rest, rows):
    return pl.pallas_call(
        own_rows_kernel,
        out_shape=(
            jax.ShapeDtypeStruct((2 * ROW_ROOM[0], 2 * COL_ROOM[0]), f32),
            jax.ShapeDtypeStruct((2 * ROW_ROOM[1], 2 * COL_ROOM[1]), f32),
        ),
        compiler_params=pltpu.CompilerParams(vmem_limit_bytes=32 << 20),
        cost_estimate=pl.CostEstimate(flops=4_800_000_000, bytes_accessed=20_000_000, transcendentals=0),
        name="own_rows",
    )(own, table, inner, rest, rows)


def levels_kernel(part_ref, second_ref, below_ref, above_ref, table_ref, inner_ref, added_ref, *refs):
    col_refs = (None,) + refs[0:3]
    row_refs = (None, None) + refs[3:5]
    leader_refs = refs[5:9]
    approx_ref = refs[9]
    peak_ref = refs[10]
    sub = iota((8, 128), 0)
    above = [
        jnp.concatenate(
            [
                above_ref[at * 16 : at * 16 + 16, :],
                jnp.where(sub == 0, above_ref[80 + at : 81 + at, :], 0.0),
            ],
            axis=0,
        )
        for at in range(5)
    ]
    near = mm3_left(table_ref, unpack_tiles(above))
    half = COL_ROOM[0]
    sixes = [
        unpack_tiles([below_ref[part * 80 + at * 16 : part * 80 + at * 16 + 16, :] for at in range(5)])
        for part in range(2)
    ]
    threes = jnp.concatenate([below_ref[160 + at * 32 : 192 + at * 32, :] for at in range(3)], axis=1)
    threes = jnp.concatenate([threes, jnp.zeros((32, half), f32)], axis=1)
    added = {0: near[0:8], 184: near[8:16], 192: near[16:24], 376: near[24:32]}
    added.update({120: sixes[0], 136: threes, 312: sixes[1]})
    cuts = sorted({0, 8, 120, 136, 168, 184, 192, 200, 312, 328, 376, 384})
    both = jnp.concatenate(
        [
            part_ref[start:stop, :] + added[start] if start in added else part_ref[start:stop, :]
            for start, stop in zip(cuts, cuts[1:])
        ],
        axis=0,
    )
    peak = None
    for level in range(4):
        room_r = ROW_ROOM[level]
        room_c = COL_ROOM[level]
        if level == 1:
            halo = jnp.concatenate([added[start][:, :half] for start, _ in SECOND_ROWS], axis=0)
            both = second_ref[...] + mm3_left(added_ref, second_columns(halo, inner_ref, col_refs[1]))
        elif level:
            both = mm3_left(row_refs[level], mm3(current, col_refs[level]))
        current = both[:room_r, :room_c]
        detail_a = both[:room_r, room_c:]
        detail_b = both[room_r:, :room_c]
        detail_c = both[room_r:, room_c:]
        now = jnp.maximum(jnp.maximum(jnp.abs(detail_a), jnp.abs(detail_b)), jnp.abs(detail_c))
        if peak is not None:
            now = jnp.maximum(now, peak)
        wide = jnp.maximum(now, jnp.maximum(pltpu.roll(now, 1, 1), pltpu.roll(now, room_c - 1, 1)))
        wide = jnp.maximum(wide, jnp.maximum(pltpu.roll(wide, 1, 0), pltpu.roll(wide, room_r - 1, 0)))
        n_r = R_DEV >> (level + 1)
        n_c = C_DEV >> (level + 1)
        leader_refs[level][...] = wide[:n_r, :n_c]
        if level < 3:
            pairs = jnp.maximum(now, pltpu.roll(now, room_c - 1, 1))
            pooled = []
            for across in range(room_c // 128):
                top = across * ROW_ROOM[0]
                peak_ref[top : top + room_r, :] = pairs[:, across * 128 : (across + 1) * 128]
                pooled.append(
                    jnp.maximum(
                        peak_ref[pl.ds(top, room_r // 2, stride=2), :],
                        peak_ref[pl.ds(top + 1, room_r // 2, stride=2), :],
                    )
                )
            high, low = hi_lo(jnp.concatenate(pooled, axis=1) if len(pooled) > 1 else pooled[0])
            room_n = COL_ROOM[level + 1]
            out = iota((room_c, room_n), 1)
            source = 2 * out + jnp.where(out < 3 * room_n // 4, 0, room_c - 2 * room_n)
            pick = (iota((room_c, room_n), 0) == source).astype(bf16)
            peak = mm(high, pick) + mm(low, pick)
    approx_ref[...] = current[: R_DEV >> 4, : C_DEV >> 4]


def all_levels(part, second, below, above, near, inner, added, cols, rows):
    shapes = [(R_DEV >> level, C_DEV >> level) for level in (1, 2, 3, 4, 4)]
    return pl.pallas_call(
        levels_kernel,
        out_shape=tuple(jax.ShapeDtypeStruct(shape, f32) for shape in shapes),
        scratch_shapes=[pltpu.VMEM((3 * ROW_ROOM[0], 128), f32)],
        compiler_params=pltpu.CompilerParams(vmem_limit_bytes=32 << 20),
        name="levels",
    )(part, second, below, above, near, inner, added, *cols, *rows)


def shifted(x, axis, by):
    size = lax.axis_size(axis)
    return lax.ppermute(x, axis, [(i, (i + by) % size) for i in range(size)])


def transform(arrived):
    table = jax.tree.map(jnp.asarray, tables())
    first, to_left, to_right = place_edges(arrived)
    from_right = shifted(to_left, "cols", -1)
    from_left = shifted(to_right, "cols", 1)
    inner = place_inner(arrived, table["inner"])
    own, to_down = outer_columns(inner, first, to_right, from_right, from_left, table["outer"])
    above = shifted(to_down, "rows", 1)
    below = shifted(upward(own, table["below"]), "rows", -1)
    part, second = own_rows(own, table["own"], table["inner"], table["cols"][0], table["rows"][0])
    return all_levels(
        part, second, below, above, table["above"], table["inner"], table["second"], table["cols"], table["rows"][1:]
    )


def on_device(offsets, lens_weight, counts, owners, brick_slot):
    packed = deposit_and_pack(offsets, lens_weight, counts, owners, brick_slot)
    arrived = lax.all_to_all(
        packed.reshape(N_DEST, MESSAGE // 4, 4, 128), ("rows", "cols"), split_axis=0, concat_axis=0, tiled=True
    )
    return transform(arrived.reshape(N_DEST * MESSAGE, 128))


def solution(mesh):
    placed = (
        P(("rows", "cols"), None, None),
        P(("rows", "cols"), None),
        P(("rows", "cols")),
        P(("rows", "cols")),
        P(("rows", "cols")),
    )
    return jax.shard_map(
        on_device,
        mesh=mesh,
        in_specs=placed,
        out_specs=(P("rows", "cols"),) * 5,
        check_vma=False,
    )
```

```python
import functools

import jax
import jax.numpy as jnp
import numpy as np
from jax import lax
from jax.experimental import pallas as pl
from jax.experimental.pallas import tpu as pltpu
from jax.sharding import PartitionSpec as P

R_DEV = 256
C_DEV = 512
PMAX = 256
CAP = 8
N_DEST = 128
BRICKS = 512
SLOTS = N_DEST * CAP

TILE_ROWS = 272
UP_ROWS = 80
DOWN_ROWS = 24
DOWN_FROM = 240
ROW_ROOM = (192, 96, 48, 24)
COL_ROOM = (384, 256, 128, 128)

taps_low = (
    0.33267055295008263,
    0.8068915093110925,
    0.4598775021184915,
    -0.13501102001025458,
    -0.08544127388202666,
    0.03522629188570953,
)
taps_high = tuple(((-1.0) ** index * taps_low[5 - index] for index in range(6)))

f32 = jnp.float32
bf16 = jnp.bfloat16


def spans(size):
    out = []
    for level in range(1, 5):
        n = size >> level
        before = 8 >> (level - 1)
        after = (36, 16, 6, 1)[level - 1]
        out.append((-before, n + after, -before, n + before))
    return out


def level_table(sources, room, span):
    low_from, low_to, high_from, high_to = span
    table = np.zeros((len(sources), 2 * room), np.float64)
    for position, index in enumerate(sources):
        if index is None:
            continue
        for half, (lo, hi, taps) in enumerate(
            ((low_from, low_to, taps_low), (high_from, high_to, taps_high))
        ):
            for tap in range(6):
                if (index - tap) % 2 == 0:
                    k = (index - tap) // 2
                    if lo <= k < hi:
                        table[position, half * room + (k % room)] += taps[tap]
    return table


def room_sources(room, low_from, low_to):
    out = [None] * room
    for k in range(low_from, low_to):
        out[k % room] = k
    return out


def split(table):
    table = np.asarray(table, np.float32)
    high = table.astype(jnp.bfloat16)
    low = (table - high.astype(np.float32)).astype(jnp.bfloat16)
    return np.stack([high, low])


ABOVE_ROWS = ((0, 8), (184, 192), (192, 200), (376, 384))
BELOW_ROWS = ((120, 136), (312, 328), (136, 168))
SECOND_ROWS = ((0, 8), (120, 136), (136, 168), (184, 192))
UP_MESSAGE = 5 * 16 + 5 * 16 + 3 * 32
DOWN_MESSAGE = 5 * 16 + 8
LEFT_MESSAGE = TILE_ROWS // 2 + 40


@functools.lru_cache(maxsize=1)
def tables():
    col_spans = spans(C_DEV)
    row_spans = spans(R_DEV)
    inner = level_table(list(range(384)), 128, (0, 128, 0, 128))
    right = [C_DEV + j if j < 76 else None for j in range(128)] + [None] * 128
    mixed = [None] * 128 + list(range(8)) + [None] * 104 + [j - 16 for j in range(16)]
    room = COL_ROOM[0]
    beyond = level_table(right, room, (256, 292, 256, 264)) + level_table(mixed, room, (-8, 0, -8, 0))
    partial = level_table(right, room, (254, 256, 254, 256))
    outer = np.concatenate(
        [
            beyond[:, 256:384],
            beyond[:, room + 256 : room + 384],
            partial[:, 128:256],
            partial[:, room + 128 : room + 256],
        ],
        axis=1,
    )
    row_src = [i if i < 257 else None for i in range(TILE_ROWS)]
    row_src += [R_DEV + i if i < 76 else None for i in range(UP_ROWS)]
    row_src += [i - 16 if i < 17 else None for i in range(DOWN_ROWS)]
    third = [256 + j if j < 36 else j - 128 if j >= 120 else None for j in range(128)] + [None] * 128
    room = COL_ROOM[1]
    rest = level_table(third, room, col_spans[1])
    rest += level_table([None] * 128 + list(range(8)) + [None] * 120, room, (-4, 0, -4, 0))
    rest = np.concatenate([rest[:, 128:256], rest[:, room + 128 : room + 256]], axis=1)
    cols, rows = [rest], []
    for level in range(4):
        if level > 1:
            cols.append(level_table(col_src, COL_ROOM[level], col_spans[level]))
        rows.append(level_table(row_src, ROW_ROOM[level], row_spans[level]).T)
        col_src = room_sources(COL_ROOM[level], col_spans[level][0], col_spans[level][1])
        row_src = room_sources(ROW_ROOM[level], row_spans[level][0], row_spans[level][1])
    first = rows[0]
    below = first[:, TILE_ROWS : TILE_ROWS + UP_ROWS]
    above = first[:, TILE_ROWS + UP_ROWS :]
    for part, kept in ((below, BELOW_ROWS), (above, ABOVE_ROWS)):
        far = np.ones(first.shape[0], bool)
        for start, stop in kept:
            far[start:stop] = False
        assert not part[far].any()
    below = np.concatenate([below[start:stop] for start, stop in BELOW_ROWS], axis=0)
    above = np.concatenate([above[start:stop] for start, stop in ABOVE_ROWS], axis=0)
    second = np.concatenate([rows[1][:, start:stop] for start, stop in SECOND_ROWS], axis=1)
    return {
        "second": split(second),
        "inner": split(inner),
        "outer": split(outer),
        "own": split(first[:, :TILE_ROWS]),
        "below": split(below),
        "above": split(above),
        "cols": [split(t) for t in cols],
        "rows": [split(t) for t in rows[1:]],
    }


def hi_lo(x):
    high = x.astype(bf16)
    low = (x - high.astype(f32)).astype(bf16)
    return high, low


def mm(a, b):
    return jnp.dot(a, b, preferred_element_type=f32)


def mm_nt(a, b):
    return lax.dot_general(a, b, (((1,), (1,)), ((), ())), preferred_element_type=f32)


def iota(shape, dim):
    return lax.broadcasted_iota(jnp.int32, shape, dim)


STEPS = 4
STEP_BRICKS = BRICKS // STEPS
MESSAGE = 20


def deposit_kernel(
    off_hbm,
    w_hbm,
    counts_hbm,
    owners_hbm,
    slot_hbm,
    out_ref,
    off_ref,
    w_ref,
    counts_ref,
    owners_ref,
    slot_ref,
    cnt_ref,
    patch_ref,
    edge_ref,
    small_sem,
    off_sem,
    w_sem,
):
    small = [
        pltpu.make_async_copy(src, dst, small_sem.at[n])
        for n, (src, dst) in enumerate(
            ((owners_hbm, owners_ref), (slot_hbm, slot_ref), (counts_hbm, counts_ref))
        )
    ]
    for copy in small:
        copy.start()

    def fetch(index):
        off_rows = pl.ds(index * 4 * STEP_BRICKS, 4 * STEP_BRICKS)
        w_rows = pl.ds(index * STEP_BRICKS, STEP_BRICKS)
        return (
            pltpu.make_async_copy(off_hbm.at[off_rows], off_ref.at[off_rows], off_sem.at[index]),
            pltpu.make_async_copy(w_hbm.at[w_rows], w_ref.at[w_rows], w_sem.at[index]),
        )

    for index in range(STEPS):
        for copy in fetch(index):
            copy.start()
    for copy in small:
        copy.wait()

    owners = owners_ref[...]
    dest = (iota((N_DEST, BRICKS), 0) == owners).astype(f32)
    before = (iota((BRICKS, BRICKS), 0) < iota((BRICKS, BRICKS), 1)).astype(bf16)
    ranks = jnp.sum(mm(dest.astype(bf16), before) * dest, axis=0, keepdims=True)
    position = ranks.astype(jnp.int32) * N_DEST + owners

    slot = slot_ref[...]
    grid_row = slot // 32
    grid_col = slot % 32
    coarse = (grid_col % 8) * 4 + grid_col // 8
    row_id = iota((256, BRICKS), 0)
    spread = jnp.where(
        row_id < 128,
        counts_ref[...],
        jnp.where(row_id == 168, coarse, jnp.where(row_id == 169, grid_row, 0)),
    )
    eye = (iota((BRICKS, BRICKS), 0) == iota((BRICKS, BRICKS), 1)).astype(bf16)
    cnt_ref[...] = mm_nt(eye, spread.astype(f32).astype(bf16))

    lane = iota((8, 128), 1)
    sub = iota((8, 128), 0)
    particle = iota((8, PMAX), 1).astype(f32)
    cell = iota((16, PMAX), 0).astype(f32)

    zero = jnp.zeros((), bf16)
    bit = {at: (lane >> at) % 2 == 1 for at in (3, 4, 5, 6)}

    def choose(tiles, mask):
        return [jnp.where(mask, odd, even) for even, odd in zip(tiles[0::2], tiles[1::2])]

    def one_group(start):
        first = start * 4
        rows_at = jnp.concatenate([off_ref[pl.ds(first + 2 * half, 8, stride=4), :] for half in range(2)], axis=1)
        cols_at = jnp.concatenate([off_ref[pl.ds(first + 2 * half + 1, 8, stride=4), :] for half in range(2)], axis=1)
        count = cnt_ref[pl.ds(start, 8), 0:128]
        count = jnp.concatenate([count, count], axis=1)
        weight = jnp.where(particle < count, w_ref[pl.ds(start, 8), :], 0.0)
        lag = rows_at * weight
        left = []
        for i in range(17):
            left.append(weight - jnp.abs(lag))
            lag = lag - weight
        left = jnp.maximum(jnp.concatenate(left, axis=0).astype(bf16), zero)
        right = []
        for g in range(8):
            at = first + 4 * ((8 - g) % 8) + 1
            column = jnp.concatenate([off_ref[pl.ds(at + 2 * half, 8, stride=0), :] for half in range(2)], axis=1)
            right += [1.0 - jnp.abs(column - cell[0:8]), 1.0 - jnp.abs(column - cell[8:16])]
        last = cols_at - 15.0
        right = [jnp.maximum(jnp.concatenate(right, axis=0).astype(bf16), zero)]
        right += [jnp.maximum(jnp.concatenate([last, last], axis=0).astype(bf16), zero)] * 8
        full = mm_nt(left, jnp.concatenate(right, axis=0))
        halves = []
        for half in range(2):
            pairs = []
            for pair in range(4):
                at = (half * 8 + pair * 2) * 8
                even = pltpu.roll(full[at : at + 8, 0:128], 0, 1, stride=16, stride_axis=0)
                odd = pltpu.roll(full[at + 8 : at + 16, 0:128], 16, 1, stride=16, stride_axis=0)
                both = jnp.where(bit[4], odd, even)
                pairs.append(pltpu.roll(both, 32 * pair, 1) if pair else both)
            halves.append(choose(choose(pairs, bit[5]), bit[6])[0])
        bottom = pltpu.roll(full[128:136, 0:128], 0, 1, stride=16, stride_axis=0)
        corner = jnp.sum(jnp.where(lane == sub, full[128:136, 128:256], 0.0), axis=1, keepdims=True)
        third = jnp.where(lane < 16, bottom, jnp.where(lane == 32, corner, 0.0))
        edge = [full[8 * i : 8 * i + 8, 128:256] for i in range(16)]
        for at in range(3, 7):
            edge = choose(edge, bit[at])
        edge = jnp.where(lane % 8 == sub, edge[0], 0.0)
        patch_ref[pl.ds(start, 8), 0:128] = halves[0]
        patch_ref[pl.ds(start, 8), 128:256] = halves[1]
        patch_ref[pl.ds(start, 8), 256:384] = third + cnt_ref[pl.ds(start, 8), 128:256]
        edge_ref[pl.ds(start, 8), :] = edge

    for index in range(STEPS):
        for copy in fetch(index):
            copy.wait()
    for group in range(BRICKS // 8):
        one_group(group * 8)

    gather = (iota((128, 128), 1) == iota((128, 128), 0) // 8 + 16).astype(bf16)
    edge_high, edge_low = hi_lo(edge_ref[...])
    third = patch_ref[:, 256:384] + (mm(edge_high, gather) + mm(edge_low, gather))

    high, low = hi_lo(patch_ref[:, 0:256])
    ends = jnp.concatenate(hi_lo(third), axis=1)
    lane_wide = iota((N_DEST, 128), 1)
    for pair in range(4):
        edges = []
        for rank in (2 * pair, 2 * pair + 1):
            pick = (iota((N_DEST, BRICKS), 0) + rank * N_DEST == position).astype(bf16)
            inner = mm(pick, high) + mm(pick, low)
            out_ref[pl.ds(rank, N_DEST, stride=MESSAGE), :] = inner[:, 0:128]
            out_ref[pl.ds(8 + rank, N_DEST, stride=MESSAGE), :] = inner[:, 128:256]
            both = mm(pick, ends)
            edges.append(both[:, 0:128] + both[:, 128:256])
        joined = jnp.where(lane_wide < 64, edges[0], pltpu.roll(edges[1], 64, 1))
        out_ref[pl.ds(16 + pair, N_DEST, stride=MESSAGE), :] = joined


def deposit_and_pack(offsets, weights, counts, owners, slots):
    flat = offsets.reshape(BRICKS, 2, 2, 128).transpose(0, 2, 1, 3).reshape(4 * BRICKS, 128)
    return pl.pallas_call(
        deposit_kernel,
        out_shape=jax.ShapeDtypeStruct((N_DEST * MESSAGE, 128), f32),
        in_specs=[pl.BlockSpec(memory_space=pltpu.MemorySpace.HBM)] * 5,
        scratch_shapes=[
            pltpu.VMEM((4 * BRICKS, 128), f32),
            pltpu.VMEM((BRICKS, PMAX), f32),
            pltpu.VMEM((1, BRICKS), jnp.int32),
            pltpu.VMEM((1, BRICKS), jnp.int32),
            pltpu.VMEM((1, BRICKS), jnp.int32),
            pltpu.VMEM((BRICKS, 256), f32),
            pltpu.VMEM((BRICKS, 384), f32),
            pltpu.VMEM((BRICKS, 128), f32),
            pltpu.SemaphoreType.DMA((3,)),
            pltpu.SemaphoreType.DMA((STEPS,)),
            pltpu.SemaphoreType.DMA((STEPS,)),
        ],
        compiler_params=pltpu.CompilerParams(vmem_limit_bytes=40 << 20),
        name="deposit",
    )(*(pltpu.with_memory_space_constraint(x, pltpu.MemorySpace.HBM) for x in (
        flat,
        weights,
        counts.reshape(1, BRICKS),
        owners.reshape(1, BRICKS),
        slots.reshape(1, BRICKS),
    )))


def mm3(data, table):
    high, low = hi_lo(data)
    return mm(high, table[0]) + (mm(low, table[0]) + mm(high, table[1]))


def mm3_left(table, data):
    high, low = hi_lo(data)
    return mm(table[0], high) + (mm(table[0], low) + mm(table[1], high))


def block_slots(block):
    row = iota((128, SLOTS), 0)
    return (row // 16) * 64 + row % 16 + block * 16


def edge_slots():
    row = iota((128, SLOTS), 0)
    return (row // 16) * 64 + row % 16 + jnp.where(row < 80, 0, 64 + 48)


def place(x_ref, grid_ref, picks):
    lane8 = iota((8, 128), 1)
    upper = jnp.concatenate([x_ref[pl.ds(rank, N_DEST, stride=MESSAGE), :] for rank in range(8)], axis=0)
    lower = jnp.concatenate([x_ref[pl.ds(8 + rank, N_DEST, stride=MESSAGE), :] for rank in range(8)], axis=0)
    ends = []
    for pair in range(4):
        joined = x_ref[pl.ds(16 + pair, N_DEST, stride=MESSAGE), :]
        ends += [joined, pltpu.roll(joined, 64, 1)]
    ends_high, ends_low = hi_lo(jnp.concatenate(ends, axis=0))
    weigh = jnp.where(lane8 == 40, 16.0, jnp.where(lane8 == 41, 1.0, 0.0)).astype(bf16)
    slot = mm_nt(weigh, ends_high)[0:1, :].astype(jnp.int32)
    high, low = hi_lo(jnp.concatenate([upper, lower], axis=1))
    ends = jnp.concatenate([ends_high, ends_low], axis=1)
    for at, slots in enumerate(picks):
        rows = slice(at * 128, (at + 1) * 128)
        pick = (slots == slot).astype(bf16)
        grid_ref[rows, 0:256] = mm(pick, high) + mm(pick, low)
        both = mm(pick, ends)
        grid_ref[rows, 256:384] = both[:, 0:128] + both[:, 128:256]


def swap_groups(tiles):
    group = iota((8, 128), 1) // 16
    for d in (1, 2, 4):
        mask = (group // d) % 2 == 0
        new = list(tiles)
        for a in range(8):
            if (a // d) % 2 == 0:
                one, two = tiles[a], tiles[a + d]
                new[a] = jnp.where(mask, one, pltpu.roll(two, 16 * d, 1))
                new[a + d] = jnp.where(mask, pltpu.roll(one, 128 - 16 * d, 1), two)
        tiles = new
    return tiles


def turn(side, corner):
    turned = [[pltpu.roll(side[half], 16 - i, 1) for half in range(2)] for i in range(16)]
    return turned + [[pltpu.roll(corner[half], 16, 1) for half in range(2)]]


def unpack_block(grid_ref, starts):
    rows = [[None, None] for _ in range(17)]
    side, corner = [None, None], [None, None]
    none = jnp.zeros((8, 128), f32)
    for half in range(2):
        parts = []
        for third in range(3):
            lanes = slice(third * 128, (third + 1) * 128)
            parts.append(
                swap_groups(
                    [none if at is None else grid_ref[at + half * 8 : at + half * 8 + 8, lanes] for at in starts]
                )
            )
        for i in range(8):
            rows[i][half] = parts[0][i]
            rows[8 + i][half] = parts[1][i]
        rows[16][half] = parts[2][0]
        side[half] = parts[2][1]
        corner[half] = parts[2][2]
    return rows, side, corner


def add_spills(rows, turned, previous):
    lane8 = iota((8, 128), 1)
    out = []
    for i in range(17):
        pair = []
        for half in range(2):
            spill = jnp.where(lane8 % 16 == 0, turned[i][half], 0.0)
            first = 0.0 if previous is None else previous[i][half]
            pair.append(rows[i][half] + jnp.where(lane8 == 0, first, spill))
        out.append(pair)
    return out


def store_block(rows, ref):
    sub = iota((8, 128), 0)
    down = [pltpu.roll(rows[16][half], 1, 0) for half in range(2)]
    for i in range(16):
        low, high = rows[i]
        if i == 0:
            low = low + jnp.where(sub == 0, 0.0, down[0])
            high = high + jnp.where(sub == 0, down[0], down[1])
        ref[pl.ds(i, 8, stride=16), :] = low
        ref[pl.ds(128 + i, 8, stride=16), :] = high
    ref[256:264, :] = jnp.where(sub == 0, down[1], 0.0)
    ref[264:TILE_ROWS, :] = jnp.zeros((8, 128), f32)


def place_edges_kernel(x_ref, first_ref, left_ref, right_ref, grid_ref, side_ref):
    place(x_ref, grid_ref, [edge_slots()])
    lane8 = iota((8, 128), 1)
    rows, side, corner = unpack_block(grid_ref, [0, 16, 32, 48, 64, None, None, None])
    store_block(add_spills(rows, turn(side, corner), None), first_ref)
    rows, side, corner = unpack_block(grid_ref, [None] * 6 + [80, 96])
    turned = turn(side, corner)
    rows = add_spills(rows, turned, None)
    store_block(
        [[jnp.where(lane8 == 0, turned[i][half], rows[i][half]) for half in range(2)] for i in range(17)], side_ref
    )
    right = [jnp.zeros((8, 128), f32)] * 5
    left = [jnp.zeros((8, 128), f32)] * 5
    for tile in range(33):
        group, at = divmod(tile, 5)
        rows8 = slice(tile * 8, tile * 8 + 8)
        both = side_ref[rows8, :]
        moved = jnp.where(lane8 == 112 + group, pltpu.roll(both, 112 + group, 1), right[at])
        right[at] = jnp.where(lane8 // 16 == group, pltpu.roll(both, 16 * group + 16, 1), moved)
        turned64 = pltpu.roll(first_ref[rows8, :], (64 + 16 * group) % 128, 1) if group != 4 else first_ref[rows8, :]
        left[at] = jnp.where(lane8 // 16 == group, turned64, left[at])
    for at in range(5):
        right_ref[at * 8 : at * 8 + 8, :] = right[at]
        left_ref[136 + at * 8 : 144 + at * 8, :] = left[at]
    lane = iota((136, 128), 1)
    left_ref[0:136, :] = jnp.where(lane < 64, first_ref[0:136, :], pltpu.roll(first_ref[136:272, :], 64, 1))


def place_edges(arrived):
    tile = jax.ShapeDtypeStruct((TILE_ROWS, 128), f32)
    return pl.pallas_call(
        place_edges_kernel,
        out_shape=(
            tile,
            jax.ShapeDtypeStruct((LEFT_MESSAGE, 128), f32),
            jax.ShapeDtypeStruct((40, 128), f32),
        ),
        scratch_shapes=[pltpu.VMEM((128, 384), f32), pltpu.VMEM((TILE_ROWS, 128), f32)],
        compiler_params=pltpu.CompilerParams(vmem_limit_bytes=32 << 20),
        cost_estimate=pl.CostEstimate(flops=600_000_000, bytes_accessed=2_000_000, transcendentals=0),
        name="place_edges",
    )(arrived)


def place_inner_kernel(x_ref, inner_ref, own_ref, grid_ref, *tile_refs):
    place(x_ref, grid_ref, [block_slots(block) for block in range(4)])
    previous = None
    for block, ref in enumerate(tile_refs):
        rows, side, corner = unpack_block(grid_ref, [block * 128 + col * 16 for col in range(8)])
        turned = turn(side, corner)
        store_block(add_spills(rows, turned, previous), ref)
        previous = turned
    own_ref[:, 0:256] = mm3(jnp.concatenate([ref[...] for ref in tile_refs[0:3]], axis=1), inner_ref)
    own_ref[:, 256:512] = mm3(jnp.concatenate([ref[...] for ref in tile_refs[2:4]], axis=1), inner_ref[:, 0:256, :])


def place_inner(arrived, inner):
    return pl.pallas_call(
        place_inner_kernel,
        out_shape=jax.ShapeDtypeStruct((TILE_ROWS, 512), f32),
        scratch_shapes=[pltpu.VMEM((BRICKS, 384), f32)] + [pltpu.VMEM((TILE_ROWS, 128), f32)] * 4,
        compiler_params=pltpu.CompilerParams(vmem_limit_bytes=32 << 20),
        cost_estimate=pl.CostEstimate(flops=800_000_000, bytes_accessed=3_000_000, transcendentals=0),
        name="place_inner",
    )(arrived, inner)


def pack_tiles(tiles):
    lane = iota(tiles[0].shape, 1)
    shared = jnp.where((lane >= 56) & (lane < 72), pltpu.roll(tiles[5], 64, 1), tiles[2])
    return [tiles[0], tiles[1], shared, tiles[3], tiles[4]]


def unpack_tiles(tiles):
    return jnp.concatenate([*tiles, pltpu.roll(tiles[2], 64, 1)], axis=1)


def columns_kernel(
    own_ref, first_ref, to_right_ref, from_right_ref, from_left_ref, outer_ref, below_ref, out_ref, up_ref, down_ref
):
    lane8 = iota((8, 128), 1)
    none = jnp.zeros((8, 128), f32)
    spills, rows = [], []
    for tile in range(TILE_ROWS // 8):
        group, at = divmod(tile, 5)
        own = first_ref[tile * 8 : tile * 8 + 8, :]
        if tile == 33:
            spills.append(none)
            rows.append(jnp.concatenate([none, jnp.where(lane8 < 8, own, 0.0)], axis=1))
            continue
        packed = from_left_ref[at * 8 : at * 8 + 8, :]
        spill = jnp.where(lane8 == 0, pltpu.roll(packed, 16 - group, 1), 0.0)
        near = pltpu.roll(packed, 112 - 16 * group, 1)
        spills.append(spill)
        mixed = jnp.where(lane8 < 8, own + spill, jnp.where(lane8 >= 112, near, 0.0))
        wide = from_right_ref[(tile % 17) * 8 : (tile % 17) * 8 + 8, :]
        if tile >= 17:
            wide = pltpu.roll(wide, 64, 1)
        rest = from_right_ref[136 + at * 8 : 144 + at * 8, :]
        if group != 4:
            rest = pltpu.roll(rest, (64 - 16 * group) % 128, 1)
        over = jnp.where(lane8 == 0, pltpu.roll(to_right_ref[at * 8 : at * 8 + 8, :], 16 - group, 1), 0.0)
        right = jnp.where(lane8 < 64, wide, jnp.where(lane8 < 80, rest, 0.0)) + over
        rows.append(jnp.concatenate([right, mixed], axis=1))
    spill = jnp.concatenate(spills, axis=0)
    outer = mm3(jnp.concatenate(rows, axis=0), outer_ref)
    pieces = [
        own_ref[:, 0:128] + taps_low[0] * spill,
        own_ref[:, 256:384] + outer[:, 256:384],
        outer[:, 0:128],
        own_ref[:, 128:256] + taps_high[0] * spill,
        own_ref[:, 384:512] + outer[:, 384:512],
        outer[:, 128:256],
    ]
    low = mm3_left(below_ref, jnp.concatenate([piece[0:UP_ROWS] for piece in pieces[0:3]], axis=1))
    high = mm3_left(below_ref[:, 0:32, :], jnp.concatenate([piece[0:UP_ROWS] for piece in pieces[3:6]], axis=1))
    for part in range(2):
        rows16 = slice(part * 16, part * 16 + 16)
        fives = pack_tiles([half[rows16, at * 128 : (at + 1) * 128] for half in (low, high) for at in range(3)])
        for at, tile in enumerate(fives):
            up_ref[part * 80 + at * 16 : part * 80 + at * 16 + 16, :] = tile
    for at in range(3):
        up_ref[160 + at * 32 : 192 + at * 32, :] = low[32:64, at * 128 : (at + 1) * 128]
    for at, tile in enumerate(pack_tiles([piece[DOWN_FROM : DOWN_FROM + 24] for piece in pieces])):
        down_ref[at * 16 : at * 16 + 16, :] = tile[0:16]
        down_ref[80 + at : 81 + at, :] = tile[16:17]
    down_ref[85:88, :] = jnp.zeros((3, 128), f32)
    for at, piece in enumerate(pieces):
        out_ref[:, at * 128 : (at + 1) * 128] = piece


def outer_columns(own, first, to_right, from_right, from_left, outer, below):
    width = 2 * COL_ROOM[0]
    return pl.pallas_call(
        columns_kernel,
        out_shape=(
            jax.ShapeDtypeStruct((TILE_ROWS, width), f32),
            jax.ShapeDtypeStruct((UP_MESSAGE, 128), f32),
            jax.ShapeDtypeStruct((DOWN_MESSAGE, 128), f32),
        ),
        compiler_params=pltpu.CompilerParams(vmem_limit_bytes=32 << 20),
        cost_estimate=pl.CostEstimate(flops=220_000_000, bytes_accessed=2_000_000, transcendentals=0),
        name="columns",
    )(own, first, to_right, from_right, from_left, outer, below)


def second_columns(current, inner, rest):
    main = mm3(current, inner)
    rest = mm3(jnp.concatenate([current[:, 256:384], current[:, 0:128]], axis=1), rest)
    return jnp.concatenate([main[:, 0:128], rest[:, 0:128], main[:, 128:256], rest[:, 128:256]], axis=1)


def own_rows_kernel(own_ref, table_ref, inner_ref, rest_ref, rows_ref, out_ref, second_ref):
    for at in range(3):
        cols = slice(at * 256, (at + 1) * 256)
        out_ref[:, cols] = mm3_left(table_ref, own_ref[:, cols])
    current = out_ref[0 : ROW_ROOM[0], 0 : COL_ROOM[0]]
    second_ref[...] = mm3_left(rows_ref, second_columns(current, inner_ref, rest_ref))


def own_rows(own, table, inner, rest, rows):
    return pl.pallas_call(
        own_rows_kernel,
        out_shape=(
            jax.ShapeDtypeStruct((2 * ROW_ROOM[0], 2 * COL_ROOM[0]), f32),
            jax.ShapeDtypeStruct((2 * ROW_ROOM[1], 2 * COL_ROOM[1]), f32),
        ),
        compiler_params=pltpu.CompilerParams(vmem_limit_bytes=32 << 20),
        cost_estimate=pl.CostEstimate(flops=4_800_000_000, bytes_accessed=20_000_000, transcendentals=0),
        name="own_rows",
    )(own, table, inner, rest, rows)


def levels_kernel(part_ref, second_ref, below_ref, above_ref, table_ref, inner_ref, added_ref, *refs):
    col_refs = (None,) + refs[0:3]
    row_refs = (None, None) + refs[3:5]
    leader_refs = refs[5:9]
    approx_ref = refs[9]
    peak_ref = refs[10]
    sub = iota((8, 128), 0)
    above = [
        jnp.concatenate(
            [
                above_ref[at * 16 : at * 16 + 16, :],
                jnp.where(sub == 0, above_ref[80 + at : 81 + at, :], 0.0),
            ],
            axis=0,
        )
        for at in range(5)
    ]
    near = mm3_left(table_ref, unpack_tiles(above))
    half = COL_ROOM[0]
    sixes = [
        unpack_tiles([below_ref[part * 80 + at * 16 : part * 80 + at * 16 + 16, :] for at in range(5)])
        for part in range(2)
    ]
    threes = jnp.concatenate([below_ref[160 + at * 32 : 192 + at * 32, :] for at in range(3)], axis=1)
    threes = jnp.concatenate([threes, jnp.zeros((32, half), f32)], axis=1)
    added = {0: near[0:8], 184: near[8:16], 192: near[16:24], 376: near[24:32]}
    added.update({120: sixes[0], 136: threes, 312: sixes[1]})
    cuts = sorted({0, 8, 120, 136, 168, 184, 192, 200, 312, 328, 376, 384})
    both = jnp.concatenate(
        [
            part_ref[start:stop, :] + added[start] if start in added else part_ref[start:stop, :]
            for start, stop in zip(cuts, cuts[1:])
        ],
        axis=0,
    )
    peak = None
    for level in range(4):
        room_r = ROW_ROOM[level]
        room_c = COL_ROOM[level]
        if level == 1:
            halo = jnp.concatenate([added[start][:, :half] for start, _ in SECOND_ROWS], axis=0)
            both = second_ref[...] + mm3_left(added_ref, second_columns(halo, inner_ref, col_refs[1]))
        elif level:
            both = mm3_left(row_refs[level], mm3(current, col_refs[level]))
        current = both[:room_r, :room_c]
        detail_a = both[:room_r, room_c:]
        detail_b = both[room_r:, :room_c]
        detail_c = both[room_r:, room_c:]
        now = jnp.maximum(jnp.maximum(jnp.abs(detail_a), jnp.abs(detail_b)), jnp.abs(detail_c))
        if peak is not None:
            now = jnp.maximum(now, peak)
        n_r = R_DEV >> (level + 1)
        n_c = C_DEV >> (level + 1)
        after = pltpu.roll(now[: n_r + 8], n_r + 7, 0)[:n_r]
        before = pltpu.roll(jnp.concatenate([now[room_r - 8 :], now[:n_r]], axis=0), 1, 0)[8:]
        tall = jnp.maximum(now[:n_r], jnp.maximum(after, before))
        wide = jnp.maximum(tall, jnp.maximum(pltpu.roll(tall, 1, 1), pltpu.roll(tall, room_c - 1, 1)))
        leader_refs[level][...] = wide[:, :n_c]
        if level < 3:
            pairs = jnp.maximum(now, pltpu.roll(now, room_c - 1, 1))
            pooled = []
            for across in range(room_c // 128):
                top = across * ROW_ROOM[0]
                peak_ref[top : top + room_r, :] = pairs[:, across * 128 : (across + 1) * 128]
                pooled.append(
                    jnp.maximum(
                        peak_ref[pl.ds(top, room_r // 2, stride=2), :],
                        peak_ref[pl.ds(top + 1, room_r // 2, stride=2), :],
                    )
                )
            high, low = hi_lo(jnp.concatenate(pooled, axis=1) if len(pooled) > 1 else pooled[0])
            room_n = COL_ROOM[level + 1]
            out = iota((room_c, room_n), 1)
            source = 2 * out + jnp.where(out < 3 * room_n // 4, 0, room_c - 2 * room_n)
            pick = (iota((room_c, room_n), 0) == source).astype(bf16)
            peak = mm(high, pick) + mm(low, pick)
    approx_ref[...] = current[: R_DEV >> 4, : C_DEV >> 4]


def all_levels(part, second, below, above, near, inner, added, cols, rows):
    shapes = [(R_DEV >> level, C_DEV >> level) for level in (1, 2, 3, 4, 4)]
    return pl.pallas_call(
        levels_kernel,
        out_shape=tuple(jax.ShapeDtypeStruct(shape, f32) for shape in shapes),
        scratch_shapes=[pltpu.VMEM((3 * ROW_ROOM[0], 128), f32)],
        compiler_params=pltpu.CompilerParams(vmem_limit_bytes=32 << 20),
        name="levels",
    )(part, second, below, above, near, inner, added, *cols, *rows)


def shifted(x, axis, by):
    size = lax.axis_size(axis)
    return lax.ppermute(x, axis, [(i, (i + by) % size) for i in range(size)])


def transform(arrived):
    table = jax.tree.map(jnp.asarray, tables())
    first, to_left, to_right = place_edges(arrived)
    from_right = shifted(to_left, "cols", -1)
    from_left = shifted(to_right, "cols", 1)
    inner = place_inner(arrived, table["inner"])
    own, to_up, to_down = outer_columns(
        inner, first, to_right, from_right, from_left, table["outer"], table["below"]
    )
    above = shifted(to_down, "rows", 1)
    below = shifted(to_up, "rows", -1)
    part, second = own_rows(own, table["own"], table["inner"], table["cols"][0], table["rows"][0])
    return all_levels(
        part, second, below, above, table["above"], table["inner"], table["second"], table["cols"], table["rows"][1:]
    )


def on_device(offsets, lens_weight, counts, owners, brick_slot):
    packed = deposit_and_pack(offsets, lens_weight, counts, owners, brick_slot)
    arrived = lax.all_to_all(
        packed.reshape(N_DEST, MESSAGE // 4, 4, 128), ("rows", "cols"), split_axis=0, concat_axis=0, tiled=True
    )
    return transform(arrived.reshape(N_DEST * MESSAGE, 128))


def solution(mesh):
    placed = (
        P(("rows", "cols"), None, None),
        P(("rows", "cols"), None),
        P(("rows", "cols")),
        P(("rows", "cols")),
        P(("rows", "cols")),
    )
    return jax.shard_map(
        on_device,
        mesh=mesh,
        in_specs=placed,
        out_specs=(P("rows", "cols"),) * 5,
        check_vma=False,
    )
```
